256 devices in a mesh: seq: 64 (over y, z_hi, x, core), dp: 4 (over z_lo).
Axes of the slice: x: 4, y: 4, z: 8 (z_hi: 2, z_lo: 4; z = z_hi * 4 + z_lo), core: 2. Of those that a mesh axis runs over, the one named last changes fastest.
Arguments:
- query: bfloat16 [4, 8192, 2048], P('dp', 'seq'), may hold values from -6 to 6
- keys: bfloat16 [4, 8192, 512], P('dp', 'seq'), may hold values from -6 to 6
- values: bfloat16 [4, 8192, 512], P('dp', 'seq'), may hold values from -6 to 6
- out_grad: bfloat16 [4, 8192, 2048], P('dp', 'seq'), may hold values from -16 to 16
- normed_input: bfloat16 [4, 8192, 4096], P('dp', 'seq'), may hold values from -16 to 16
- q_start: int32 [8], P('dp'), may hold values from 2048 to 3071, as said below
- q_len: int32 [8], P('dp'), may hold values from 1 to 512, as said below
Outputs:
- q_grad: bfloat16 [4, 8192, 2048], P('dp', 'seq')
- k_grad: bfloat16 [4, 8192, 512], P('dp', 'seq')
- v_grad: bfloat16 [4, 8192, 512], P('dp', 'seq')
- kv_weight_grad: float32 [4096, 1024], P(('seq', 'dp'))
The draws below stay inside these ranges and needn't reach their ends.
Inputs may be any that keep to these rules, and one draw needn't show every extreme that they name: `q_start`: the visual part of each sequence ends here. `q_len`: tokens after the question are padding.
All inputs are finite; a program needn't handle non-finite values.
Results may differ from the reference program's by a relative error of at most 0.013.
Values may be sent and summed in bfloat16 or wider, within the bound.
A program may use at most 128 MiB of HBM per device.

```python
import math
import jax
import jax.numpy as jnp
from jax import lax

D = 4096
HEADS = 16
KV_HEADS = 4
HEAD_DIM = 128
LEN = 4096
GROUP = 8192
SEQS = 8
N_DP = 4


def draw_keys(key, part):
    shape_full = (N_DP, GROUP, KV_HEADS, HEAD_DIM)
    base = jnp.clip(jax.random.normal(jax.random.fold_in(key, 21), shape_full, jnp.float32), -6.0, 6.0)
    return base.reshape(N_DP, GROUP, KV_HEADS * HEAD_DIM).astype(jnp.bfloat16)


def draw_query(key, part):
    shape_full = (N_DP, GROUP, HEADS, HEAD_DIM)
    base = jnp.clip(1.5 * jax.random.normal(jax.random.fold_in(key, 31), shape_full, jnp.float32), -6.0, 6.0)
    return base.reshape(N_DP, GROUP, HEADS * HEAD_DIM).astype(jnp.bfloat16)


def draw_q_start(key, part):
    lowest = LEN // 2
    highest = 3 * LEN // 4 - 1
    drawn = jax.random.randint(jax.random.fold_in(key, 11), (SEQS,), lowest, highest + 1)
    order = jax.random.permutation(jax.random.fold_in(key, 12), SEQS)
    drawn = drawn.at[order[0]].set(lowest).at[order[1]].set(highest)
    return drawn.astype(jnp.int32)


def draw_q_len(key, part):
    highest = LEN // 8
    drawn = jax.random.randint(jax.random.fold_in(key, 13), (SEQS,), 1, highest + 1)
    order = jax.random.permutation(jax.random.fold_in(key, 14), SEQS)
    drawn = drawn.at[order[0]].set(1).at[order[1]].set(highest)
    return drawn.astype(jnp.int32)


def with_spikes(result, rng, source, target, parts, factor):
    owner, partner = [(jnp.arange(result.shape[position]) // (result.shape[position] // parts)).reshape([-1 if axis == position else 1 for axis in range(result.ndim)]) for position in (source, target)]
    chosen = jax.random.permutation(rng, parts)[partner]
    strong = (owner == chosen) | (owner == (partner + parts // 2) % parts)
    return jnp.where(strong, factor * result, result)


def steps_of(stream_key, shape, pieces, low, high):
    gain, own = 1.0, jax.random.fold_in(stream_key, 6)
    for position, shards_of in pieces:
        draws = jnp.exp(jax.random.uniform(jax.random.fold_in(own, position), (shards_of,), jnp.float32, low / len(pieces), high / len(pieces)))
        gain = gain * jnp.repeat(draws, shape[position] // shards_of).reshape([-1 if axis == position else 1 for axis in range(len(shape))])
    return gain


def centred(own_key, extent, width, bound, cuts=(), held_as=jnp.bfloat16):
    entries = width * jax.random.normal(own_key, extent, jnp.float32)
    if cuts:
        entries = entries * steps_of(own_key, extent, cuts, -0.22, 0.18)
    return jnp.clip(entries, -bound, bound).astype(held_as)


def heavy_noise(rng, shape, spread, bound, cuts, heavy, held_as=jnp.bfloat16):
    array = spread * jax.random.normal(rng, shape, jnp.float32)
    if cuts:
        array = array * steps_of(rng, shape, cuts, -0.22, 0.18)
    return jnp.clip(with_spikes(array, jax.random.fold_in(rng, 3), *heavy), -bound, bound).astype(held_as)


def setup_inputs(seed: int = 0) -> dict:
    splits = jax.random.split(jax.random.key(seed), 8)
    query = draw_query(jax.random.fold_in(splits[7], 71), 0)
    keys = draw_keys(jax.random.fold_in(splits[7], 71), 0)
    values = centred(splits[2], (N_DP, GROUP, KV_HEADS * HEAD_DIM), 1.0, 6.0, ((0, 4), (1, 64)))
    out_grad = centred(splits[3], (N_DP, GROUP, HEADS * HEAD_DIM), 4.0, 16.0, ((0, 4), (1, 64)))
    normed_input = heavy_noise(splits[4], (N_DP, GROUP, D), 1.0, 16.0, ((0, 4), (1, 64)), (1, 2, 64, 4.0))
    q_start = draw_q_start(jax.random.fold_in(splits[7], 71), 0)
    q_len = draw_q_len(jax.random.fold_in(splits[7], 71), 0)
    return dict(query=query, keys=keys, values=values, out_grad=out_grad, normed_input=normed_input, q_start=q_start, q_len=q_len)


def sequence_grads(query_seq, keys_seq, values_seq, grad_seq, start_pos, span_len):
    score_scale = 1.0 / math.sqrt(HEAD_DIM)
    repeat_by = HEADS // KV_HEADS
    block_rows = min(512, LEN)
    query_heads = query_seq.reshape(LEN, HEADS, HEAD_DIM).astype(jnp.float32)
    grad_heads = grad_seq.reshape(LEN, HEADS, HEAD_DIM).astype(jnp.float32)
    key_heads = jnp.repeat(keys_seq.reshape(LEN, KV_HEADS, HEAD_DIM), repeat_by, axis=1).astype(jnp.float32)
    value_heads = jnp.repeat(values_seq.reshape(LEN, KV_HEADS, HEAD_DIM), repeat_by, axis=1).astype(jnp.float32)
    key_pos = jnp.arange(LEN, dtype=jnp.int32)
    end_pos = start_pos + span_len

    def one_block(carry, block_idx):
        key_acc, value_acc = carry
        first_row = block_idx * block_rows
        query_block = lax.dynamic_slice_in_dim(query_heads, first_row, block_rows, 0)
        grad_block = lax.dynamic_slice_in_dim(grad_heads, first_row, block_rows, 0)
        query_pos = first_row + jnp.arange(block_rows, dtype=jnp.int32)
        visible = (key_pos[None, :] < end_pos) & ((key_pos[None, :] <= query_pos[:, None]) | (key_pos[None, :] < start_pos))
        scores = jnp.einsum('qhd,khd->hqk', query_block, key_heads) * score_scale
        scores = jnp.where(visible[None], scores, -jnp.inf)
        row_max = lax.optimization_barrier(jnp.max(scores, axis=-1, keepdims=True))
        exponent = jnp.where(visible[None], jnp.exp(scores - row_max), 0.0)
        probability = exponent / lax.optimization_barrier(jnp.sum(exponent, axis=-1, keepdims=True))
        prob_low = lax.optimization_barrier(probability.astype(jnp.bfloat16)).astype(jnp.float32)
        dprob = jnp.einsum('qhd,khd->hqk', grad_block, value_heads)
        row_delta = lax.optimization_barrier(jnp.sum(probability * dprob, axis=-1, keepdims=True))
        dscore = lax.optimization_barrier((probability * (dprob - row_delta) * score_scale).astype(jnp.bfloat16)).astype(jnp.float32)
        query_grad = jnp.einsum('hqk,khd->qhd', dscore, key_heads).astype(jnp.bfloat16)
        key_acc = key_acc + jnp.einsum('hqk,qhd->khd', dscore, query_block)
        value_acc = value_acc + jnp.einsum('hqk,qhd->khd', prob_low, grad_block)
        return ((key_acc, value_acc), query_grad)
    zero_state = jnp.zeros((LEN, HEADS, HEAD_DIM), jnp.float32)
    (key_acc, value_acc), query_grads = lax.scan(one_block, (zero_state, zero_state), jnp.arange(LEN // block_rows, dtype=jnp.int32))
    query_grads = query_grads.reshape(LEN, HEADS * HEAD_DIM)
    key_grads = key_acc.reshape(LEN, KV_HEADS, repeat_by, HEAD_DIM).sum(axis=2).astype(jnp.bfloat16).reshape(LEN, KV_HEADS * HEAD_DIM)
    value_grads = value_acc.reshape(LEN, KV_HEADS, repeat_by, HEAD_DIM).sum(axis=2).astype(jnp.bfloat16).reshape(LEN, KV_HEADS * HEAD_DIM)
    return (query_grads, key_grads, value_grads)

def reference(query, keys, values, out_grad, normed_input, q_start, q_len):
    query_all = []
    key_all = []
    value_all = []
    weight_sum = jnp.zeros((D, 2 * KV_HEADS * HEAD_DIM), jnp.float32)
    for group_idx in range(N_DP):
        query_parts = []
        key_parts = []
        value_parts = []
        for seq_idx in range(2):
            lower = seq_idx * LEN
            upper = lower + LEN
            sample = 2 * group_idx + seq_idx
            query_piece, key_piece, value_piece = sequence_grads(query[group_idx, lower:upper], keys[group_idx, lower:upper], values[group_idx, lower:upper], out_grad[group_idx, lower:upper], q_start[sample], q_len[sample])
            query_parts.append(query_piece)
            key_parts.append(key_piece)
            value_parts.append(value_piece)
        key_group = jnp.concatenate(key_parts, axis=0)
        value_group = jnp.concatenate(value_parts, axis=0)
        joined = jnp.concatenate([key_group, value_group], axis=1)
        weight_sum = weight_sum + jnp.dot(normed_input[group_idx].T, joined, preferred_element_type=jnp.float32)
        query_all.append(jnp.concatenate(query_parts, axis=0))
        key_all.append(key_group)
        value_all.append(value_group)
    return (jnp.stack(query_all), jnp.stack(key_all), jnp.stack(value_all), weight_sum)
```

```python
import math
import functools
import jax
import jax.numpy as jnp
from jax import lax
from jax.experimental import pallas as pl
from jax.experimental.pallas import tpu as pltpu
from jax.sharding import PartitionSpec as P

HEAD_DIM = 128
SCALE = 1.0 / math.sqrt(HEAD_DIM)
EXPC = SCALE * math.log2(math.e)
NEG = -1e30
F32 = jnp.float32
BF16 = jnp.bfloat16
CK = 512


def dot_nt(a, b):
    return lax.dot_general(a, b, (((1,), (1,)), ((), ())), preferred_element_type=F32)


def dot_nn(a, b):
    return lax.dot_general(a, b, (((1,), (0,)), ((), ())), preferred_element_type=F32)


def dot_tn(a, b):
    return lax.dot_general(a, b, (((0,), (0,)), ((), ())), preferred_element_type=F32)


def att_body(q_ref, g_ref, kv_ref, lim_ref, dq_ref, kvg_ref, s_ref, d_ref, dk_ref, dv_ref, kt_ref, variant):
    dk_ref[...] = jnp.zeros_like(dk_ref)
    dv_ref[...] = jnp.zeros_like(dv_ref)
    if variant == "kt":
        for j in range(7):
            kt_ref[:, j * CK:(j + 1) * CK] = kv_ref[pl.ds(j * CK, CK), 0:128].T

    def unit(h, yl, nk):
        cols = pl.ds(pl.multiple_of(h * 128, 128), 128)
        q = q_ref[yl, :, cols]
        g = g_ref[yl, :, cols]
        lim = lim_ref[yl]
        m = jnp.full((1, 256), NEG, F32)
        for j in range(nk):
            rows = pl.ds(j * CK, CK)
            s = dot_nt(kv_ref[rows, 0:128], q)
            if j >= 4:
                kpos = lax.broadcasted_iota(jnp.int32, (CK, 256), 0) + j * CK
                s = jnp.where(kpos < lim, s, NEG)
            s_ref[rows, :] = s
            m = jnp.maximum(m, jnp.max(s, axis=0, keepdims=True))
        l = jnp.zeros((1, 256), F32)
        dl = jnp.zeros((1, 256), F32)
        for j in range(nk):
            rows = pl.ds(j * CK, CK)
            e = jnp.exp2((s_ref[rows, :] - m) * EXPC)
            dp = dot_nt(kv_ref[rows, 128:256], g)
            l = l + jnp.sum(e, axis=0, keepdims=True)
            dl = dl + jnp.sum(e * dp, axis=0, keepdims=True)
            s_ref[rows, :] = e
            d_ref[rows, :] = dp
        inv = 1.0 / l
        delta = dl * inv
        if variant == "kt":
            dq = jnp.zeros((128, 256), F32)
        else:
            dq = jnp.zeros((256, 128), F32)
        for j in range(nk):
            rows = pl.ds(j * CK, CK)
            p = s_ref[rows, :] * inv
            ds = (p * (d_ref[rows, :] - delta)).astype(BF16)
            dk_ref[rows, :] += dot_nn(ds, q)
            dv_ref[rows, :] += dot_nn(p.astype(BF16), g)
            if variant == "kt":
                dq = dq + dot_nn(kt_ref[:, j * CK:(j + 1) * CK], ds)
            else:
                dq = dq + dot_tn(ds, kv_ref[rows, 0:128])
        if variant == "kt":
            dq = dq.T
        dq_ref[yl, :, cols] = (dq * SCALE).astype(BF16)

    def head(h, carry):
        unit(h, 0, 6)
        unit(h, 1, 7)
        return carry

    lax.fori_loop(0, 4, head, 0)
    for j in range(7):
        rows = pl.ds(j * CK, CK)
        kvg_ref[rows, 0:128] = (dk_ref[rows, :] * SCALE).astype(BF16)
        kvg_ref[rows, 128:256] = dv_ref[rows, :].astype(BF16)
    kvg_ref[pl.ds(3584, CK), :] = jnp.zeros((CK, 256), BF16)


def attention(q, g, kv, lim, variant="tn"):
    return pl.pallas_call(
        functools.partial(att_body, variant=variant),
        name="attention_grads",
        out_shape=(jax.ShapeDtypeStruct((2, 256, 512), BF16), jax.ShapeDtypeStruct((4096, 256), BF16)),
        in_specs=[pl.BlockSpec(memory_space=pltpu.VMEM)] * 4,
        out_specs=[pl.BlockSpec(memory_space=pltpu.VMEM)] * 2,
        scratch_shapes=[
            pltpu.VMEM((3584, 256), F32),
            pltpu.VMEM((3584, 256), F32),
            pltpu.VMEM((3584, 128), F32),
            pltpu.VMEM((3584, 128), F32),
            pltpu.VMEM((128, 3584), BF16),
        ],
        compiler_params=pltpu.CompilerParams(vmem_limit_bytes=56 << 20),
    )(q, g, kv, lim)


def coords():
    seq = lax.axis_index("seq")
    c = lax.rem(seq, 2)
    x = lax.rem(seq // 2, 4)
    zh = lax.rem(seq // 8, 2)
    yl = lax.rem(seq // 16, 2)
    s = seq // 32
    zl = lax.axis_index("dp")
    return s, yl, zh, x, c, zl


def seq_of(s, yl, zh, x, c):
    return s * 32 + yl * 16 + zh * 8 + x * 2 + c


def rcopy(src, dst, ssem, rsem, seq, dp):
    return pltpu.make_async_remote_copy(
        src_ref=src, dst_ref=dst, send_sem=ssem, recv_sem=rsem,
        device_id={"seq": seq, "dp": dp}, device_id_type=pl.DeviceIdType.MESH)


def greet(peers):
    barrier = pltpu.get_barrier_semaphore()
    for seq, dp in peers:
        pl.semaphore_signal(barrier, inc=1, device_id={"seq": seq, "dp": dp},
                            device_id_type=pl.DeviceIdType.MESH)
    pl.semaphore_wait(barrier, len(peers))


def gather_body(q_in, g_in, k_in, v_in, q_out, g_out, kv_out,
                g_send, g_recv, z_send, z_recv, x_send, x_recv, l_sem):
    s, yl, zh, x, c, zl = coords()
    group = []
    for d in range(1, 4):
        dy, dc = d // 2, d % 2
        group.append(((yl + dy) % 2, (c + dc) % 2))
    xs = [(x + d) % 4 for d in range(1, 4)]
    peers = [(seq_of(s, py, zh, x, pc), zl) for py, pc in group]
    peers.append((seq_of(s, yl, 1 - zh, x, c), zl))
    peers += [(seq_of(s, yl, zh, px, c), zl) for px in xs]
    greet(peers)

    def cols(h, w):
        return pl.ds(pl.multiple_of(h * w, 128), w)

    my_rows = pl.ds(pl.multiple_of(c * 128, 128), 128)
    kv_sends = []
    sends = []
    for i, (py, pc) in enumerate(group):
        h = py * 2 + pc
        dev = seq_of(s, py, zh, x, pc)
        kv_sends.append(rcopy(k_in.at[0, :, cols(h, 128)], kv_out.at[yl, zh, x, my_rows, pl.ds(0, 128)],
                              g_send.at[0, i], g_recv.at[0, i], dev, zl))
        kv_sends.append(rcopy(v_in.at[0, :, cols(h, 128)], kv_out.at[yl, zh, x, my_rows, pl.ds(128, 128)],
                              g_send.at[1, i], g_recv.at[1, i], dev, zl))
    for i, (py, pc) in enumerate(group):
        h = py * 2 + pc
        dev = seq_of(s, py, zh, x, pc)
        sends.append(rcopy(q_in.at[0, :, cols(h, 512)], q_out.at[yl, my_rows, :],
                           g_send.at[2, i], g_recv.at[2, i], dev, zl))
        sends.append(rcopy(g_in.at[0, :, cols(h, 512)], g_out.at[yl, my_rows, :],
                           g_send.at[3, i], g_recv.at[3, i], dev, zl))
    for cp in kv_sends:
        cp.start()
    h = yl * 2 + c
    own_kv = [
        pltpu.make_async_copy(k_in.at[0, :, cols(h, 128)], kv_out.at[yl, zh, x, my_rows, pl.ds(0, 128)], l_sem.at[0]),
        pltpu.make_async_copy(v_in.at[0, :, cols(h, 128)], kv_out.at[yl, zh, x, my_rows, pl.ds(128, 128)], l_sem.at[1]),
    ]
    own = [
        pltpu.make_async_copy(q_in.at[0, :, cols(h, 512)], q_out.at[yl, my_rows, :], l_sem.at[2]),
        pltpu.make_async_copy(g_in.at[0, :, cols(h, 512)], g_out.at[yl, my_rows, :], l_sem.at[3]),
    ]
    for cp in own_kv + own:
        cp.start()
    for cp in sends:
        cp.start()
    for cp in own_kv:
        cp.wait()
    for cp in kv_sends:
        cp.wait_recv()
    zcopy = rcopy(kv_out.at[:, zh, x], kv_out.at[:, zh, x], z_send, z_recv,
                  seq_of(s, yl, 1 - zh, x, c), zl)
    zcopy.start()
    xcopies = []
    for i, px in enumerate(xs):
        cp = rcopy(kv_out.at[:, zh, x], kv_out.at[:, zh, x], x_send.at[0, i], x_recv.at[0, i],
                   seq_of(s, yl, zh, px, c), zl)
        cp.start()
        xcopies.append(cp)
    zcopy.wait_recv()
    for i, px in enumerate(xs):
        cp = rcopy(kv_out.at[:, 1 - zh, x], kv_out.at[:, 1 - zh, x], x_send.at[1, i], x_recv.at[1, i],
                   seq_of(s, yl, zh, px, c), zl)
        cp.start()
        xcopies.append(cp)
    for cp in own:
        cp.wait()
    for cp in sends:
        cp.wait_recv()
    for cp in xcopies:
        cp.wait_recv()
    for cp in kv_sends + sends + [zcopy] + xcopies:
        cp.wait_send()


def gather(q, g, k, v):
    dma = pltpu.SemaphoreType.DMA
    return pl.pallas_call(
        gather_body,
        name="gather_heads",
        out_shape=(jax.ShapeDtypeStruct((2, 256, 512), BF16), jax.ShapeDtypeStruct((2, 256, 512), BF16),
                   jax.ShapeDtypeStruct((2, 2, 4, 256, 256), BF16)),
        in_specs=[pl.BlockSpec(memory_space=pl.ANY)] * 4,
        out_specs=[pl.BlockSpec(memory_space=pl.ANY)] * 3,
        scratch_shapes=[dma((4, 3)), dma((4, 3)), dma, dma, dma((2, 3)), dma((2, 3)), dma((4,))],
        compiler_params=pltpu.CompilerParams(collective_id=0, has_side_effects=True),
    )(q, g, k, v)


def reduce_body(dq_in, kvg_in, n_in, dq_out, kg_out, vg_out, w_out,
                nbuf, xr, acc, zsend, zrecv, kg, wpart, w1r, w2r, w2s, w3r, w3s, w4s, w4r,
                n_send, n_recv, q_send, q_recv, x_send, x_recv, z_send, z_recv, k_send, k_recv,
                w1_send, w1_recv, w2_send, w2_recv, w3_send, w3_recv, w4_send, w4_recv, l_sem):
    s, yl, zh, x, c, zl = coords()
    me = seq_of(s, yl, zh, x, c)
    group = []
    for d in range(1, 4):
        dy, dc = d // 2, d % 2
        group.append(((yl + dy) % 2, (c + dc) % 2))
    xs = [(x + d) % 4 for d in range(1, 4)]
    z = zh * 4 + zl
    zs = [((z + d) % 8) for d in range(1, 8)]
    peers = [(seq_of(s, py, zh, x, pc), zl) for py, pc in group]
    peers += [(seq_of(s, yl, zh, px, c), zl) for px in xs]
    peers += [(seq_of(s, yl, pz // 4, x, c), pz % 4) for pz in zs]
    peers.append((seq_of(1 - s, yl, zh, x, c), zl))
    greet(peers)

    def cols(h, w):
        return pl.ds(pl.multiple_of(h * w, 128), w)

    h = yl * 2 + c
    my_rows = pl.ds(pl.multiple_of(c * 128, 128), 128)
    sends = []

    def go(cp):
        cp.start()
        sends.append(cp)
        return cp

    far = [go(rcopy(kvg_in.at[:, 1 - zh, px], xr.at[0, i], x_send.at[0, i], x_recv.at[0, i],
                    seq_of(s, yl, zh, px, c), zl)) for i, px in enumerate(xs)]
    near = [go(rcopy(kvg_in.at[:, zh, px], xr.at[1, i], x_send.at[1, i], x_recv.at[1, i],
                     seq_of(s, yl, zh, px, c), zl)) for i, px in enumerate(xs)]
    own_a = pltpu.make_async_copy(kvg_in.at[:, 1 - zh, x], zsend, l_sem.at[0])
    own_b = pltpu.make_async_copy(kvg_in.at[:, zh, x], kg, l_sem.at[1])
    own_a.start()
    own_b.start()
    n_own = pltpu.make_async_copy(n_in.at[0], nbuf.at[yl, my_rows, :], l_sem.at[2])
    n_own.start()
    n_y = go(rcopy(n_in.at[0], nbuf.at[yl, my_rows, :], n_send.at[0], n_recv.at[0],
                   seq_of(s, 1 - yl, zh, x, c), zl))
    n_c = go(rcopy(n_in.at[0], nbuf.at[yl, my_rows, :], n_send.at[1], n_recv.at[1],
                   seq_of(s, yl, zh, x, 1 - c), zl))
    dq_own = pltpu.make_async_copy(dq_in.at[yl, my_rows, :], dq_out.at[0, :, cols(h, 512)], l_sem.at[3])
    dq_own.start()
    dqs = []
    for i, (py, pc) in enumerate(group):
        dqs.append(go(rcopy(dq_in.at[py, pl.ds(pl.multiple_of(pc * 128, 128), 128), :],
                            dq_out.at[0, :, cols(h, 512)], q_send.at[i], q_recv.at[i],
                            seq_of(s, py, zh, x, pc), zl)))
    own_a.wait()
    for cp in far:
        cp.wait_recv()
    zsend[...] = (zsend[...].astype(F32) + xr[0, 0].astype(F32) + xr[0, 1].astype(F32)
                  + xr[0, 2].astype(F32)).astype(BF16)
    zc = go(rcopy(zsend, zrecv, z_send, z_recv, seq_of(s, yl, 1 - zh, x, c), zl))
    own_b.wait()
    for cp in near:
        cp.wait_recv()
    acc[...] = (kg[...].astype(F32) + xr[1, 0].astype(F32) + xr[1, 1].astype(F32) + xr[1, 2].astype(F32))
    n_y.wait_recv()
    other = nbuf.at[1 - yl, my_rows, :]
    n_f = go(rcopy(other, other, n_send.at[2], n_recv.at[2], seq_of(s, yl, zh, x, 1 - c), zl))
    zc.wait_recv()
    kg[...] = (acc[...] + zrecv[...].astype(F32)).astype(BF16)
    kgs = []
    for i, (py, pc) in enumerate(group):
        prow = pl.ds(pl.multiple_of(pc * 128, 128), 128)
        dev = seq_of(s, py, zh, x, pc)
        kgs.append(go(rcopy(kg.at[py, prow, pl.ds(0, 128)], kg_out.at[0, :, cols(h, 128)],
                            k_send.at[0, i], k_recv.at[0, i], dev, zl)))
        kgs.append(go(rcopy(kg.at[py, prow, pl.ds(128, 128)], vg_out.at[0, :, cols(h, 128)],
                            k_send.at[1, i], k_recv.at[1, i], dev, zl)))
    k_own = [pltpu.make_async_copy(kg.at[yl, my_rows, pl.ds(0, 128)], kg_out.at[0, :, cols(h, 128)], l_sem.at[4]),
             pltpu.make_async_copy(kg.at[yl, my_rows, pl.ds(128, 128)], vg_out.at[0, :, cols(h, 128)], l_sem.at[5])]
    for cp in k_own:
        cp.start()
    n_own.wait()
    n_c.wait_recv()
    n_f.wait_recv()
    kgv = kg[...].reshape(512, 256)

    def wblock(i, carry):
        rows = pl.ds(pl.multiple_of(i * 512, 512), 512)
        part = dot_tn(nbuf[:, :, rows].reshape(512, 512), kgv)
        wpart[pl.ds(i, 1)] = part.astype(BF16).reshape(1, 4, 128, 256)
        return carry

    lax.fori_loop(0, 8, wblock, 0)
    w1 = [go(rcopy(wpart.at[:, px], w1r.at[i], w1_send.at[i], w1_recv.at[i],
                   seq_of(s, yl, zh, px, c), zl)) for i, px in enumerate(xs)]
    for cp in w1:
        cp.wait_recv()

    def add1(i, carry):
        blk = pl.ds(i, 1)
        a = wpart[blk, pl.ds(x, 1)].reshape(128, 256).astype(F32)
        a = a + w1r[0, blk].reshape(128, 256).astype(F32) + w1r[1, blk].reshape(128, 256).astype(F32)
        a = a + w1r[2, blk].reshape(128, 256).astype(F32)
        w2s[pl.ds(i // 2, 1), pl.ds(lax.rem(i, 2), 1)] = a.astype(BF16).reshape(1, 1, 2, 4, 16, 256)
        return carry

    lax.fori_loop(0, 8, add1, 0)
    w2 = [go(rcopy(w2s.at[:, pz // 4, :, pz % 4], w2r.at[i], w2_send.at[i], w2_recv.at[i],
                   seq_of(s, yl, pz // 4, x, c), pz % 4)) for i, pz in enumerate(zs)]
    for cp in w2:
        cp.wait_recv()
    t = w2s[:, pl.ds(zh, 1), :, pl.ds(zl, 1)].reshape(4, 2, 16, 256).astype(F32)
    for i in range(7):
        t = t + w2r[i].astype(F32)
    w3s[...] = t.reshape(2, 2, 2, 16, 256)
    w3 = go(rcopy(w3s.at[1 - s], w3r, w3_send, w3_recv, seq_of(1 - s, yl, zh, x, c), zl))
    w3.wait_recv()
    w4s[...] = w3s[s] + w3r[...]
    w4 = []
    for i, (py, pc) in enumerate(group):
        w4.append(go(rcopy(w4s.at[py, pc], w4r.at[h], w4_send.at[i], w4_recv.at[i],
                           seq_of(s, py, zh, x, pc), zl)))
    w4r[pl.ds(h, 1)] = w4s[yl, c].reshape(1, 16, 256)
    for cp in w4:
        cp.wait_recv()
    for hh in range(4):
        w_out[:, hh * 128:(hh + 1) * 128] = w4r[hh, :, 0:128]
        w_out[:, 512 + hh * 128:512 + (hh + 1) * 128] = w4r[hh, :, 128:256]
    for cp in dqs + kgs:
        cp.wait_recv()
    for cp in k_own + [dq_own]:
        cp.wait()
    for cp in sends:
        cp.wait_send()


def reduce_all(dq, kvg, n):
    dma = pltpu.SemaphoreType.DMA
    V = pltpu.VMEM
    return pl.pallas_call(
        reduce_body,
        name="reduce_grads",
        out_shape=(jax.ShapeDtypeStruct((1, 128, 2048), BF16), jax.ShapeDtypeStruct((1, 128, 512), BF16),
                   jax.ShapeDtypeStruct((1, 128, 512), BF16), jax.ShapeDtypeStruct((16, 1024), F32)),
        in_specs=[pl.BlockSpec(memory_space=pl.ANY)] * 3,
        out_specs=[pl.BlockSpec(memory_space=pl.ANY)] * 3 + [pl.BlockSpec(memory_space=pltpu.VMEM)],
        scratch_shapes=[
            V((2, 256, 4096), BF16), V((2, 3, 2, 256, 256), BF16), V((2, 256, 256), F32),
            V((2, 256, 256), BF16), V((2, 256, 256), BF16), V((2, 256, 256), BF16),
            V((8, 4, 128, 256), BF16), V((3, 8, 128, 256), BF16),
            V((7, 4, 2, 16, 256), BF16), V((4, 2, 2, 4, 16, 256), BF16),
            V((2, 2, 16, 256), F32), V((2, 2, 2, 16, 256), F32),
            V((2, 2, 16, 256), F32), V((4, 16, 256), F32),
            dma((3,)), dma((3,)), dma((3,)), dma((3,)), dma((2, 3)), dma((2, 3)), dma, dma,
            dma((2, 3)), dma((2, 3)), dma((3,)), dma((3,)), dma((7,)), dma((7,)), dma, dma, dma((3,)), dma((3,)),
            dma((6,)),
        ],
        compiler_params=pltpu.CompilerParams(collective_id=1, has_side_effects=True, vmem_limit_bytes=48 << 20),
    )(dq, kvg, n)


def local(query, keys, values, out_grad, normed_input, q_start, q_len):
    s, yl, zh, x, c, zl = coords()
    start = lax.dynamic_index_in_dim(q_start, s, 0, keepdims=False)
    end = start + lax.dynamic_index_in_dim(q_len, s, 0, keepdims=False)
    pos = (jnp.arange(2, dtype=jnp.int32)[:, None, None] * 2048 + zh * 1024 + x * 256
           + jnp.arange(256, dtype=jnp.int32)[None, None, :])
    lim = jnp.maximum(start, jnp.minimum(end, pos + 1))
    q_rx, g_rx, kv = gather(query, out_grad, keys, values)
    dq, kvg = attention(q_rx, g_rx, kv.reshape(4096, 256), lim)
    return reduce_all(dq, kvg.reshape(2, 2, 4, 256, 256), normed_input)


def solution(mesh):
    tok = P("dp", "seq", None)
    return jax.shard_map(
        local, mesh=mesh,
        in_specs=(tok, tok, tok, tok, tok, P("dp"), P("dp")),
        out_specs=(tok, tok, tok, P(("seq", "dp"), None)),
        check_vma=False)
```

```python
import math
import jax
import jax.numpy as jnp
from jax import lax
from jax.experimental import pallas as pl
from jax.experimental.pallas import tpu as pltpu
from jax.sharding import PartitionSpec as P

HEAD_DIM = 128
SCALE = 1.0 / math.sqrt(HEAD_DIM)
EXPC = SCALE * math.log2(math.e)
NEG = -1e30
F32 = jnp.float32
BF16 = jnp.bfloat16
CK = 512


def dot_nt(a, b):
    return lax.dot_general(a, b, (((1,), (1,)), ((), ())), preferred_element_type=F32)


def dot_nn(a, b):
    return lax.dot_general(a, b, (((1,), (0,)), ((), ())), preferred_element_type=F32)


def dot_tn(a, b):
    return lax.dot_general(a, b, (((0,), (0,)), ((), ())), preferred_element_type=F32)


def coords():
    seq = lax.axis_index("seq")
    c = lax.rem(seq, 2)
    x = lax.rem(seq // 2, 4)
    zh = lax.rem(seq // 8, 2)
    yl = lax.rem(seq // 16, 2)
    s = seq // 32
    zl = lax.axis_index("dp")
    return s, yl, zh, x, c, zl


def seq_of(s, yl, zh, x, c):
    return s * 32 + yl * 16 + zh * 8 + x * 2 + c


def rcopy(src, dst, ssem, rsem, dev):
    return pltpu.make_async_remote_copy(
        src_ref=src, dst_ref=dst, send_sem=ssem, recv_sem=rsem,
        device_id={"seq": dev[0], "dp": dev[1]}, device_id_type=pl.DeviceIdType.MESH)


def greet(peers):
    barrier = pltpu.get_barrier_semaphore()
    for seq, dp in peers:
        pl.semaphore_signal(barrier, inc=1, device_id={"seq": seq, "dp": dp},
                            device_id_type=pl.DeviceIdType.MESH)
    pl.semaphore_wait(barrier, len(peers))


def blk(i, w):
    return pl.ds(pl.multiple_of(i * w, w), w)


def body(q_in, g_in, k_in, v_in, n_in, start_ref, len_ref,
         dq_out, kg_out, vg_out, w_out,
         q_ref, g_ref, kv, nbuf, s_ref, d_ref, dk_ref, dv_ref, dq_ref,
         csend, crx, ysend, yrx, acc0, acc1, zsend, zrx, kga,
         w1s, w1r, w2s, w2r, w3s, w4r,
         kx_s, kx_r, qx_s, qx_r, kz_s, kz_r, ky_s, ky_r, kc_s, kc_r, n_s, n_r, dq_s, dq_r,
         c_s, c_r, y_s, y_r, z_s, z_r, kc2_s, kc2_r, ko_s, ko_r,
         w1_s, w1_r, w2_s, w2_r, w4_s, w4_r, l_sem, nl_sem, dql_sem):
    s, yl, zh, x, c, zl = coords()
    y = s * 2 + yl
    z = zh * 4 + zl
    me8 = x * 2 + c

    def dev(s_=None, yl_=None, zh_=None, x_=None, c_=None, zl_=None):
        return (seq_of(s if s_ is None else s_, yl if yl_ is None else yl_, zh if zh_ is None else zh_,
                       x if x_ is None else x_, c if c_ is None else c_), zl if zl_ is None else zl_)

    row8 = [lax.rem(me8 + d, 8) for d in range(1, 8)]
    xs = [lax.rem(x + d, 4) for d in range(1, 4)]
    ys = [lax.rem(y + d, 4) for d in range(1, 4)]
    zs = [lax.rem(z + d, 8) for d in range(1, 8)]
    ydev = [dev(s_=p // 2, yl_=lax.rem(p, 2)) for p in ys]
    zdev = [dev(zh_=p // 4, zl_=lax.rem(p, 4)) for p in zs]
    core_dev = dev(c_=1 - c)
    y_dev = dev(yl_=1 - yl)
    z_dev = dev(zh_=1 - zh)
    greet([dev(x_=p // 2, c_=lax.rem(p, 2)) for p in row8] + ydev + zdev)

    sends = []

    def go(cp):
        cp.start()
        sends.append(cp)
        return cp

    crow = blk(c, 128)
    orow = blk(1 - c, 128)

    kx = []
    for i, px in enumerate(xs):
        kx.append((go(rcopy(k_in.at[0, :, blk(px, 128)], kv.at[yl, zh, x, crow, pl.ds(0, 128)],
                            kx_s.at[0, i], kx_r.at[0, i], dev(x_=px))),
                   go(rcopy(v_in.at[0, :, blk(px, 128)], kv.at[yl, zh, x, crow, pl.ds(128, 128)],
                            kx_s.at[1, i], kx_r.at[1, i], dev(x_=px)))))
    own_kv = [pltpu.make_async_copy(k_in.at[0, :, blk(x, 128)], kv.at[yl, zh, x, crow, pl.ds(0, 128)], l_sem.at[0]),
              pltpu.make_async_copy(v_in.at[0, :, blk(x, 128)], kv.at[yl, zh, x, crow, pl.ds(128, 128)], l_sem.at[1])]
    own_q = [pltpu.make_async_copy(q_in.at[0, :, blk(x, 512)], q_ref.at[x], l_sem.at[2]),
             pltpu.make_async_copy(g_in.at[0, :, blk(x, 512)], g_ref.at[x], l_sem.at[3])]
    for cp in own_kv + own_q:
        cp.start()
    qx = []
    for i, px in enumerate(xs):
        qx.append(go(rcopy(q_in.at[0, :, blk(px, 512)], q_ref.at[x], qx_s.at[0, i], qx_r.at[0, i], dev(x_=px))))
        qx.append(go(rcopy(g_in.at[0, :, blk(px, 512)], g_ref.at[x], qx_s.at[1, i], qx_r.at[1, i], dev(x_=px))))

    def piece(yl_, zh_, k):
        return kv.at[yl_, zh_, lax.rem(x - k + 4, 4), crow]

    zc, y0, y1, cc = [], [], [], []
    for k in range(4):
        for cp in (own_kv if k == 0 else ()):
            cp.wait()
        if k:
            kx[k - 1][0].wait_recv()
            kx[k - 1][1].wait_recv()
        p = piece(yl, zh, k)
        zc.append(go(rcopy(p, p, kz_s.at[k], kz_r.at[k], z_dev)))
        y0.append(go(rcopy(p, p, ky_s.at[0, k], ky_r.at[0, k], y_dev)))
        cc.append(go(rcopy(p, p, kc_s.at[0, k], kc_r.at[0, k], core_dev)))
    for k in range(4):
        y0[k].wait_recv()
        p = piece(1 - yl, zh, k)
        cc.append(go(rcopy(p, p, kc_s.at[1, k], kc_r.at[1, k], core_dev)))
    for k in range(4):
        zc[k].wait_recv()
        p = piece(yl, 1 - zh, k)
        y1.append(go(rcopy(p, p, ky_s.at[1, k], ky_r.at[1, k], y_dev)))
        cc.append(go(rcopy(p, p, kc_s.at[2, k], kc_r.at[2, k], core_dev)))
    for cp in own_q:
        cp.wait()
    for cp in qx:
        cp.wait_recv()

    def nsend(rr, carry):
        for i, t in enumerate(row8):
            tc = lax.rem(t, 2)
            rcopy(n_in.at[0, :, pl.ds(pl.multiple_of(rr * 512 + tc * 256, 256), 256)], nbuf.at[rr, x, c],
                  n_s.at[i, rr], n_r.at[i, rr], dev(x_=t // 2, c_=tc)).start()
        pltpu.make_async_copy(n_in.at[0, :, pl.ds(pl.multiple_of(rr * 512 + c * 256, 256), 256)],
                              nbuf.at[rr, x, c], nl_sem.at[rr]).start()
        return carry

    lax.fori_loop(0, 8, nsend, 0)

    for k in range(4):
        y1[k].wait_recv()
        p = piece(1 - yl, 1 - zh, k)
        cc.append(go(rcopy(p, p, kc_s.at[3, k], kc_r.at[3, k], core_dev)))
    for cp in cc:
        cp.wait_recv()

    start = start_ref[s]
    end = start + len_ref[s]
    dk_ref[...] = jnp.zeros_like(dk_ref)
    dv_ref[...] = jnp.zeros_like(dv_ref)
    lane = lax.broadcasted_iota(jnp.int32, (1, 256), 1)

    def keys(j):
        return kv[j // 4, (j // 2) % 2, (j % 2) * 2:(j % 2) * 2 + 2, :, 0:128].reshape(CK, 128)

    def values(j):
        return kv[j // 4, (j // 2) % 2, (j % 2) * 2:(j % 2) * 2 + 2, :, 128:256].reshape(CK, 128)

    def unit(h, half, nk):
        cols = blk(h, 128)
        q = q_ref[2 * half:2 * half + 2, :, cols].reshape(256, 128)
        g = g_ref[2 * half:2 * half + 2, :, cols].reshape(256, 128)
        pos = yl * 2048 + zh * 1024 + (2 * half + lane // 128) * 256 + c * 128 + lax.rem(lane, 128)
        lim = jnp.maximum(start, jnp.minimum(end, pos + 1))
        m = jnp.full((1, 256), NEG, F32)
        for j in range(nk):
            rows = pl.ds(j * CK, CK)
            sc = dot_nt(keys(j), q)
            if j >= 4:
                kpos = lax.broadcasted_iota(jnp.int32, (CK, 256), 0) + j * CK
                sc = jnp.where(kpos < lim, sc, NEG)
            s_ref[rows, :] = sc
            m = jnp.maximum(m, jnp.max(sc, axis=0, keepdims=True))
        l = jnp.zeros((1, 256), F32)
        dl = jnp.zeros((1, 256), F32)
        for j in range(nk):
            rows = pl.ds(j * CK, CK)
            e = jnp.exp2((s_ref[rows, :] - m) * EXPC)
            dp = dot_nt(values(j), g)
            l = l + jnp.sum(e, axis=0, keepdims=True)
            dl = dl + jnp.sum(e * dp, axis=0, keepdims=True)
            s_ref[rows, :] = e
            d_ref[rows, :] = dp
        inv = 1.0 / l
        delta = dl * inv
        dq = jnp.zeros((256, 128), F32)
        for j in range(nk):
            rows = pl.ds(j * CK, CK)
            p = s_ref[rows, :] * inv
            ds = (p * (d_ref[rows, :] - delta)).astype(BF16)
            dk_ref[rows, :] += dot_nn(ds, q)
            dv_ref[rows, :] += dot_nn(p.astype(BF16), g)
            dq = dq + dot_tn(ds, keys(j))
        dq_ref[2 * half:2 * half + 2, :, cols] = (dq * SCALE).astype(BF16).reshape(2, 128, 128)

    def dq_copy(h, i):
        px = xs[i]
        return rcopy(dq_ref.at[px, :, blk(h, 128)], dq_out.at[0, :, blk(x * 4 + h, 128)],
                     dq_s.at[h, i], dq_r.at[h, i], dev(x_=px))

    def dq_local(h):
        return pltpu.make_async_copy(dq_ref.at[x, :, blk(h, 128)], dq_out.at[0, :, blk(x * 4 + h, 128)],
                                     dql_sem.at[h])

    def heads(nk):
        def head(h, carry):
            unit(h, 0, nk)
            unit(h, 1, nk)
            for i in range(3):
                dq_copy(h, i).start()
            dq_local(h).start()
            return carry
        lax.fori_loop(0, 4, head, 0)

    last = yl * zh

    @pl.when(last == 1)
    def _():
        heads(7)

    @pl.when(last == 0)
    def _():
        heads(6)

    def grads(yl_, zh_, x_, c_):
        r = pl.ds(pl.multiple_of(((yl_ * 2 + zh_) * 4 + x_) * 256 + c_ * 128, 128), 128)
        return jnp.concatenate([dk_ref[r, :] * SCALE, dv_ref[r, :]], axis=1)

    quad = [(1 - yl, 1 - zh), (yl, 1 - zh), (1 - yl, zh), (yl, zh)]
    cx = []
    for k, (a, b) in enumerate(quad):
        for x_ in range(4):
            csend[k, x_] = grads(a, b, x_, 1 - c).astype(BF16)
        cx.append(go(rcopy(csend.at[k], crx.at[k], c_s.at[k], c_r.at[k], core_dev)))

    def pair(k, x_):
        a, b = quad[k]
        return grads(a, b, x_, c) + crx[k, x_].astype(F32)

    yx = {}

    def y_stage(k, slot):
        cx[k].wait_recv()
        for hp in range(2):
            for x_ in (2 * hp, 2 * hp + 1):
                ysend[slot, x_] = pair(k, x_).astype(BF16)
            part = pl.ds(2 * hp, 2)
            yx[slot, hp] = go(rcopy(ysend.at[slot, part], yrx.at[slot, part], y_s.at[slot, hp], y_r.at[slot, hp], y_dev))

    y_stage(0, 0)
    cx[1].wait_recv()
    for x_ in range(4):
        acc1[x_] = pair(1, x_)
    y_stage(2, 1)
    cx[3].wait_recv()
    for x_ in range(4):
        acc0[x_] = pair(3, x_)
    zx = []
    for hp in range(2):
        yx[0, hp].wait_recv()
        part = pl.ds(2 * hp, 2)
        zsend[part] = (acc1[part] + yrx[0, part].astype(F32)).astype(BF16)
        zx.append(go(rcopy(zsend.at[part], zrx.at[part], z_s.at[hp], z_r.at[hp], z_dev)))
    for hp in range(2):
        yx[1, hp].wait_recv()
    acc0[...] = acc0[...] + yrx[1].astype(F32)

    def nwait(rr, carry):
        for i, t in enumerate(row8):
            tc = lax.rem(t, 2)
            cp = rcopy(n_in.at[0, :, pl.ds(pl.multiple_of(rr * 512 + tc * 256, 256), 256)], nbuf.at[rr, x, c],
                       n_s.at[i, rr], n_r.at[i, rr], dev(x_=t // 2, c_=tc))
            cp.wait_send()
            cp.wait_recv()
        pltpu.make_async_copy(n_in.at[0, :, pl.ds(pl.multiple_of(rr * 512 + c * 256, 256), 256)],
                              nbuf.at[rr, x, c], nl_sem.at[rr]).wait()
        return carry

    lax.fori_loop(0, 8, nwait, 0)
    k2 = []
    for hp in range(2):
        zx[hp].wait_recv()
        part = pl.ds(2 * hp, 2)
        kga[part, pl.ds(c, 1)] = (acc0[part] + zrx[part].astype(F32)).astype(BF16).reshape(2, 1, 128, 256)
        mine = kga.at[part, c]
        k2.append(go(rcopy(mine, mine, kc2_s.at[hp], kc2_r.at[hp], core_dev)))
    ko = []
    for i, px in enumerate(xs):
        ko.append(go(rcopy(kga.at[px, c, :, pl.ds(0, 128)], kg_out.at[0, :, blk(x, 128)],
                           ko_s.at[0, i], ko_r.at[0, i], dev(x_=px))))
        ko.append(go(rcopy(kga.at[px, c, :, pl.ds(128, 128)], vg_out.at[0, :, blk(x, 128)],
                           ko_s.at[1, i], ko_r.at[1, i], dev(x_=px))))
    ko_own = [pltpu.make_async_copy(kga.at[x, c, :, pl.ds(0, 128)], kg_out.at[0, :, blk(x, 128)], l_sem.at[4]),
              pltpu.make_async_copy(kga.at[x, c, :, pl.ds(128, 128)], vg_out.at[0, :, blk(x, 128)], l_sem.at[5])]
    for cp in ko_own:
        cp.start()
    for cp in k2:
        cp.wait_recv()

    kgall = kga[...].reshape(1024, 256)
    w1 = []
    for d in range(4):
        py = lax.rem(y + d + 1, 4)
        for b in range(2):
            part = dot_tn(nbuf[py * 2 + b].reshape(1024, 256), kgall)
            w1s[d, b] = part.astype(BF16)
        if d < 3:
            w1.append(go(rcopy(w1s.at[d], w1r.at[d], w1_s.at[d], w1_r.at[d], ydev[d])))
    for cp in w1:
        cp.wait_recv()
    for b in range(2):
        t = w1s[3, b].astype(F32)
        for d in range(3):
            t = t + w1r[d, b].astype(F32)
        w2s[b] = t.astype(BF16).reshape(4, 4, 16, 256)
    w2 = []
    for i, pz in enumerate(zs):
        w2.append(go(rcopy(w2s.at[pz // 4, :, lax.rem(pz, 4)], w2r.at[i], w2_s.at[i], w2_r.at[i], zdev[i])))
    for cp in w2:
        cp.wait_recv()
    t = w2s[zh, :, pl.ds(zl, 1)].reshape(4, 16, 256).astype(F32)
    for i in range(7):
        t = t + w2r[i].astype(F32)
    w3s[...] = t
    self_core = x // 2

    def w4_copy(xl, cc_):
        return rcopy(w3s.at[xl * 2 + cc_], w4r.at[x], w4_s.at[xl * 2 + cc_], w4_r.at[x],
                     dev(x_=2 * c + xl, c_=cc_))

    for xl in range(2):
        for cc_ in range(2):
            is_me = (2 * c + xl == x) & (c == cc_)

            @pl.when(is_me)
            def _():
                w4r[pl.ds(x, 1)] = w3s[xl * 2 + cc_].reshape(1, 16, 256)

            @pl.when(jnp.logical_not(is_me))
            def _():
                w4_copy(xl, cc_).start()
    for xx in range(4):
        @pl.when(jnp.logical_not((x == xx) & (c == self_core)))
        def _():
            rcopy(w3s.at[0], w4r.at[xx], w4_s.at[0], w4_r.at[xx], core_dev).wait_recv()
    for xx in range(4):
        w_out[:, xx * 128:(xx + 1) * 128] = w4r[xx, :, 0:128]
        w_out[:, 512 + xx * 128:512 + (xx + 1) * 128] = w4r[xx, :, 128:256]
    for xl in range(2):
        for cc_ in range(2):
            @pl.when(jnp.logical_not((2 * c + xl == x) & (c == cc_)))
            def _():
                w4_copy(xl, cc_).wait_send()
    for h in range(4):
        for i in range(3):
            dq_copy(h, i).wait()
        dq_local(h).wait()
    for cp in ko:
        cp.wait_recv()
    for cp in ko_own:
        cp.wait()
    for cp in sends:
        cp.wait_send()


def local(query, keys, values, out_grad, normed_input, q_start, q_len):
    dma = pltpu.SemaphoreType.DMA
    V = pltpu.VMEM
    hbm = pl.BlockSpec(memory_space=pl.ANY)
    smem = pl.BlockSpec(memory_space=pltpu.SMEM)
    return pl.pallas_call(
        body,
        name="attention_grads",
        out_shape=(jax.ShapeDtypeStruct((1, 128, 2048), BF16), jax.ShapeDtypeStruct((1, 128, 512), BF16),
                   jax.ShapeDtypeStruct((1, 128, 512), BF16), jax.ShapeDtypeStruct((16, 1024), F32)),
        in_specs=[hbm] * 5 + [smem] * 2,
        out_specs=[hbm] * 3 + [pl.BlockSpec(memory_space=pltpu.VMEM)],
        scratch_shapes=[
            V((4, 128, 512), BF16), V((4, 128, 512), BF16), V((2, 2, 4, 256, 256), BF16),
            V((8, 4, 2, 128, 256), BF16),
            V((3584, 256), F32), V((3584, 256), F32), V((4096, 128), F32), V((4096, 128), F32),
            V((4, 128, 512), BF16),
            V((4, 4, 128, 256), BF16), V((4, 4, 128, 256), BF16),
            V((2, 4, 128, 256), BF16), V((2, 4, 128, 256), BF16),
            V((4, 128, 256), F32), V((4, 128, 256), F32), V((4, 128, 256), BF16), V((4, 128, 256), BF16),
            V((4, 2, 128, 256), BF16),
            V((4, 2, 256, 256), BF16), V((3, 2, 256, 256), BF16), V((2, 4, 4, 16, 256), BF16),
            V((7, 4, 16, 256), BF16), V((4, 16, 256), F32), V((4, 16, 256), F32),
            dma((2, 3)), dma((2, 3)), dma((2, 3)), dma((2, 3)), dma((4,)), dma((4,)), dma((2, 4)), dma((2, 4)),
            dma((4, 4)), dma((4, 4)), dma((7, 8)), dma((7, 8)), dma((4, 3)), dma((4, 3)),
            dma((4,)), dma((4,)), dma((2, 2)), dma((2, 2)), dma((2,)), dma((2,)), dma((2,)), dma((2,)),
            dma((2, 3)), dma((2, 3)),
            dma((3,)), dma((3,)), dma((7,)), dma((7,)), dma((4,)), dma((4,)), dma((6,)), dma((8,)), dma((4,)),
        ],
        compiler_params=pltpu.CompilerParams(collective_id=0, has_side_effects=True, vmem_limit_bytes=56 << 20),
    )(query, out_grad, keys, values, normed_input, q_start, q_len)


def solution(mesh):
    tok = P("dp", "seq", None)
    return jax.shard_map(
        local, mesh=mesh,
        in_specs=(tok, tok, tok, tok, tok, P("dp"), P("dp")),
        out_specs=(tok, tok, tok, P(("seq", "dp"), None)),
        check_vma=False)
```

```python
import math
import jax
import jax.numpy as jnp
from jax import lax
from jax.experimental import pallas as pl
from jax.experimental.pallas import tpu as pltpu
from jax.sharding import PartitionSpec as P

HEAD_DIM = 128
SCALE = 1.0 / math.sqrt(HEAD_DIM)
EXPC = SCALE * math.log2(math.e)
NEG = -1e30
F32 = jnp.float32
BF16 = jnp.bfloat16
CK = 512


def dot_nt(a, b):
    return lax.dot_general(a, b, (((1,), (1,)), ((), ())), preferred_element_type=F32)


def dot_nn(a, b):
    return lax.dot_general(a, b, (((1,), (0,)), ((), ())), preferred_element_type=F32)


def dot_tn(a, b):
    return lax.dot_general(a, b, (((0,), (0,)), ((), ())), preferred_element_type=F32)


def coords():
    seq = lax.axis_index("seq")
    c = lax.rem(seq, 2)
    x = lax.rem(seq // 2, 4)
    zh = lax.rem(seq // 8, 2)
    yl = lax.rem(seq // 16, 2)
    s = seq // 32
    zl = lax.axis_index("dp")
    return s, yl, zh, x, c, zl


def seq_of(s, yl, zh, x, c):
    return s * 32 + yl * 16 + zh * 8 + x * 2 + c


def rcopy(src, dst, ssem, rsem, dev):
    return pltpu.make_async_remote_copy(
        src_ref=src, dst_ref=dst, send_sem=ssem, recv_sem=rsem,
        device_id={"seq": dev[0], "dp": dev[1]}, device_id_type=pl.DeviceIdType.MESH)


def greet(peers):
    barrier = pltpu.get_barrier_semaphore()
    for seq, dp in peers:
        pl.semaphore_signal(barrier, inc=1, device_id={"seq": seq, "dp": dp},
                            device_id_type=pl.DeviceIdType.MESH)
    pl.semaphore_wait(barrier, len(peers))


def blk(i, w):
    return pl.ds(pl.multiple_of(i * w, w), w)


def body(q_in, g_in, k_in, v_in, n_in, start_ref, len_ref,
         dq_out, kg_out, vg_out, w_out,
         q_ref, g_ref, kv, nbuf, s_ref, d_ref, dk_ref, dv_ref, dq_ref,
         csend, crx, ysend, yrx, acc0, acc1, zsend, zrx, kga,
         w1s, w1r, w1o, kt_ref, st, fac, dlt, dqa, w2s, w2r, w3s, w4r,
         kx_s, kx_r, qx_s, qx_r, kz_s, kz_r, ky_s, ky_r, kc_s, kc_r, n_s, n_r, nf_s, nf_r, nc_s, nc_r, dq_s, dq_r,
         c_s, c_r, y_s, y_r, z_s, z_r, kc2_s, kc2_r, ko_s, ko_r,
         w1_s, w1_r, w2_s, w2_r, w4_s, w4_r, l_sem, nl_sem, dql_sem):
    s, yl, zh, x, c, zl = coords()
    y = s * 2 + yl
    z = zh * 4 + zl
    me8 = x * 2 + c

    def dev(s_=None, yl_=None, zh_=None, x_=None, c_=None, zl_=None):
        return (seq_of(s if s_ is None else s_, yl if yl_ is None else yl_, zh if zh_ is None else zh_,
                       x if x_ is None else x_, c if c_ is None else c_), zl if zl_ is None else zl_)

    row8 = [lax.rem(me8 + d, 8) for d in range(1, 8)]
    xs = [lax.rem(x + d, 4) for d in range(1, 4)]
    ys = [lax.rem(y + d, 4) for d in range(1, 4)]
    zs = [lax.rem(z + d, 8) for d in range(1, 8)]
    ydev = [dev(s_=p // 2, yl_=lax.rem(p, 2)) for p in ys]
    zdev = [dev(zh_=p // 4, zl_=lax.rem(p, 4)) for p in zs]
    core_dev = dev(c_=1 - c)
    y_dev = dev(yl_=1 - yl)
    z_dev = dev(zh_=1 - zh)
    greet([dev(x_=p // 2, c_=lax.rem(p, 2)) for p in row8] + ydev + zdev)

    sends = []

    def go(cp):
        cp.start()
        sends.append(cp)
        return cp

    crow = blk(c, 128)
    last = yl * zh

    def slot(yl_, zh_, plane):
        return jnp.where(yl_ == 0, jnp.where(zh_ == plane, 0, 1), 2 + zh_)

    mine = slot(yl, zh, zh)
    kx = []
    for i, px in enumerate(xs):
        kx.append((go(rcopy(k_in.at[0, :, blk(px, 128)], kv.at[mine, x, crow, pl.ds(0, 128)],
                            kx_s.at[0, i], kx_r.at[0, i], dev(x_=px))),
                   go(rcopy(v_in.at[0, :, blk(px, 128)], kv.at[mine, x, crow, pl.ds(128, 128)],
                            kx_s.at[1, i], kx_r.at[1, i], dev(x_=px)))))
    own_kv = [pltpu.make_async_copy(k_in.at[0, :, blk(x, 128)], kv.at[mine, x, crow, pl.ds(0, 128)], l_sem.at[0]),
              pltpu.make_async_copy(v_in.at[0, :, blk(x, 128)], kv.at[mine, x, crow, pl.ds(128, 128)], l_sem.at[1])]
    own_q = [pltpu.make_async_copy(q_in.at[0, :, blk(x, 512)], q_ref.at[x], l_sem.at[2]),
             pltpu.make_async_copy(g_in.at[0, :, blk(x, 512)], g_ref.at[x], l_sem.at[3])]
    for cp in own_kv + own_q:
        cp.start()

    def q_send(ph):
        out = []
        for i, px in enumerate(xs):
            src = pl.ds(pl.multiple_of(px * 512 + ph * 256, 256), 256)
            dst = pl.ds(ph * 256, 256)
            out.append(go(rcopy(q_in.at[0, :, src], q_ref.at[x, :, dst], qx_s.at[ph, 0, i], qx_r.at[ph, 0, i], dev(x_=px))))
            out.append(go(rcopy(g_in.at[0, :, src], g_ref.at[x, :, dst], qx_s.at[ph, 1, i], qx_r.at[ph, 1, i], dev(x_=px))))
        return out

    qx0 = q_send(0)

    def piece(sl, k):
        return kv.at[sl, lax.rem(x - k + 4, 4), crow]

    zc, y0, y1 = [], [], []
    cc = [[], [], [], []]

    def to_core(e, k, p):
        cc[e].append(go(rcopy(p, p, kc_s.at[e, k], kc_r.at[e, k], core_dev)))

    for k in range(4):
        for cp in (own_kv if k == 0 else kx[k - 1]):
            cp.wait() if k == 0 else cp.wait_recv()
        zc.append(go(rcopy(piece(mine, k), piece(slot(yl, zh, 1 - zh), k), kz_s.at[k], kz_r.at[k], z_dev)))
        y0.append(go(rcopy(piece(mine, k), piece(mine, k), ky_s.at[0, k], ky_r.at[0, k], y_dev)))
        to_core(0, k, piece(mine, k))
    ev = [mine, slot(1 - yl, zh, zh), slot(yl, 1 - zh, zh), slot(1 - yl, 1 - zh, zh)]

    dk_ref[...] = jnp.zeros_like(dk_ref)
    dv_ref[...] = jnp.zeros_like(dv_ref)
    st[:, 0] = jnp.full((8, 16, 256), NEG, F32)
    st[:, 1:3] = jnp.zeros((8, 2, 16, 256), F32)
    dqa[...] = jnp.zeros_like(dqa)
    start = start_ref[s]
    end = start + len_ref[s]
    lane = lax.broadcasted_iota(jnp.int32, (1, 256), 1)

    def keys(j, n):
        if isinstance(j, int):
            return kv[j // 4, j % 4:j % 4 + n].reshape(n * 256, 256)[:, 0:128]
        return kv[j // 4, pl.ds(lax.rem(j, 4), n), :, 0:128].reshape(n * 256, 128)

    def values(j):
        return kv[j // 4, j % 4, :, 128:256]

    def rows_of(j, n=1):
        return pl.ds(j * 256 if isinstance(j, int) else pl.multiple_of(j * 256, 256), n * 256)

    def unit(u):
        h, half = u // 2, (u % 2 if isinstance(u, int) else lax.rem(u, 2))
        cols = pl.ds(h * 128 if isinstance(h, int) else pl.multiple_of(h * 128, 128), 128)
        xx = pl.ds(2 * half, 2)
        pos = yl * 2048 + zh * 1024 + (2 * half + lane // 128) * 256 + c * 128 + lax.rem(lane, 128)
        lim = jnp.maximum(start, jnp.minimum(end, pos + 1))
        return q_ref[xx, :, cols].reshape(256, 128), g_ref[xx, :, cols].reshape(256, 128), lim

    def dq_store(u, dq):
        h, half = u // 2, (u % 2 if isinstance(u, int) else lax.rem(u, 2))
        cols = pl.ds(h * 128 if isinstance(h, int) else pl.multiple_of(h * 128, 128), 128)
        dq_ref[pl.ds(2 * half, 2), :, cols] = (dq.T * SCALE).astype(BF16).reshape(2, 128, 128)

    def pass12(u, su, j, masked):
        q, g, lim = unit(u)
        rows = rows_of(j)
        sc = dot_nt(kv[j // 4, (j % 4 if isinstance(j, int) else lax.rem(j, 4)), :, 0:128], q)
        if masked:
            kpos = lax.broadcasted_iota(jnp.int32, (256, 256), 0)
            sc = jnp.where(kpos < lim - j * 256, sc, NEG)
        m = jnp.max(sc, axis=0, keepdims=True)
        e = jnp.exp2((sc - m) * EXPC)
        dp = dot_nt(kv[j // 4, (j % 4 if isinstance(j, int) else lax.rem(j, 4)), :, 128:256], g)
        st[u, 0, pl.ds(j, 1)] = m
        st[u, 1, pl.ds(j, 1)] = jnp.sum(e, axis=0, keepdims=True)
        st[u, 2, pl.ds(j, 1)] = jnp.sum(e * dp, axis=0, keepdims=True)
        s_ref[su, rows, :] = e
        d_ref[su, rows, :] = dp

    def finish(u, su):
        m = jnp.max(st[u, 0], axis=0, keepdims=True)
        f = jnp.exp2((st[u, 0] - m) * EXPC)
        f = f * (1.0 / jnp.sum(st[u, 1] * f, axis=0, keepdims=True))
        fac[su] = f
        dlt[su] = jnp.sum(st[u, 2] * f, axis=0, keepdims=True)

    def pass3(u, su, j, n, dq):
        q, g, _ = unit(u)
        dlv = dlt[su]
        ds_, p_ = [], []
        for i in range(n):
            r = rows_of(j + i)
            p = s_ref[su, r, :] * fac[su, pl.ds(j + i, 1)]
            ds_.append((p * (d_ref[su, r, :] - dlv)).astype(BF16))
            p_.append(p.astype(BF16))
        ds = ds_[0] if n == 1 else jnp.concatenate(ds_, axis=0)
        p = p_[0] if n == 1 else jnp.concatenate(p_, axis=0)
        rows = rows_of(j, n)
        dk_ref[rows, :] += dot_nn(ds, q)
        dv_ref[rows, :] += dot_nn(p, g)
        return dq + dot_nn(kt_ref[:, rows], ds)

    def arrive(e):
        sl = ev[e]

        def one(b, carry):
            j = sl * 4 + b
            kt_ref[:, rows_of(j)] = keys(j, 1).T
            for u in range(4):
                pass12(u, u, j, True)
            return carry
        lax.fori_loop(0, jnp.where(sl < 3, 4, 2 * last), one, 0)

    for k in range(4):
        y0[k].wait_recv()
        to_core(1, k, piece(ev[1], k))
    for cp in own_q:
        cp.wait()
    for cp in qx0:
        cp.wait_recv()
    qx1 = q_send(1)
    for cp in cc[0]:
        cp.wait_recv()
    arrive(0)

    def n_copy(rr, side, cc_):
        px = lax.rem(x + (1 if side == 0 else 3), 4)
        return rcopy(n_in.at[0, :, pl.ds(pl.multiple_of(rr * 512 + cc_ * 256, 256), 256)], nbuf.at[rr, x, c],
                     n_s.at[side, cc_, rr], n_r.at[side, c, rr], dev(x_=px, c_=cc_))

    def n_fwd(i, side, cc_):
        rr = i + 4 * side
        src = nbuf.at[rr, lax.rem(x + (3 if side == 0 else 1), 4), cc_]
        px = lax.rem(x + (1 if side == 0 else 3), 4)
        return rcopy(src, src, nf_s.at[side, cc_, i], nf_r.at[side, cc_, i], dev(x_=px))

    def n_core(rr):
        return rcopy(n_in.at[0, :, pl.ds(pl.multiple_of(rr * 512 + (1 - c) * 256, 256), 256)], nbuf.at[rr, x, c],
                     nc_s.at[rr], nc_r.at[rr], core_dev)

    def n_local(rr):
        return pltpu.make_async_copy(n_in.at[0, :, pl.ds(pl.multiple_of(rr * 512 + c * 256, 256), 256)],
                                     nbuf.at[rr, x, c], nl_sem.at[rr])

    def nsend(i, carry):
        for cc_ in range(2):
            n_copy(i, 0, cc_).start()
            n_copy(lax.rem(i + 4, 8), 1, cc_).start()
        n_core(i).start()
        n_local(i).start()
        return carry

    for k in range(2):
        zc[k].wait_recv()
        p = piece(ev[2], k)
        y1.append(go(rcopy(p, piece(slot(yl, 1 - zh, zh), k), ky_s.at[1, k], ky_r.at[1, k], y_dev)))
        to_core(2, k, p)
    lax.fori_loop(0, 8, nsend, 0)
    for cp in cc[1]:
        cp.wait_recv()
    arrive(1)
    for k in range(2, 4):
        zc[k].wait_recv()
        p = piece(ev[2], k)
        y1.append(go(rcopy(p, piece(slot(yl, 1 - zh, zh), k), ky_s.at[1, k], ky_r.at[1, k], y_dev)))
        to_core(2, k, p)
    for k in range(4):
        y1[k].wait_recv()
        to_core(3, k, piece(ev[3], k))
    for cp in cc[2]:
        cp.wait_recv()
    arrive(2)
    for cp in cc[3]:
        cp.wait_recv()
    arrive(3)
    for u in range(4):
        finish(u, u)
    for cp in qx1:
        cp.wait_recv()

    def mid(u, carry):
        dq = jnp.zeros((128, 256), F32)
        for j in range(12):
            dq = pass3(u, u, j, 1, dq)
            pass12(u + 4, u, j, j >= 8)
        dqa[4] = dq

        @pl.when(last == 1)
        def _():
            d2 = dqa[4]
            for j in range(12, 14):
                d2 = pass3(u, u, j, 1, d2)
                pass12(u + 4, u, j, True)
            dqa[4] = d2
        dq_store(u, dqa[4])
        finish(u + 4, u)
        return carry

    lax.fori_loop(0, 3, mid, 0)

    def fwd(i, carry):
        for side in range(2):
            for cc_ in range(2):
                rcopy(nbuf.at[0, 0, 0], nbuf.at[i + 4 * side, x, cc_], n_s.at[side, cc_, i],
                      n_r.at[side, cc_, i + 4 * side], core_dev).wait_recv()
                n_fwd(i, side, cc_).start()
        return carry

    lax.fori_loop(0, 4, fwd, 0)
    lax.fori_loop(3, 4, mid, 0)

    def dq_copy(h, i):
        px = xs[i]
        return rcopy(dq_ref.at[px, :, blk(h, 128)], dq_out.at[0, :, blk(x * 4 + h, 128)],
                     dq_s.at[h, i], dq_r.at[h, i], dev(x_=px))

    def dq_local(h):
        return pltpu.make_async_copy(dq_ref.at[x, :, blk(h, 128)], dq_out.at[0, :, blk(x * 4 + h, 128)],
                                     dql_sem.at[h])

    def dq_send(h):
        for i in range(3):
            dq_copy(h, i).start()
        dq_local(h).start()

    dq_send(0)
    dq_send(1)

    def back(sl, trips):
        def two(b, carry):
            for u in range(4):
                dqa[u] = pass3(u + 4, u, sl * 4 + 2 * b, 2, dqa[u])
            return carry
        lax.fori_loop(0, trips, two, 0)

    def grads(yl_, zh_, x_, c_):
        r = pl.ds(pl.multiple_of((slot(yl_, zh_, zh) * 4 + x_) * 256 + c_ * 128, 128), 128)
        return jnp.concatenate([dk_ref[r, :] * SCALE, dv_ref[r, :]], axis=1)

    quad = [(1 - yl, 1 - zh), (yl, 1 - zh), (1 - yl, zh), (yl, zh)]
    cx = []

    def core_send(k):
        for x_ in range(4):
            csend[k, x_] = grads(quad[k][0], quad[k][1], x_, 1 - c).astype(BF16)
        cx.append(go(rcopy(csend.at[k], crx.at[k], c_s.at[k], c_r.at[k], core_dev)))

    def pair(k, x_):
        return grads(quad[k][0], quad[k][1], x_, c) + crx[k, x_].astype(F32)

    yx = {}

    def y_stage(k, sl):
        cx[k].wait_recv()
        for hp in range(2):
            for x_ in (2 * hp, 2 * hp + 1):
                ysend[sl, x_] = pair(k, x_).astype(BF16)
            part = pl.ds(2 * hp, 2)
            yx[sl, hp] = go(rcopy(ysend.at[sl, part], yrx.at[sl, part], y_s.at[sl, hp], y_r.at[sl, hp], y_dev))

    back(1, 2)
    back(2, 2 * zh)
    core_send(0)
    core_send(1)
    back(0, 2)
    y_stage(0, 0)
    cx[1].wait_recv()
    for x_ in range(4):
        acc1[x_] = pair(1, x_)
    back(2, 2 * (1 - zh))
    back(3, last)
    core_send(2)
    core_send(3)
    zx = []
    for hp in range(2):
        yx[0, hp].wait_recv()
        part = pl.ds(2 * hp, 2)
        zsend[part] = (acc1[part] + yrx[0, part].astype(F32)).astype(BF16)
        zx.append(go(rcopy(zsend.at[part], zrx.at[part], z_s.at[hp], z_r.at[hp], z_dev)))
    y_stage(2, 1)
    for u in range(4):
        dq_store(u + 4, dqa[u])
    dq_send(2)
    dq_send(3)
    cx[3].wait_recv()
    for x_ in range(4):
        acc0[x_] = pair(3, x_)
    for hp in range(2):
        yx[1, hp].wait_recv()
    acc0[...] = acc0[...] + yrx[1].astype(F32)

    def nwait(i, carry):
        for cc_ in range(2):
            for side in range(2):
                n_copy(i, side, cc_).wait_send()
        n_core(i).wait()
        n_local(i).wait()
        return carry

    def nwait4(i, carry):
        for side in range(2):
            for cc_ in range(2):
                rr = i + 4 * (1 - side)
                rcopy(nbuf.at[0, 0, 0], nbuf.at[rr, x, cc_], n_s.at[side, cc_, i],
                      n_r.at[side, cc_, rr], core_dev).wait_recv()
                n_fwd(i, side, cc_).wait()
        return carry

    lax.fori_loop(0, 8, nwait, 0)
    lax.fori_loop(0, 4, nwait4, 0)
    k2 = []
    for hp in range(2):
        zx[hp].wait_recv()
        part = pl.ds(2 * hp, 2)
        kga[part, pl.ds(c, 1)] = (acc0[part] + zrx[part].astype(F32)).astype(BF16).reshape(2, 1, 128, 256)
        own = kga.at[part, c]
        k2.append(go(rcopy(own, own, kc2_s.at[hp], kc2_r.at[hp], core_dev)))
    ko = []
    for i, px in enumerate(xs):
        ko.append(go(rcopy(kga.at[px, c, :, pl.ds(0, 128)], kg_out.at[0, :, blk(x, 128)],
                           ko_s.at[0, i], ko_r.at[0, i], dev(x_=px))))
        ko.append(go(rcopy(kga.at[px, c, :, pl.ds(128, 128)], vg_out.at[0, :, blk(x, 128)],
                           ko_s.at[1, i], ko_r.at[1, i], dev(x_=px))))
    ko_own = [pltpu.make_async_copy(kga.at[x, c, :, pl.ds(0, 128)], kg_out.at[0, :, blk(x, 128)], l_sem.at[4]),
              pltpu.make_async_copy(kga.at[x, c, :, pl.ds(128, 128)], vg_out.at[0, :, blk(x, 128)], l_sem.at[5])]
    for cp in ko_own:
        cp.start()
    for cp in k2:
        cp.wait_recv()

    kgall = kga[...].reshape(1024, 256)
    border = [1 - zh, zh]
    w1 = {}
    for bi, b in enumerate(border):
        for d in range(3):
            py = lax.rem(y + d + 1, 4)
            w1s[d, bi] = dot_tn(nbuf[py * 2 + b].reshape(1024, 256), kgall).astype(BF16)
            w1[d, bi] = go(rcopy(w1s.at[d, bi], w1r.at[d, bi], w1_s.at[d, bi], w1_r.at[d, bi], ydev[d]))
    for bi, b in enumerate(border):
        w1o[bi] = dot_tn(nbuf[y * 2 + b].reshape(1024, 256), kgall)
    w2 = []
    for bi, b in enumerate(border):
        for d in range(3):
            w1[d, bi].wait_recv()
        t = w1o[bi]
        for d in range(3):
            t = t + w1r[d, bi].astype(F32)
        w2s[bi] = t.astype(BF16).reshape(4, 4, 16, 256)
        for i in range(bi, 4):
            pz = lax.rem(zl + i, 4)
            sl = i if bi == 0 else 3 + i
            w2.append(go(rcopy(w2s.at[bi, :, pz], w2r.at[sl], w2_s.at[sl], w2_r.at[sl],
                               dev(zh_=b, zl_=pz))))
    for cp in w2:
        cp.wait_recv()
    t = w2s[1, :, pl.ds(zl, 1)].reshape(4, 16, 256).astype(F32)
    for i in range(7):
        t = t + w2r[i].astype(F32)
    w3s[...] = t
    self_core = x // 2

    def w4_copy(xl, cc_):
        return rcopy(w3s.at[xl * 2 + cc_], w4r.at[x], w4_s.at[xl * 2 + cc_], w4_r.at[x],
                     dev(x_=2 * c + xl, c_=cc_))

    for xl in range(2):
        for cc_ in range(2):
            is_me = (2 * c + xl == x) & (c == cc_)

            @pl.when(is_me)
            def _():
                w4r[pl.ds(x, 1)] = w3s[xl * 2 + cc_].reshape(1, 16, 256)

            @pl.when(jnp.logical_not(is_me))
            def _():
                w4_copy(xl, cc_).start()
    for xx in range(4):
        @pl.when(jnp.logical_not((x == xx) & (c == self_core)))
        def _():
            rcopy(w3s.at[0], w4r.at[xx], w4_s.at[0], w4_r.at[xx], core_dev).wait_recv()
    for xx in range(4):
        w_out[:, xx * 128:(xx + 1) * 128] = w4r[xx, :, 0:128]
        w_out[:, 512 + xx * 128:512 + (xx + 1) * 128] = w4r[xx, :, 128:256]
    for xl in range(2):
        for cc_ in range(2):
            @pl.when(jnp.logical_not((2 * c + xl == x) & (c == cc_)))
            def _():
                w4_copy(xl, cc_).wait_send()
    for h in range(4):
        for i in range(3):
            dq_copy(h, i).wait()
        dq_local(h).wait()
    for cp in ko:
        cp.wait_recv()
    for cp in ko_own:
        cp.wait()
    for cp in sends:
        cp.wait_send()


def local(query, keys, values, out_grad, normed_input, q_start, q_len):
    dma = pltpu.SemaphoreType.DMA
    V = pltpu.VMEM
    hbm = pl.BlockSpec(memory_space=pl.ANY)
    smem = pl.BlockSpec(memory_space=pltpu.SMEM)
    return pl.pallas_call(
        body,
        name="attention_grads",
        out_shape=(jax.ShapeDtypeStruct((1, 128, 2048), BF16), jax.ShapeDtypeStruct((1, 128, 512), BF16),
                   jax.ShapeDtypeStruct((1, 128, 512), BF16), jax.ShapeDtypeStruct((16, 1024), F32)),
        in_specs=[hbm] * 5 + [smem] * 2,
        out_specs=[hbm] * 3 + [pl.BlockSpec(memory_space=pltpu.VMEM)],
        scratch_shapes=[
            V((4, 128, 512), BF16), V((4, 128, 512), BF16), V((4, 4, 256, 256), BF16),
            V((8, 4, 2, 128, 256), BF16),
            V((4, 3584, 256), F32), V((4, 3584, 256), F32), V((4096, 128), F32), V((4096, 128), F32),
            V((4, 128, 512), BF16),
            V((4, 4, 128, 256), BF16), V((4, 4, 128, 256), BF16),
            V((2, 4, 128, 256), BF16), V((2, 4, 128, 256), BF16),
            V((4, 128, 256), F32), V((4, 128, 256), F32), V((4, 128, 256), BF16), V((4, 128, 256), BF16),
            V((4, 2, 128, 256), BF16),
            V((3, 2, 256, 256), BF16), V((3, 2, 256, 256), BF16), V((2, 256, 256), F32),
            V((128, 4096), BF16), V((8, 3, 16, 256), F32), V((4, 16, 256), F32), V((4, 1, 256), F32),
            V((5, 128, 256), F32), V((2, 4, 4, 16, 256), BF16),
            V((7, 4, 16, 256), BF16), V((4, 16, 256), F32), V((4, 16, 256), F32),
            dma((2, 3)), dma((2, 3)), dma((2, 2, 3)), dma((2, 2, 3)), dma((4,)), dma((4,)), dma((2, 4)), dma((2, 4)),
            dma((4, 4)), dma((4, 4)), dma((2, 2, 8)), dma((2, 2, 8)), dma((2, 2, 4)), dma((2, 2, 4)),
            dma((8,)), dma((8,)), dma((4, 3)), dma((4, 3)),
            dma((4,)), dma((4,)), dma((2, 2)), dma((2, 2)), dma((2,)), dma((2,)), dma((2,)), dma((2,)),
            dma((2, 3)), dma((2, 3)),
            dma((3, 2)), dma((3, 2)), dma((7,)), dma((7,)), dma((4,)), dma((4,)), dma((6,)), dma((8,)), dma((4,)),
        ],
        compiler_params=pltpu.CompilerParams(collective_id=0, has_side_effects=True, vmem_limit_bytes=60 << 20),
    )(query, out_grad, keys, values, normed_input, q_start, q_len)


def solution(mesh):
    tok = P("dp", "seq", None)
    return jax.shard_map(
        local, mesh=mesh,
        in_specs=(tok, tok, tok, tok, tok, P("dp"), P("dp")),
        out_specs=(tok, tok, tok, P(("seq", "dp"), None)),
        check_vma=False)
```

```python
import math
import jax
import jax.numpy as jnp
from jax import lax
from jax.experimental import pallas as pl
from jax.experimental.pallas import tpu as pltpu
from jax.sharding import PartitionSpec as P

HEAD_DIM = 128
SCALE = 1.0 / math.sqrt(HEAD_DIM)
EXPC = SCALE * math.log2(math.e)
NEG = -1e30
F32 = jnp.float32
BF16 = jnp.bfloat16


def dot_nt(a, b):
    return lax.dot_general(a, b, (((1,), (1,)), ((), ())), preferred_element_type=F32)


def dot_nn(a, b):
    return lax.dot_general(a, b, (((1,), (0,)), ((), ())), preferred_element_type=F32)


def dot_tn(a, b):
    return lax.dot_general(a, b, (((0,), (0,)), ((), ())), preferred_element_type=F32)


def coords():
    seq = lax.axis_index("seq")
    c = lax.rem(seq, 2)
    x = lax.rem(seq // 2, 4)
    zh = lax.rem(seq // 8, 2)
    yl = lax.rem(seq // 16, 2)
    s = seq // 32
    zl = lax.axis_index("dp")
    return s, yl, zh, x, c, zl


def seq_of(s, yl, zh, x, c):
    return s * 32 + yl * 16 + zh * 8 + x * 2 + c


def rcopy(src, dst, ssem, rsem, dev):
    return pltpu.make_async_remote_copy(
        src_ref=src, dst_ref=dst, send_sem=ssem, recv_sem=rsem,
        device_id={"seq": dev[0], "dp": dev[1]}, device_id_type=pl.DeviceIdType.MESH)


def greet(peers):
    barrier = pltpu.get_barrier_semaphore()
    for seq, dp in peers:
        pl.semaphore_signal(barrier, inc=1, device_id={"seq": seq, "dp": dp},
                            device_id_type=pl.DeviceIdType.MESH)
    pl.semaphore_wait(barrier, len(peers))


def blk(i, w):
    return pl.ds(pl.multiple_of(i * w, w), w)


def body(q_in, g_in, k_in, v_in, n_in, start_ref, len_ref,
         dq_out, kg_out, vg_out, w_out,
         q_ref, g_ref, kv, nbuf, s_ref, d_ref, dk_ref, dv_ref, dq_ref,
         csend, crx, ysend, yrx, acc0, acc1, zsend, zrx, kga,
         w1s, w1r, w1o, nt, kt_ref, st, fac, dlt, dqa, w2s, w2r, w3s, w4r,
         s1, s3, kx_r, qx_r, kz_r, ky_r, kc_r, n_s, n_r, nf_s, nf_r, nc_s, nc_r, dq_s, dq_r,
         c_r, y_r, z_r, kc2_r, ko_r, w1_r, w2_r, w4_s, w4_r, l_sem, nl_sem, dql_sem):
    s, yl, zh, x, c, zl = coords()
    y = s * 2 + yl
    z = zh * 4 + zl
    me8 = x * 2 + c

    def dev(s_=None, yl_=None, zh_=None, x_=None, c_=None, zl_=None):
        return (seq_of(s if s_ is None else s_, yl if yl_ is None else yl_, zh if zh_ is None else zh_,
                       x if x_ is None else x_, c if c_ is None else c_), zl if zl_ is None else zl_)

    row8 = [lax.rem(me8 + d, 8) for d in range(1, 8)]
    xs = [lax.rem(x + d, 4) for d in range(1, 4)]
    ys = [lax.rem(y + d, 4) for d in range(1, 4)]
    zs = [lax.rem(z + d, 8) for d in range(1, 8)]
    ydev = [dev(s_=p // 2, yl_=lax.rem(p, 2)) for p in ys]
    zdev = [dev(zh_=p // 4, zl_=lax.rem(p, 4)) for p in zs]
    core_dev = dev(c_=1 - c)
    y_dev = dev(yl_=1 - yl)
    z_dev = dev(zh_=1 - zh)
    greet([dev(x_=p // 2, c_=lax.rem(p, 2)) for p in row8] + ydev + zdev)

    sent = {}

    def go(cp, key, kb):
        cp.start()
        sent[key] = sent.get(key, 0) + kb
        return cp

    def kib(n):
        return s_ref.at[0, pl.ds(0, n)]

    def drain(sem, n):
        rcopy(kib(n), kib(n), sem, sem, (seq_of(s, yl, zh, x, 1 - c), zl)).wait_send()

    def got(sem, n):
        rcopy(kib(n), kib(n), sem, sem, (seq_of(s, yl, zh, x, 1 - c), zl)).wait_recv()

    crow = blk(c, 128)
    last = yl * zh

    def slot(yl_, zh_, plane):
        return jnp.where(yl_ == 0, jnp.where(zh_ == plane, 0, 1), 2 + zh_)

    mine = slot(yl, zh, zh)
    for i, px in enumerate(xs):
        go(rcopy(k_in.at[0, :, blk(px, 128)], kv.at[mine, x, crow, pl.ds(0, 128)], s1, kx_r.at[i], dev(x_=px)), 1, 32)
        go(rcopy(v_in.at[0, :, blk(px, 128)], kv.at[mine, x, crow, pl.ds(128, 128)], s1, kx_r.at[i], dev(x_=px)), 1, 32)
    own_kv = [pltpu.make_async_copy(k_in.at[0, :, blk(x, 128)], kv.at[mine, x, crow, pl.ds(0, 128)], l_sem.at[0]),
              pltpu.make_async_copy(v_in.at[0, :, blk(x, 128)], kv.at[mine, x, crow, pl.ds(128, 128)], l_sem.at[1])]
    own_q = [pltpu.make_async_copy(q_in.at[0, :, blk(x, 512)], q_ref.at[x], l_sem.at[2]),
             pltpu.make_async_copy(g_in.at[0, :, blk(x, 512)], g_ref.at[x], l_sem.at[3])]
    for cp in own_kv + own_q:
        cp.start()

    def q_send(ph):
        for i, px in enumerate(xs):
            src = pl.ds(pl.multiple_of(px * 512 + ph * 256, 256), 256)
            dst = pl.ds(ph * 256, 256)
            go(rcopy(q_in.at[0, :, src], q_ref.at[x, :, dst], s1, qx_r.at[ph], dev(x_=px)), 1, 64)
            go(rcopy(g_in.at[0, :, src], g_ref.at[x, :, dst], s1, qx_r.at[ph], dev(x_=px)), 1, 64)

    q_send(0)

    def piece(sl, k):
        return kv.at[sl, lax.rem(x - k + 4, 4), crow]

    def to_core(e, k, p):
        return rcopy(p, p, s1, kc_r.at[4 * max(e - 1, 0) + k if e > 1 else e], core_dev)

    def z_copy(k):
        return rcopy(piece(mine, k), piece(slot(yl, zh, 1 - zh), k), s1, kz_r.at[k], z_dev)

    def y_copy(e, sl, k):
        return rcopy(piece(sl, k), piece(sl, k), s1, ky_r.at[4 * e + k], y_dev)

    for k in range(4):
        if k == 0:
            for cp in own_kv:
                cp.wait()
        else:
            got(kx_r.at[k - 1], 64)
        go(z_copy(k), 1, 64)
        go(y_copy(0, mine, k), 1, 64)
        go(to_core(0, k, piece(mine, k)), 1, 64)
    ev = [mine, slot(1 - yl, zh, zh), slot(yl, 1 - zh, zh), slot(1 - yl, 1 - zh, zh)]

    dk_ref[...] = jnp.zeros_like(dk_ref)
    dv_ref[...] = jnp.zeros_like(dv_ref)
    st[:, 0] = jnp.full((8, 16, 256), NEG, F32)
    st[:, 1:3] = jnp.zeros((8, 2, 16, 256), F32)
    dqa[...] = jnp.zeros_like(dqa)
    start = start_ref[s]
    end = start + len_ref[s]
    lane = lax.broadcasted_iota(jnp.int32, (1, 256), 1)

    def keys(j, n):
        if isinstance(j, int):
            return kv[j // 4, j % 4:j % 4 + n].reshape(n * 256, 256)[:, 0:128]
        return kv[j // 4, pl.ds(lax.rem(j, 4), n), :, 0:128].reshape(n * 256, 128)

    def values(j):
        return kv[j // 4, j % 4, :, 128:256]

    def rows_of(j, n=1):
        return pl.ds(j * 256 if isinstance(j, int) else pl.multiple_of(j * 256, 256), n * 256)

    def unit(u):
        h, half = u // 2, (u % 2 if isinstance(u, int) else lax.rem(u, 2))
        cols = pl.ds(h * 128 if isinstance(h, int) else pl.multiple_of(h * 128, 128), 128)
        xx = pl.ds(2 * half, 2)
        pos = yl * 2048 + zh * 1024 + (2 * half + lane // 128) * 256 + c * 128 + lax.rem(lane, 128)
        lim = jnp.maximum(start, jnp.minimum(end, pos + 1))
        return q_ref[xx, :, cols].reshape(256, 128), g_ref[xx, :, cols].reshape(256, 128), lim

    def dq_store(u, dq):
        h, half = u // 2, (u % 2 if isinstance(u, int) else lax.rem(u, 2))
        cols = pl.ds(h * 128 if isinstance(h, int) else pl.multiple_of(h * 128, 128), 128)
        dq_ref[pl.ds(2 * half, 2), :, cols] = (dq.T * SCALE).astype(BF16).reshape(2, 128, 128)

    def pass12(u, su, j, masked):
        q, g, lim = unit(u)
        rows = rows_of(j)
        sc = dot_nt(kv[j // 4, (j % 4 if isinstance(j, int) else lax.rem(j, 4)), :, 0:128], q)
        if masked:
            kpos = lax.broadcasted_iota(jnp.int32, (256, 256), 0)
            sc = jnp.where(kpos < lim - j * 256, sc, NEG)
        m = jnp.max(sc, axis=0, keepdims=True)
        e = jnp.exp2((sc - m) * EXPC)
        dp = dot_nt(kv[j // 4, (j % 4 if isinstance(j, int) else lax.rem(j, 4)), :, 128:256], g)
        st[u, 0, pl.ds(j, 1)] = m
        st[u, 1, pl.ds(j, 1)] = jnp.sum(e, axis=0, keepdims=True)
        st[u, 2, pl.ds(j, 1)] = jnp.sum(e * dp, axis=0, keepdims=True)
        s_ref[su, rows, :] = e
        d_ref[su, rows, :] = dp

    def finish(u, su):
        m = jnp.max(st[u, 0], axis=0, keepdims=True)
        f = jnp.exp2((st[u, 0] - m) * EXPC)
        f = f * (1.0 / jnp.sum(st[u, 1] * f, axis=0, keepdims=True))
        fac[su] = f
        dlt[su] = jnp.sum(st[u, 2] * f, axis=0, keepdims=True)

    def pass3(u, su, j, n, dq):
        q, g, _ = unit(u)
        dlv = dlt[su]
        ds_, p_ = [], []
        for i in range(n):
            r = rows_of(j + i)
            p = s_ref[su, r, :] * fac[su, pl.ds(j + i, 1)]
            ds_.append((p * (d_ref[su, r, :] - dlv)).astype(BF16))
            p_.append(p.astype(BF16))
        ds = ds_[0] if n == 1 else jnp.concatenate(ds_, axis=0)
        p = p_[0] if n == 1 else jnp.concatenate(p_, axis=0)
        rows = rows_of(j, n)
        dk_ref[rows, :] += dot_nn(ds, q)
        dv_ref[rows, :] += dot_nn(p, g)
        return dq + dot_nn(kt_ref[:, rows], ds)

    def arrive(e):
        sl = ev[e]

        def one(b, carry):
            j = sl * 4 + b
            kt_ref[:, rows_of(j)] = keys(j, 1).T
            for u in range(4):
                pass12(u, u, j, True)
            return carry
        lax.fori_loop(0, jnp.where(sl < 3, 4, 2 * last), one, 0)

    for k in range(4):
        y_copy(0, ev[1], k).wait_recv()
        go(to_core(1, k, piece(ev[1], k)), 1, 64)
    for cp in own_q:
        cp.wait()
    got(qx_r.at[0], 384)
    q_send(1)
    got(kc_r.at[0], 256)
    arrive(0)

    def n_copy(rr, side, cc_):
        px = lax.rem(x + (1 if side == 0 else 3), 4)
        return rcopy(n_in.at[0, :, pl.ds(pl.multiple_of(rr * 512 + cc_ * 256, 256), 256)], nbuf.at[rr, x, c],
                     n_s, n_r.at[side, rr // 4], dev(x_=px, c_=cc_))

    def n_fwd(i, side, cc_):
        rr = i + 4 * side
        src = nbuf.at[rr, lax.rem(x + (3 if side == 0 else 1), 4), cc_]
        px = lax.rem(x + (1 if side == 0 else 3), 4)
        return rcopy(src, src, nf_s, nf_r, dev(x_=px))

    def nsend(i, carry):
        for cc_ in range(2):
            n_copy(i, 0, cc_).start()
            n_copy(lax.rem(i + 4, 8), 1, cc_).start()
        mine_ = pl.ds(pl.multiple_of(i * 512 + c * 256, 256), 256)
        theirs = pl.ds(pl.multiple_of(i * 512 + (1 - c) * 256, 256), 256)
        rcopy(n_in.at[0, :, theirs], nbuf.at[i, x, c], nc_s, nc_r, core_dev).start()
        pltpu.make_async_copy(n_in.at[0, :, mine_], nbuf.at[i, x, c], nl_sem).start()
        return carry

    lax.fori_loop(0, 8, nsend, 0)
    got(kc_r.at[1], 256)
    arrive(1)

    def block(e, k):
        xb = lax.rem(x - k + 4, 4)

        @pl.when((ev[e] < 3) | ((last == 1) & (xb < 2)))
        def _():
            j = ev[e] * 4 + xb
            kt_ref[:, rows_of(j)] = keys(j, 1).T
            for u in range(4):
                pass12(u, u, j, True)

    sent[1] += 12 * 64

    def far(k, carry):
        @pl.when(k < 4)
        def _():
            z_copy(k).wait_recv()
            y_copy(1, ev[2], k).start()
            cp = to_core(2, k, piece(ev[2], k))
            cp.start()
            cp.wait_recv()
            block(2, k)

        @pl.when(k > 0)
        def _():
            y_copy(1, ev[3], k - 1).wait_recv()
            cp = to_core(3, k - 1, piece(ev[3], k - 1))
            cp.start()
            cp.wait_recv()
            block(3, k - 1)
        return carry

    lax.fori_loop(0, 5, far, 0)
    for u in range(4):
        finish(u, u)
    got(qx_r.at[1], 384)

    def mid(u, carry):
        dq = jnp.zeros((128, 256), F32)
        for j in range(12):
            dq = pass3(u, u, j, 1, dq)
            pass12(u + 4, u, j, j >= 8)
        dqa[4] = dq

        @pl.when(last == 1)
        def _():
            d2 = dqa[4]
            for j in range(12, 14):
                d2 = pass3(u, u, j, 1, d2)
                pass12(u + 4, u, j, True)
            dqa[4] = d2
        dq_store(u, dqa[4])
        finish(u + 4, u)
        return carry

    lax.fori_loop(0, 3, mid, 0)

    for side in range(2):
        got(n_r.at[side, side], 512)

    def fwd(i, carry):
        for side in range(2):
            for cc_ in range(2):
                n_fwd(i, side, cc_).start()
        return carry

    lax.fori_loop(0, 4, fwd, 0)
    lax.fori_loop(3, 4, mid, 0)

    def dq_copy(h, i):
        px = xs[i]
        return rcopy(dq_ref.at[px, :, blk(h, 128)], dq_out.at[0, :, blk(x * 4 + h, 128)],
                     dq_s, dq_r, dev(x_=px))

    def dq_local(h):
        return pltpu.make_async_copy(dq_ref.at[x, :, blk(h, 128)], dq_out.at[0, :, blk(x * 4 + h, 128)],
                                     dql_sem)

    def dq_send(h):
        for i in range(3):
            dq_copy(h, i).start()
        dq_local(h).start()

    dq_send(0)
    dq_send(1)

    def back(sl, trips):
        def two(b, carry):
            for u in range(4):
                dqa[u] = pass3(u + 4, u, sl * 4 + 2 * b, 2, dqa[u])
            return carry
        lax.fori_loop(0, trips, two, 0)

    def grads(yl_, zh_, x_, c_):
        r = pl.ds(pl.multiple_of((slot(yl_, zh_, zh) * 4 + x_) * 256 + c_ * 128, 128), 128)
        return jnp.concatenate([dk_ref[r, :] * SCALE, dv_ref[r, :]], axis=1)

    quad = [(1 - yl, 1 - zh), (yl, 1 - zh), (1 - yl, zh), (yl, zh)]
    cx = []

    def core_send(k):
        for x_ in range(4):
            csend[k, x_] = grads(quad[k][0], quad[k][1], x_, 1 - c).astype(BF16)
        cx.append(go(rcopy(csend.at[k], crx.at[k], s3, c_r.at[k], core_dev), 3, 256))

    def pair(k, x_, ch):
        r = pl.ds(pl.multiple_of((slot(quad[k][0], quad[k][1], zh) * 4 + x_) * 256 + c * 128, 128), 128)
        own = dk_ref[r, :] * SCALE if ch == 0 else dv_ref[r, :]
        return own + crx[k, x_, :, ch * 128:(ch + 1) * 128].astype(F32)

    yx = {}

    def y_stage(k, sl):
        cx[k].wait_recv()
        for ch in (1, 0):
            for x_ in range(4):
                ysend[sl, ch, x_] = pair(k, x_, ch).astype(BF16)
            yx[sl, ch] = go(rcopy(ysend.at[sl, ch], yrx.at[sl, ch], s3, y_r.at[sl, ch], y_dev), 3, 128)

    back(1, 2)
    back(2, 2 * zh)
    core_send(0)
    core_send(1)
    back(0, 2)
    y_stage(0, 0)
    cx[1].wait_recv()
    for ch in range(2):
        for x_ in range(4):
            acc1[ch, x_] = pair(1, x_, ch)
    back(2, 2 * (1 - zh))
    back(3, last)
    core_send(2)
    core_send(3)
    zx = {}
    for ch in (1, 0):
        yx[0, ch].wait_recv()
        zsend[ch] = (acc1[ch] + yrx[0, ch].astype(F32)).astype(BF16)
        zx[ch] = go(rcopy(zsend.at[ch], zrx.at[ch], s3, z_r.at[ch], z_dev), 3, 128)
    y_stage(2, 1)
    for u in range(4):
        dq_store(u + 4, dqa[u])
    dq_send(2)
    dq_send(3)
    cx[3].wait_recv()
    for ch in range(2):
        for x_ in range(4):
            acc0[ch, x_] = pair(3, x_, ch)
    for ch in (1, 0):
        yx[1, ch].wait_recv()
        acc0[ch] = acc0[ch] + yrx[1, ch].astype(F32)

    for side in range(2):
        got(n_r.at[side, 1 - side], 512)
    got(nf_r, 1024)
    got(nc_r, 512)
    pltpu.make_async_copy(kib(512), d_ref.at[0, pl.ds(0, 512)], nl_sem).wait()

    def turn(i, carry):
        nt[i] = nbuf[i].reshape(1024, 256).T
        return carry

    lax.fori_loop(0, 8, turn, 0)

    border = [1 - zh, zh]
    ko_own = []

    def final_half(ch):
        zx[ch].wait_recv()
        kga[ch, :, pl.ds(c, 1)] = (acc0[ch] + zrx[ch].astype(F32)).astype(BF16).reshape(4, 1, 128, 128)
        own = kga.at[ch, :, c]
        k2 = go(rcopy(own, own, s3, kc2_r.at[ch], core_dev), 3, 128)
        out = kg_out if ch == 0 else vg_out
        for i, px in enumerate(xs):
            go(rcopy(kga.at[ch, px, c], out.at[0, :, blk(x, 128)], s3, ko_r, dev(x_=px)), 3, 32)
        cp = pltpu.make_async_copy(kga.at[ch, x, c], out.at[0, :, blk(x, 128)], l_sem.at[4 + ch])
        cp.start()
        ko_own.append(cp)
        k2.wait_recv()
        kgall = kga[ch].reshape(1024, 128)
        for bi, b in enumerate(border):
            for d in range(3):
                py = lax.rem(y + d + 1, 4)
                w1s[ch, bi, d] = dot_nn(nt[py * 2 + b], kgall).astype(BF16)
                go(rcopy(w1s.at[ch, bi, d], w1r.at[ch, bi, d], s3, w1_r.at[ch, bi], ydev[d]), 3, 64)
        for bi, b in enumerate(border):
            w1o[ch, bi] = dot_nn(nt[y * 2 + b], kgall)

    def z_half(ch):
        for bi, b in enumerate(border):
            got(w1_r.at[ch, bi], 192)
            t = w1o[ch, bi]
            for d in range(3):
                t = t + w1r[ch, bi, d].astype(F32)
            w2s[ch, bi] = t.astype(BF16).reshape(4, 4, 16, 128)
            for i in range(bi, 4):
                pz = lax.rem(zl + i, 4)
                sl = i if bi == 0 else 3 + i
                go(rcopy(w2s.at[ch, bi, :, pz], w2r.at[ch, sl], s3, w2_r.at[ch], dev(zh_=b, zl_=pz)), 3, 16)

    final_half(1)
    final_half(0)
    z_half(1)
    z_half(0)
    for ch in (1, 0):
        got(w2_r.at[ch], 112)
        t = w2s[ch, 1, :, pl.ds(zl, 1)].reshape(4, 16, 128).astype(F32)
        for i in range(7):
            t = t + w2r[ch, i].astype(F32)
        w3s[:, :, ch * 128:(ch + 1) * 128] = t
    self_core = x // 2

    def w4_copy(xl, cc_):
        return rcopy(w3s.at[xl * 2 + cc_], w4r.at[x], w4_s.at[xl * 2 + cc_], w4_r.at[x],
                     dev(x_=2 * c + xl, c_=cc_))

    for xl in range(2):
        for cc_ in range(2):
            is_me = (2 * c + xl == x) & (c == cc_)

            @pl.when(is_me)
            def _():
                w4r[pl.ds(x, 1)] = w3s[xl * 2 + cc_].reshape(1, 16, 256)

            @pl.when(jnp.logical_not(is_me))
            def _():
                w4_copy(xl, cc_).start()
    for xx in range(4):
        @pl.when(jnp.logical_not((x == xx) & (c == self_core)))
        def _():
            rcopy(w3s.at[0], w4r.at[xx], w4_s.at[0], w4_r.at[xx], core_dev).wait_recv()
    for xx in range(4):
        w_out[:, xx * 128:(xx + 1) * 128] = w4r[xx, :, 0:128]
        w_out[:, 512 + xx * 128:512 + (xx + 1) * 128] = w4r[xx, :, 128:256]
    for xl in range(2):
        for cc_ in range(2):
            @pl.when(jnp.logical_not((2 * c + xl == x) & (c == cc_)))
            def _():
                w4_copy(xl, cc_).wait_send()
    drain(dq_s, 384)
    got(dq_r, 384)
    pltpu.make_async_copy(kib(128), d_ref.at[0, pl.ds(0, 128)], dql_sem).wait()
    got(ko_r, 192)
    for cp in ko_own:
        cp.wait()
    drain(n_s, 2048)
    drain(nf_s, 1024)
    drain(nc_s, 512)
    drain(s1, sent[1])
    drain(s3, sent[3])


def place(*refs):
    ins, outs, sem = refs[:4], refs[4:8], refs[8]
    cps = [pltpu.make_async_copy(a, b, sem.at[i]) for i, (a, b) in enumerate(zip(ins, outs))]
    for cp in cps:
        cp.start()
    for cp in cps:
        cp.wait()


def local(query, keys, values, out_grad, normed_input, q_start, q_len):
    dma = pltpu.SemaphoreType.DMA
    V = pltpu.VMEM
    hbm = pl.BlockSpec(memory_space=pl.ANY)
    smem = pl.BlockSpec(memory_space=pltpu.SMEM)
    outs = pl.pallas_call(
        body,
        name="attention_grads",
        out_shape=(jax.ShapeDtypeStruct((1, 128, 2048), BF16), jax.ShapeDtypeStruct((1, 128, 512), BF16),
                   jax.ShapeDtypeStruct((1, 128, 512), BF16), jax.ShapeDtypeStruct((16, 1024), F32)),
        in_specs=[hbm] * 5 + [smem] * 2,
        out_specs=[hbm] * 3 + [pl.BlockSpec(memory_space=pltpu.VMEM)],
        scratch_shapes=[
            V((4, 128, 512), BF16), V((4, 128, 512), BF16), V((4, 4, 256, 256), BF16),
            V((8, 4, 2, 128, 256), BF16),
            V((4, 3584, 256), F32), V((4, 3584, 256), F32), V((4096, 128), F32), V((4096, 128), F32),
            V((4, 128, 512), BF16),
            V((4, 4, 128, 256), BF16), V((4, 4, 128, 256), BF16),
            V((2, 2, 4, 128, 128), BF16), V((2, 2, 4, 128, 128), BF16),
            V((2, 4, 128, 128), F32), V((2, 4, 128, 128), F32), V((2, 4, 128, 128), BF16), V((2, 4, 128, 128), BF16),
            V((2, 4, 2, 128, 128), BF16),
            V((2, 2, 3, 256, 128), BF16), V((2, 2, 3, 256, 128), BF16), V((2, 2, 256, 128), F32), V((8, 256, 1024), BF16),
            V((128, 4096), BF16), V((8, 3, 16, 256), F32), V((4, 16, 256), F32), V((4, 1, 256), F32),
            V((5, 128, 256), F32), V((2, 2, 4, 4, 16, 128), BF16),
            V((2, 7, 4, 16, 128), BF16), V((4, 16, 256), F32), V((4, 16, 256), F32),
            dma, dma, dma((3,)), dma((2,)), dma((4,)), dma((8,)), dma((12,)), dma, dma((2, 2)), dma, dma, dma, dma,
            dma, dma, dma((4,)), dma((2, 2)), dma((2,)), dma((2,)), dma, dma((2, 2)), dma((2,)), dma((4,)), dma((4,)),
            dma((6,)), dma, dma,
        ],
        compiler_params=pltpu.CompilerParams(collective_id=0, has_side_effects=True, vmem_limit_bytes=60 << 20),
    )(query, out_grad, keys, values, normed_input, q_start, q_len)
    return pl.pallas_call(
        place,
        name="place_outputs",
        out_shape=[jax.ShapeDtypeStruct(o.shape, o.dtype) for o in outs],
        in_specs=[hbm] * 4,
        out_specs=[hbm] * 4,
        scratch_shapes=[dma((4,))],
    )(*outs)


def solution(mesh):
    tok = P("dp", "seq", None)
    return jax.shard_map(
        local, mesh=mesh,
        in_specs=(tok, tok, tok, tok, tok, P("dp"), P("dp")),
        out_specs=(tok, tok, tok, P(("seq", "dp"), None)),
        check_vma=False)
```

```python
import math
import jax
import jax.numpy as jnp
from jax import lax
from jax.experimental import pallas as pl
from jax.experimental.pallas import tpu as pltpu
from jax.sharding import PartitionSpec as P

HEAD_DIM = 128
SCALE = 1.0 / math.sqrt(HEAD_DIM)
EXPC = SCALE * math.log2(math.e)
NEG = -1e30
F32 = jnp.float32
BF16 = jnp.bfloat16


def dot_nt(a, b):
    return lax.dot_general(a, b, (((1,), (1,)), ((), ())), preferred_element_type=F32)


def dot_nn(a, b):
    return lax.dot_general(a, b, (((1,), (0,)), ((), ())), preferred_element_type=F32)


def dot_tn(a, b):
    return lax.dot_general(a, b, (((0,), (0,)), ((), ())), preferred_element_type=F32)


def coords():
    seq = lax.axis_index("seq")
    c = lax.rem(seq, 2)
    x = lax.rem(seq // 2, 4)
    zh = lax.rem(seq // 8, 2)
    yl = lax.rem(seq // 16, 2)
    s = seq // 32
    zl = lax.axis_index("dp")
    return s, yl, zh, x, c, zl


def seq_of(s, yl, zh, x, c):
    return s * 32 + yl * 16 + zh * 8 + x * 2 + c


def rcopy(src, dst, ssem, rsem, dev):
    return pltpu.make_async_remote_copy(
        src_ref=src, dst_ref=dst, send_sem=ssem, recv_sem=rsem,
        device_id={"seq": dev[0], "dp": dev[1]}, device_id_type=pl.DeviceIdType.MESH)


def greet(peers):
    barrier = pltpu.get_barrier_semaphore()
    for seq, dp in peers:
        pl.semaphore_signal(barrier, inc=1, device_id={"seq": seq, "dp": dp},
                            device_id_type=pl.DeviceIdType.MESH)
    pl.semaphore_wait(barrier, len(peers))


def blk(i, w):
    return pl.ds(pl.multiple_of(i * w, w), w)


def body(q_in, g_in, k_in, v_in, n_in, start_ref, len_ref,
         dq_out, kg_out, vg_out, w_out,
         q_ref, g_ref, kv, nbuf, s_ref, d_ref, dk_ref, dv_ref, dq_ref,
         csend, crx, ysend, yrx, acc0, acc1, zsend, zrx, kga,
         w1s, w1r, nt, kt_ref, st, fac, dlt, dqa, w2s, w2r, w3s, w4r,
         s1, s3, kx_r, qx_r, kz_r, ky_r, kc_r, n_s, n_r, nf_s, nf_r, nc_s, nc_r, dq_s, dq_r,
         c_r, y_r, z_s, z_r, kc2_r, ko_r, w1_r, w2_r, w4_s, w4_r, l_sem, nl_sem, dql_sem):
    s, yl, zh, x, c, zl = coords()
    y = s * 2 + yl
    z = zh * 4 + zl
    me8 = x * 2 + c

    def dev(s_=None, yl_=None, zh_=None, x_=None, c_=None, zl_=None):
        return (seq_of(s if s_ is None else s_, yl if yl_ is None else yl_, zh if zh_ is None else zh_,
                       x if x_ is None else x_, c if c_ is None else c_), zl if zl_ is None else zl_)

    row8 = [lax.rem(me8 + d, 8) for d in range(1, 8)]
    xs = [lax.rem(x + d, 4) for d in range(1, 4)]
    ys = [lax.rem(y + d, 4) for d in range(1, 4)]
    zs = [lax.rem(z + d, 8) for d in range(1, 8)]
    ydev = [dev(s_=p // 2, yl_=lax.rem(p, 2)) for p in ys]
    zdev = [dev(zh_=p // 4, zl_=lax.rem(p, 4)) for p in zs]
    core_dev = dev(c_=1 - c)
    y_dev = dev(yl_=1 - yl)
    z_dev = dev(zh_=1 - zh)
    greet([dev(x_=p // 2, c_=lax.rem(p, 2)) for p in row8] + ydev + zdev)

    sent = {}

    def go(cp, key, kb):
        cp.start()
        sent[key] = sent.get(key, 0) + kb
        return cp

    def kib(n):
        return s_ref.at[0, pl.ds(0, n)]

    def drain(sem, n):
        rcopy(kib(n), kib(n), sem, sem, (seq_of(s, yl, zh, x, 1 - c), zl)).wait_send()

    def got(sem, n):
        rcopy(kib(n), kib(n), sem, sem, (seq_of(s, yl, zh, x, 1 - c), zl)).wait_recv()

    crow = blk(c, 128)
    last = yl * zh

    def slot(yl_, zh_, plane):
        return jnp.where(yl_ == 0, jnp.where(zh_ == plane, 0, 1), 2 + zh_)

    mine = slot(yl, zh, zh)
    for i, px in enumerate(xs):
        go(rcopy(k_in.at[0, :, blk(px, 128)], kv.at[mine, x, crow, pl.ds(0, 128)], s1, kx_r.at[i], dev(x_=px)), 1, 32)
        go(rcopy(v_in.at[0, :, blk(px, 128)], kv.at[mine, x, crow, pl.ds(128, 128)], s1, kx_r.at[i], dev(x_=px)), 1, 32)
    own_kv = [pltpu.make_async_copy(k_in.at[0, :, blk(x, 128)], kv.at[mine, x, crow, pl.ds(0, 128)], l_sem.at[0]),
              pltpu.make_async_copy(v_in.at[0, :, blk(x, 128)], kv.at[mine, x, crow, pl.ds(128, 128)], l_sem.at[1])]
    own_q = [pltpu.make_async_copy(q_in.at[0, :, blk(x, 512)], q_ref.at[x], l_sem.at[2]),
             pltpu.make_async_copy(g_in.at[0, :, blk(x, 512)], g_ref.at[x], l_sem.at[3])]
    for cp in own_kv + own_q:
        cp.start()

    def q_send(ph):
        for i, px in enumerate(xs):
            src = pl.ds(pl.multiple_of(px * 512 + ph * 256, 256), 256)
            dst = pl.ds(ph * 256, 256)
            go(rcopy(q_in.at[0, :, src], q_ref.at[x, :, dst], s1, qx_r.at[ph], dev(x_=px)), 1, 64)
            go(rcopy(g_in.at[0, :, src], g_ref.at[x, :, dst], s1, qx_r.at[ph], dev(x_=px)), 1, 64)

    q_send(0)

    def piece(sl, k):
        return kv.at[sl, lax.rem(x - k + 4, 4), crow]

    def to_core(e, k, p):
        return rcopy(p, p, s1, kc_r.at[e], core_dev)

    def z_copy(k):
        return rcopy(piece(mine, k), piece(slot(yl, zh, 1 - zh), k), s1, kz_r.at[k], z_dev)

    def y_copy(e, sl, k):
        return rcopy(piece(sl, k), piece(sl, k), s1, ky_r.at[4 * e + k], y_dev)

    for k in range(4):
        if k == 0:
            for cp in own_kv:
                cp.wait()
        else:
            got(kx_r.at[k - 1], 64)
        go(z_copy(k), 1, 64)
        go(y_copy(0, mine, k), 1, 64)
        go(to_core(0, k, piece(mine, k)), 1, 64)
    ev = [mine, slot(1 - yl, zh, zh), slot(yl, 1 - zh, zh), slot(1 - yl, 1 - zh, zh)]

    dk_ref[...] = jnp.zeros_like(dk_ref)
    dv_ref[...] = jnp.zeros_like(dv_ref)
    st[:, 0] = jnp.full((8, 16, 256), NEG, F32)
    st[:, 1:3] = jnp.zeros((8, 2, 16, 256), F32)
    dqa[...] = jnp.zeros_like(dqa)
    start = start_ref[s]
    end = start + len_ref[s]
    lane = lax.broadcasted_iota(jnp.int32, (1, 256), 1)

    def keys(j, n):
        if isinstance(j, int):
            return kv[j // 4, j % 4:j % 4 + n].reshape(n * 256, 256)[:, 0:128]
        return kv[j // 4, pl.ds(lax.rem(j, 4), n), :, 0:128].reshape(n * 256, 128)

    def values(j):
        return kv[j // 4, j % 4, :, 128:256]

    def rows_of(j, n=1):
        return pl.ds(j * 256 if isinstance(j, int) else pl.multiple_of(j * 256, 256), n * 256)

    def unit(u):
        h, half = u // 2, (u % 2 if isinstance(u, int) else lax.rem(u, 2))
        cols = pl.ds(h * 128 if isinstance(h, int) else pl.multiple_of(h * 128, 128), 128)
        xx = pl.ds(2 * half, 2)
        pos = yl * 2048 + zh * 1024 + (2 * half + lane // 128) * 256 + c * 128 + lax.rem(lane, 128)
        lim = jnp.maximum(start, jnp.minimum(end, pos + 1))
        return q_ref[xx, :, cols].reshape(256, 128), g_ref[xx, :, cols].reshape(256, 128), lim

    def dq_store(u, dq):
        h, half = u // 2, (u % 2 if isinstance(u, int) else lax.rem(u, 2))
        cols = pl.ds(h * 128 if isinstance(h, int) else pl.multiple_of(h * 128, 128), 128)
        dq_ref[pl.ds(2 * half, 2), :, cols] = (dq.T * SCALE).astype(BF16).reshape(2, 128, 128)

    def pass12(u, su, j, masked):
        q, g, lim = unit(u)
        rows = rows_of(j)
        sc = dot_nt(kv[j // 4, (j % 4 if isinstance(j, int) else lax.rem(j, 4)), :, 0:128], q)
        if masked:
            kpos = lax.broadcasted_iota(jnp.int32, (256, 256), 0)
            sc = jnp.where(kpos < lim - j * 256, sc, NEG)
        m = jnp.max(sc, axis=0, keepdims=True)
        e = jnp.exp2((sc - m) * EXPC)
        dp = dot_nt(kv[j // 4, (j % 4 if isinstance(j, int) else lax.rem(j, 4)), :, 128:256], g)
        st[u, 0, pl.ds(j, 1)] = m
        st[u, 1, pl.ds(j, 1)] = jnp.sum(e, axis=0, keepdims=True)
        st[u, 2, pl.ds(j, 1)] = jnp.sum(e * dp, axis=0, keepdims=True)
        s_ref[su, rows, :] = e
        d_ref[su, rows, :] = dp

    def finish(u, su):
        m = jnp.max(st[u, 0], axis=0, keepdims=True)
        f = jnp.exp2((st[u, 0] - m) * EXPC)
        f = f * (1.0 / jnp.sum(st[u, 1] * f, axis=0, keepdims=True))
        fac[su] = f
        dlt[su] = jnp.sum(st[u, 2] * f, axis=0, keepdims=True)

    def pass3(u, su, j, n, dq):
        q, g, _ = unit(u)
        dlv = dlt[su]
        ds_, p_ = [], []
        for i in range(n):
            r = rows_of(j + i)
            p = s_ref[su, r, :] * fac[su, pl.ds(j + i, 1)]
            ds_.append((p * (d_ref[su, r, :] - dlv)).astype(BF16))
            p_.append(p.astype(BF16))
        ds = ds_[0] if n == 1 else jnp.concatenate(ds_, axis=0)
        p = p_[0] if n == 1 else jnp.concatenate(p_, axis=0)
        rows = rows_of(j, n)
        dk_ref[rows, :] += dot_nn(ds, q)
        dv_ref[rows, :] += dot_nn(p, g)
        return dq + dot_nn(kt_ref[:, rows], ds)

    def arrive(e):
        sl = ev[e]

        def one(b, carry):
            j = sl * 4 + b
            kt_ref[:, rows_of(j)] = keys(j, 1).T
            for u in range(4):
                pass12(u, u, j, True)
            return carry
        lax.fori_loop(0, jnp.where(sl < 3, 4, 2 * last), one, 0)

    for k in range(4):
        y_copy(0, ev[1], k).wait_recv()
        go(to_core(1, k, piece(ev[1], k)), 1, 64)
    for cp in own_q:
        cp.wait()
    got(qx_r.at[0], 384)
    q_send(1)
    got(kc_r.at[0], 256)
    arrive(0)

    def n_copy(rr, side, cc_):
        px = lax.rem(x + (1 if side == 0 else 3), 4)
        return rcopy(n_in.at[0, :, pl.ds(pl.multiple_of(rr * 512 + cc_ * 256, 256), 256)], nbuf.at[rr, x, c],
                     n_s, n_r.at[side, rr // 4], dev(x_=px, c_=cc_))

    def n_fwd(i, side, cc_):
        rr = i + 4 * side
        src = nbuf.at[rr, lax.rem(x + (3 if side == 0 else 1), 4), cc_]
        px = lax.rem(x + (1 if side == 0 else 3), 4)
        return rcopy(src, src, nf_s, nf_r, dev(x_=px))

    def nsend(i, carry):
        for cc_ in range(2):
            n_copy(i, 0, cc_).start()
            n_copy(lax.rem(i + 4, 8), 1, cc_).start()
        mine_ = pl.ds(pl.multiple_of(i * 512 + c * 256, 256), 256)
        theirs = pl.ds(pl.multiple_of(i * 512 + (1 - c) * 256, 256), 256)
        rcopy(n_in.at[0, :, theirs], nbuf.at[i, x, c], nc_s, nc_r, core_dev).start()
        pltpu.make_async_copy(n_in.at[0, :, mine_], nbuf.at[i, x, c], nl_sem).start()
        return carry

    def far_piece(k):
        z_copy(k).wait_recv()
        go(y_copy(1, ev[2], k), 1, 64)
        go(to_core(2, k, piece(ev[2], k)), 1, 64)

    far_piece(0)
    far_piece(1)
    lax.fori_loop(0, 8, nsend, 0)
    got(kc_r.at[1], 256)
    arrive(1)
    far_piece(2)
    far_piece(3)
    for k in range(4):
        y_copy(1, ev[3], k).wait_recv()
        go(to_core(3, k, piece(ev[3], k)), 1, 64)
    got(kc_r.at[2], 256)
    arrive(2)
    got(kc_r.at[3], 256)
    arrive(3)
    for u in range(4):
        finish(u, u)
    got(qx_r.at[1], 384)

    def mid(u, carry):
        dq = jnp.zeros((128, 256), F32)
        for j in range(12):
            dq = pass3(u, u, j, 1, dq)
            pass12(u + 4, u, j, j >= 8)
        dqa[4] = dq

        @pl.when(last == 1)
        def _():
            d2 = dqa[4]
            for j in range(12, 14):
                d2 = pass3(u, u, j, 1, d2)
                pass12(u + 4, u, j, True)
            dqa[4] = d2
        dq_store(u, dqa[4])
        finish(u + 4, u)
        return carry

    lax.fori_loop(0, 3, mid, 0)

    for side in range(2):
        got(n_r.at[side, side], 512)

    def fwd(i, carry):
        for side in range(2):
            for cc_ in range(2):
                n_fwd(i, side, cc_).start()
        return carry

    lax.fori_loop(0, 4, fwd, 0)
    lax.fori_loop(3, 4, mid, 0)

    def dq_copy(h, i):
        px = xs[i]
        return rcopy(dq_ref.at[px, :, blk(h, 128)], dq_out.at[0, :, blk(x * 4 + h, 128)],
                     dq_s, dq_r, dev(x_=px))

    def dq_local(h):
        return pltpu.make_async_copy(dq_ref.at[x, :, blk(h, 128)], dq_out.at[0, :, blk(x * 4 + h, 128)],
                                     dql_sem)

    def dq_send(h):
        for i in range(3):
            dq_copy(h, i).start()
        dq_local(h).start()

    dq_send(0)
    dq_send(1)

    def back(sl, trips):
        def two(b, carry):
            j = sl * 4 + 2 * b
            rows = rows_of(j, 2)
            dss, ps = [], []
            for u in range(4):
                dlv = dlt[u]
                d_, p_ = [], []
                for i in range(2):
                    r = rows_of(j + i)
                    p = s_ref[u, r, :] * fac[u, pl.ds(j + i, 1)]
                    d_.append((p * (d_ref[u, r, :] - dlv)).astype(BF16))
                    p_.append(p.astype(BF16))
                ds = jnp.concatenate(d_, axis=0)
                dss.append(ds)
                ps.append(jnp.concatenate(p_, axis=0))
                dqa[u] += dot_nn(kt_ref[:, rows], ds)
            q4 = jnp.concatenate([unit(u + 4)[0] for u in range(4)], axis=0)
            g4 = jnp.concatenate([unit(u + 4)[1] for u in range(4)], axis=0)
            dk_ref[rows, :] += dot_nn(jnp.concatenate(dss, axis=1), q4)
            dv_ref[rows, :] += dot_nn(jnp.concatenate(ps, axis=1), g4)
            return carry
        lax.fori_loop(0, trips, two, 0)

    def grads(yl_, zh_, x_, c_):
        r = pl.ds(pl.multiple_of((slot(yl_, zh_, zh) * 4 + x_) * 256 + c_ * 128, 128), 128)
        return jnp.concatenate([dk_ref[r, :] * SCALE, dv_ref[r, :]], axis=1)

    quad = [(1 - yl, 1 - zh), (yl, 1 - zh), (1 - yl, zh), (yl, zh)]
    cx = []

    def core_send(k):
        for x_ in range(4):
            csend[k, x_] = grads(quad[k][0], quad[k][1], x_, 1 - c).astype(BF16)
        cx.append(go(rcopy(csend.at[k], crx.at[k], s3, c_r.at[k], core_dev), 3, 256))

    def pair(k, x_, ch):
        r = pl.ds(pl.multiple_of((slot(quad[k][0], quad[k][1], zh) * 4 + x_) * 256 + c * 128, 128), 128)
        own = dk_ref[r, :] * SCALE if ch == 0 else dv_ref[r, :]
        return own + crx[k, x_, :, ch * 128:(ch + 1) * 128].astype(F32)

    yx = {}

    def y_stage(k, sl):
        cx[k].wait_recv()
        for ch in (1, 0):
            for x_ in range(4):
                ysend[sl, ch, x_] = pair(k, x_, ch).astype(BF16)
            yx[sl, ch] = go(rcopy(ysend.at[sl, ch], yrx.at[sl, ch], s3, y_r.at[sl, ch], y_dev), 3, 128)

    back(1, 2)
    back(2, 2 * zh)
    core_send(0)
    core_send(1)
    back(0, 2)
    y_stage(0, 0)
    cx[1].wait_recv()
    for ch in range(2):
        for x_ in range(4):
            acc1[ch, x_] = pair(1, x_, ch)
    back(2, 2 * (1 - zh))
    back(3, last)
    core_send(2)
    core_send(3)
    zx = {}

    def z_stage(ch):
        yx[0, ch].wait_recv()
        zsend[ch] = (acc1[ch] + yrx[0, ch].astype(F32)).astype(BF16)
        zx[ch] = rcopy(zsend.at[ch], zrx.at[ch], z_s.at[ch], z_r.at[ch], z_dev)
        zx[ch].start()

    z_stage(1)
    y_stage(2, 1)
    for u in range(4):
        dq_store(u + 4, dqa[u])
    dq_send(2)
    dq_send(3)
    cx[3].wait_recv()
    for ch in range(2):
        for x_ in range(4):
            acc0[ch, x_] = pair(3, x_, ch)
    for ch in (1, 0):
        yx[1, ch].wait_recv()
        acc0[ch] = acc0[ch] + yrx[1, ch].astype(F32)

    zx[1].wait_send()
    z_stage(0)
    for side in range(2):
        got(n_r.at[side, 1 - side], 512)
    got(nf_r, 1024)
    got(nc_r, 512)
    pltpu.make_async_copy(kib(512), d_ref.at[0, pl.ds(0, 512)], nl_sem).wait()

    def turn(i, carry):
        nt[i] = nbuf[i].reshape(1024, 256).T
        return carry

    lax.fori_loop(0, 8, turn, 0)

    border = [1 - zh, zh]
    ko_own = []

    def final_half(ch):
        zx[ch].wait_recv()
        kga[ch, :, pl.ds(c, 1)] = (acc0[ch] + zrx[ch].astype(F32)).astype(BF16).reshape(4, 1, 128, 128)
        own = kga.at[ch, :, c]
        k2 = go(rcopy(own, own, s3, kc2_r.at[ch], core_dev), 3, 128)
        out = kg_out if ch == 0 else vg_out
        for i, px in enumerate(xs):
            go(rcopy(kga.at[ch, px, c], out.at[0, :, blk(x, 128)], s3, ko_r, dev(x_=px)), 3, 32)
        cp = pltpu.make_async_copy(kga.at[ch, x, c], out.at[0, :, blk(x, 128)], l_sem.at[4 + ch])
        cp.start()
        ko_own.append(cp)
        k2.wait_recv()
        kgall = kga[ch].reshape(1024, 128)
        w1s[ch] = dot_nn(nt[...].reshape(2048, 1024), kgall).astype(BF16).reshape(4, 2, 256, 128)
        for d in range(3):
            py = lax.rem(y + d + 1, 4)
            go(rcopy(w1s.at[ch, py], w1r.at[ch, d], s3, w1_r.at[ch], ydev[d]), 3, 128)

    def z_half(ch):
        got(w1_r.at[ch], 384)
        for bi, b in enumerate(border):
            t = w1s[ch, y, b].astype(F32)
            for d in range(3):
                t = t + w1r[ch, d, b].astype(F32)
            w2s[ch, bi] = t.astype(BF16).reshape(4, 4, 16, 128)
            for i in range(bi, 4):
                pz = lax.rem(zl + i, 4)
                sl = i if bi == 0 else 3 + i
                go(rcopy(w2s.at[ch, bi, :, pz], w2r.at[ch, sl], s3, w2_r.at[ch], dev(zh_=b, zl_=pz)), 3, 16)

    final_half(1)
    final_half(0)
    z_half(1)
    z_half(0)
    for ch in (1, 0):
        got(w2_r.at[ch], 112)
        t = w2s[ch, 1, :, pl.ds(zl, 1)].reshape(4, 16, 128).astype(F32)
        for i in range(7):
            t = t + w2r[ch, i].astype(F32)
        w3s[:, :, ch * 128:(ch + 1) * 128] = t
    self_core = x // 2

    def w4_copy(xl, cc_):
        return rcopy(w3s.at[xl * 2 + cc_], w4r.at[x], w4_s.at[xl * 2 + cc_], w4_r.at[x],
                     dev(x_=2 * c + xl, c_=cc_))

    for xl in range(2):
        for cc_ in range(2):
            is_me = (2 * c + xl == x) & (c == cc_)

            @pl.when(is_me)
            def _():
                w4r[pl.ds(x, 1)] = w3s[xl * 2 + cc_].reshape(1, 16, 256)

            @pl.when(jnp.logical_not(is_me))
            def _():
                w4_copy(xl, cc_).start()
    for xx in range(4):
        @pl.when(jnp.logical_not((x == xx) & (c == self_core)))
        def _():
            rcopy(w3s.at[0], w4r.at[xx], w4_s.at[0], w4_r.at[xx], core_dev).wait_recv()
    for xx in range(4):
        w_out[:, xx * 128:(xx + 1) * 128] = w4r[xx, :, 0:128]
        w_out[:, 512 + xx * 128:512 + (xx + 1) * 128] = w4r[xx, :, 128:256]
    for xl in range(2):
        for cc_ in range(2):
            @pl.when(jnp.logical_not((2 * c + xl == x) & (c == cc_)))
            def _():
                w4_copy(xl, cc_).wait_send()
    drain(dq_s, 384)
    got(dq_r, 384)
    pltpu.make_async_copy(kib(128), d_ref.at[0, pl.ds(0, 128)], dql_sem).wait()
    got(ko_r, 192)
    for cp in ko_own:
        cp.wait()
    zx[0].wait_send()
    drain(n_s, 2048)
    drain(nf_s, 1024)
    drain(nc_s, 512)
    drain(s1, sent[1])
    drain(s3, sent[3])


def place(*refs):
    ins, outs, sem = refs[:4], refs[4:8], refs[8]
    cps = [pltpu.make_async_copy(a, b, sem.at[i]) for i, (a, b) in enumerate(zip(ins, outs))]
    for cp in cps:
        cp.start()
    for cp in cps:
        cp.wait()


def local(query, keys, values, out_grad, normed_input, q_start, q_len):
    dma = pltpu.SemaphoreType.DMA
    V = pltpu.VMEM
    hbm = pl.BlockSpec(memory_space=pl.ANY)
    smem = pl.BlockSpec(memory_space=pltpu.SMEM)
    outs = pl.pallas_call(
        body,
        name="attention_grads",
        out_shape=(jax.ShapeDtypeStruct((1, 128, 2048), BF16), jax.ShapeDtypeStruct((1, 128, 512), BF16),
                   jax.ShapeDtypeStruct((1, 128, 512), BF16), jax.ShapeDtypeStruct((16, 1024), F32)),
        in_specs=[hbm] * 5 + [smem] * 2,
        out_specs=[hbm] * 3 + [pl.BlockSpec(memory_space=pltpu.VMEM)],
        scratch_shapes=[
            V((4, 128, 512), BF16), V((4, 128, 512), BF16), V((4, 4, 256, 256), BF16),
            V((8, 4, 2, 128, 256), BF16),
            V((4, 3584, 256), F32), V((4, 3584, 256), F32), V((4096, 128), F32), V((4096, 128), F32),
            V((4, 128, 512), BF16),
            V((4, 4, 128, 256), BF16), V((4, 4, 128, 256), BF16),
            V((2, 2, 4, 128, 128), BF16), V((2, 2, 4, 128, 128), BF16),
            V((2, 4, 128, 128), F32), V((2, 4, 128, 128), F32), V((2, 4, 128, 128), BF16), V((2, 4, 128, 128), BF16),
            V((2, 4, 2, 128, 128), BF16),
            V((2, 4, 2, 256, 128), BF16), V((2, 3, 2, 256, 128), BF16), V((8, 256, 1024), BF16),
            V((128, 4096), BF16), V((8, 3, 16, 256), F32), V((4, 16, 256), F32), V((4, 1, 256), F32),
            V((5, 128, 256), F32), V((2, 2, 4, 4, 16, 128), BF16),
            V((2, 7, 4, 16, 128), BF16), V((4, 16, 256), F32), V((4, 16, 256), F32),
            dma, dma, dma((3,)), dma((2,)), dma((4,)), dma((8,)), dma((4,)), dma, dma((2, 2)), dma, dma, dma, dma,
            dma, dma, dma((4,)), dma((2, 2)), dma((2,)), dma((2,)), dma((2,)), dma, dma((2,)), dma((2,)), dma((4,)), dma((4,)),
            dma((6,)), dma, dma,
        ],
        compiler_params=pltpu.CompilerParams(collective_id=0, has_side_effects=True, vmem_limit_bytes=60 << 20),
    )(query, out_grad, keys, values, normed_input, q_start, q_len)
    return pl.pallas_call(
        place,
        name="place_outputs",
        out_shape=[jax.ShapeDtypeStruct(o.shape, o.dtype) for o in outs],
        in_specs=[pl.BlockSpec(memory_space=pltpu.VMEM)] * 4,
        out_specs=[hbm] * 4,
        scratch_shapes=[dma((4,))],
    )(*outs)


def solution(mesh):
    tok = P("dp", "seq", None)
    return jax.shard_map(
        local, mesh=mesh,
        in_specs=(tok, tok, tok, tok, tok, P("dp"), P("dp")),
        out_specs=(tok, tok, tok, P(("seq", "dp"), None)),
        check_vma=False)
```

```python
import math
import jax
import jax.numpy as jnp
from jax import lax
from jax.experimental import pallas as pl
from jax.experimental.pallas import tpu as pltpu
from jax.sharding import PartitionSpec as P

HEAD_DIM = 128
SCALE = 1.0 / math.sqrt(HEAD_DIM)
EXPC = SCALE * math.log2(math.e)
NEG = -1e30
F32 = jnp.float32
BF16 = jnp.bfloat16


def dot_nt(a, b):
    return lax.dot_general(a, b, (((1,), (1,)), ((), ())), preferred_element_type=F32)


def dot_nn(a, b):
    return lax.dot_general(a, b, (((1,), (0,)), ((), ())), preferred_element_type=F32)


def dot_tn(a, b):
    return lax.dot_general(a, b, (((0,), (0,)), ((), ())), preferred_element_type=F32)


def coords():
    seq = lax.axis_index("seq")
    c = lax.rem(seq, 2)
    x = lax.rem(seq // 2, 4)
    zh = lax.rem(seq // 8, 2)
    yl = lax.rem(seq // 16, 2)
    s = seq // 32
    zl = lax.axis_index("dp")
    return s, yl, zh, x, c, zl


def seq_of(s, yl, zh, x, c):
    return s * 32 + yl * 16 + zh * 8 + x * 2 + c


def rcopy(src, dst, ssem, rsem, dev):
    return pltpu.make_async_remote_copy(
        src_ref=src, dst_ref=dst, send_sem=ssem, recv_sem=rsem,
        device_id={"seq": dev[0], "dp": dev[1]}, device_id_type=pl.DeviceIdType.MESH)


def greet(peers):
    barrier = pltpu.get_barrier_semaphore()
    for seq, dp in peers:
        pl.semaphore_signal(barrier, inc=1, device_id={"seq": seq, "dp": dp},
                            device_id_type=pl.DeviceIdType.MESH)
    pl.semaphore_wait(barrier, len(peers))


def blk(i, w):
    return pl.ds(pl.multiple_of(i * w, w), w)


def body(q_in, g_in, k_in, v_in, n_in, start_ref, len_ref,
         dq_out, kg_out, vg_out, w_out,
         q_ref, g_ref, kv, nbuf, s_ref, d_ref, dk_ref, dv_ref, dq_ref,
         csend, crx, ysend, yrx, acc0, acc1, zsend, zrx, kga,
         w1s, w1r, nt, kt_ref, st, fac, dlt, dqa, w2s, w2r, w3s, w4r,
         s1, s3, kx_r, qx_r, kz_r, ky_r, kc_r, n_s, n_r, nf_s, nf_r, nc_s, nc_r, dq_s, dq_r,
         c_r, y_r, z_s, z_r, kc2_r, ko_r, w1_r, w2_r, w4_s, w4_r, l_sem, nl_sem, dql_sem):
    s, yl, zh, x, c, zl = coords()
    y = s * 2 + yl
    z = zh * 4 + zl
    me8 = x * 2 + c

    def dev(s_=None, yl_=None, zh_=None, x_=None, c_=None, zl_=None):
        return (seq_of(s if s_ is None else s_, yl if yl_ is None else yl_, zh if zh_ is None else zh_,
                       x if x_ is None else x_, c if c_ is None else c_), zl if zl_ is None else zl_)

    row8 = [lax.rem(me8 + d, 8) for d in range(1, 8)]
    xs = [lax.rem(x + d, 4) for d in range(1, 4)]
    ys = [lax.rem(y + d, 4) for d in range(1, 4)]
    zs = [lax.rem(z + d, 8) for d in range(1, 8)]
    ydev = [dev(s_=p // 2, yl_=lax.rem(p, 2)) for p in ys]
    zdev = [dev(zh_=p // 4, zl_=lax.rem(p, 4)) for p in zs]
    core_dev = dev(c_=1 - c)
    y_dev = dev(yl_=1 - yl)
    z_dev = dev(zh_=1 - zh)
    greet([dev(x_=p // 2, c_=lax.rem(p, 2)) for p in row8] + ydev + zdev)

    sent = {}

    def go(cp, key, kb):
        cp.start()
        sent[key] = sent.get(key, 0) + kb
        return cp

    def kib(n):
        return s_ref.at[0, pl.ds(0, n)]

    def drain(sem, n):
        rcopy(kib(n), kib(n), sem, sem, (seq_of(s, yl, zh, x, 1 - c), zl)).wait_send()

    def got(sem, n):
        rcopy(kib(n), kib(n), sem, sem, (seq_of(s, yl, zh, x, 1 - c), zl)).wait_recv()

    crow = blk(c, 128)
    last = yl * zh

    def slot(yl_, zh_, plane):
        return jnp.where(yl_ == 0, jnp.where(zh_ == plane, 0, 1), 2 + zh_)

    mine = slot(yl, zh, zh)
    for i, px in enumerate(xs):
        go(rcopy(k_in.at[0, :, blk(px, 128)], kv.at[mine, x, crow, pl.ds(0, 128)], s1, kx_r.at[i], dev(x_=px)), 1, 32)
        go(rcopy(v_in.at[0, :, blk(px, 128)], kv.at[mine, x, crow, pl.ds(128, 128)], s1, kx_r.at[i], dev(x_=px)), 1, 32)
    own_kv = [pltpu.make_async_copy(k_in.at[0, :, blk(x, 128)], kv.at[mine, x, crow, pl.ds(0, 128)], l_sem.at[0]),
              pltpu.make_async_copy(v_in.at[0, :, blk(x, 128)], kv.at[mine, x, crow, pl.ds(128, 128)], l_sem.at[1])]
    own_q = [pltpu.make_async_copy(q_in.at[0, :, blk(x, 512)], q_ref.at[x], l_sem.at[2]),
             pltpu.make_async_copy(g_in.at[0, :, blk(x, 512)], g_ref.at[x], l_sem.at[3])]
    for cp in own_kv + own_q:
        cp.start()

    def q_send(ph):
        for i, px in enumerate(xs):
            src = pl.ds(pl.multiple_of(px * 512 + ph * 256, 256), 256)
            dst = pl.ds(ph * 256, 256)
            go(rcopy(q_in.at[0, :, src], q_ref.at[x, :, dst], s1, qx_r.at[ph], dev(x_=px)), 1, 64)
            go(rcopy(g_in.at[0, :, src], g_ref.at[x, :, dst], s1, qx_r.at[ph], dev(x_=px)), 1, 64)

    q_send(0)

    def piece(sl, k):
        return kv.at[sl, lax.rem(x - k + 4, 4), crow]

    def to_core(e, k, p):
        return rcopy(p, p, s1, kc_r.at[e], core_dev)

    def z_copy(k):
        return rcopy(piece(mine, k), piece(slot(yl, zh, 1 - zh), k), s1, kz_r.at[k], z_dev)

    def y_copy(e, sl, k):
        return rcopy(piece(sl, k), piece(sl, k), s1, ky_r.at[4 * e + k], y_dev)

    for k in range(4):
        if k == 0:
            for cp in own_kv:
                cp.wait()
        else:
            got(kx_r.at[k - 1], 64)
        go(z_copy(k), 1, 64)
        go(y_copy(0, mine, k), 1, 64)
        go(to_core(0, k, piece(mine, k)), 1, 64)
    ev = [mine, slot(1 - yl, zh, zh), slot(yl, 1 - zh, zh), slot(1 - yl, 1 - zh, zh)]

    dk_ref[...] = jnp.zeros_like(dk_ref)
    dv_ref[...] = jnp.zeros_like(dv_ref)
    st[:, 0] = jnp.full((8, 16, 256), NEG, F32)
    st[:, 1:3] = jnp.zeros((8, 2, 16, 256), F32)
    dqa[...] = jnp.zeros_like(dqa)
    start = start_ref[s]
    end = start + len_ref[s]
    lane = lax.broadcasted_iota(jnp.int32, (1, 256), 1)

    def keys(j, n):
        if isinstance(j, int):
            return kv[j // 4, j % 4:j % 4 + n].reshape(n * 256, 256)[:, 0:128]
        return kv[j // 4, pl.ds(lax.rem(j, 4), n), :, 0:128].reshape(n * 256, 128)

    def values(j):
        return kv[j // 4, j % 4, :, 128:256]

    def rows_of(j, n=1):
        return pl.ds(j * 256 if isinstance(j, int) else pl.multiple_of(j * 256, 256), n * 256)

    def unit(u):
        h, half = u // 2, (u % 2 if isinstance(u, int) else lax.rem(u, 2))
        cols = pl.ds(h * 128 if isinstance(h, int) else pl.multiple_of(h * 128, 128), 128)
        xx = pl.ds(2 * half, 2)
        pos = yl * 2048 + zh * 1024 + (2 * half + lane // 128) * 256 + c * 128 + lax.rem(lane, 128)
        lim = jnp.maximum(start, jnp.minimum(end, pos + 1))
        return q_ref[xx, :, cols].reshape(256, 128), g_ref[xx, :, cols].reshape(256, 128), lim

    def dq_store(u, dq):
        h, half = u // 2, (u % 2 if isinstance(u, int) else lax.rem(u, 2))
        cols = pl.ds(h * 128 if isinstance(h, int) else pl.multiple_of(h * 128, 128), 128)
        dq_ref[pl.ds(2 * half, 2), :, cols] = (dq.T * SCALE).astype(BF16).reshape(2, 128, 128)

    def pass12(u, su, j, masked):
        q, g, lim = unit(u)
        rows = rows_of(j)
        sc = dot_nt(kv[j // 4, (j % 4 if isinstance(j, int) else lax.rem(j, 4)), :, 0:128], q)
        if masked:
            kpos = lax.broadcasted_iota(jnp.int32, (256, 256), 0)
            sc = jnp.where(kpos < lim - j * 256, sc, NEG)
        m = jnp.max(sc, axis=0, keepdims=True)
        e = jnp.exp2((sc - m) * EXPC)
        dp = dot_nt(kv[j // 4, (j % 4 if isinstance(j, int) else lax.rem(j, 4)), :, 128:256], g)
        st[u, 0, pl.ds(j, 1)] = m
        st[u, 1, pl.ds(j, 1)] = jnp.sum(e, axis=0, keepdims=True)
        st[u, 2, pl.ds(j, 1)] = jnp.sum(e * dp, axis=0, keepdims=True)
        s_ref[su, rows, :] = e
        d_ref[su, rows, :] = dp

    def finish(u, su):
        m = jnp.max(st[u, 0], axis=0, keepdims=True)
        f = jnp.exp2((st[u, 0] - m) * EXPC)
        f = f * (1.0 / jnp.sum(st[u, 1] * f, axis=0, keepdims=True))
        fac[su] = f
        dlt[su] = jnp.sum(st[u, 2] * f, axis=0, keepdims=True)

    def pass3(u, su, j, n, dq):
        q, g, _ = unit(u)
        dlv = dlt[su]
        ds_, p_ = [], []
        for i in range(n):
            r = rows_of(j + i)
            p = s_ref[su, r, :] * fac[su, pl.ds(j + i, 1)]
            ds_.append((p * (d_ref[su, r, :] - dlv)).astype(BF16))
            p_.append(p.astype(BF16))
        ds = ds_[0] if n == 1 else jnp.concatenate(ds_, axis=0)
        p = p_[0] if n == 1 else jnp.concatenate(p_, axis=0)
        rows = rows_of(j, n)
        dk_ref[rows, :] += dot_nn(ds, q)
        dv_ref[rows, :] += dot_nn(p, g)
        return dq + dot_nn(kt_ref[:, rows], ds)

    def arrive(e):
        sl = ev[e]

        def one(b, carry):
            j = sl * 4 + b
            kt_ref[:, rows_of(j)] = keys(j, 1).T
            for u in range(4):
                pass12(u, u, j, True)
            return carry
        lax.fori_loop(0, jnp.where(sl < 3, 4, 2 * last), one, 0)

    for k in range(4):
        y_copy(0, ev[1], k).wait_recv()
        go(to_core(1, k, piece(ev[1], k)), 1, 64)
    for cp in own_q:
        cp.wait()
    got(qx_r.at[0], 384)
    q_send(1)
    got(kc_r.at[0], 256)
    arrive(0)

    def n_copy(rr, side, cc_):
        px = lax.rem(x + (1 if side == 0 else 3), 4)
        return rcopy(n_in.at[0, :, pl.ds(pl.multiple_of(rr * 512 + cc_ * 256, 256), 256)], nbuf.at[rr, x, c],
                     n_s, n_r.at[side, rr // 4], dev(x_=px, c_=cc_))

    def n_fwd(i, side, cc_):
        rr = i + 4 * side
        src = nbuf.at[rr, lax.rem(x + (3 if side == 0 else 1), 4), cc_]
        px = lax.rem(x + (1 if side == 0 else 3), 4)
        return rcopy(src, src, nf_s, nf_r, dev(x_=px))

    def nsend(i, carry):
        for cc_ in range(2):
            n_copy(i, 0, cc_).start()
            n_copy(lax.rem(i + 4, 8), 1, cc_).start()
        mine_ = pl.ds(pl.multiple_of(i * 512 + c * 256, 256), 256)
        theirs = pl.ds(pl.multiple_of(i * 512 + (1 - c) * 256, 256), 256)
        rcopy(n_in.at[0, :, theirs], nbuf.at[i, x, c], nc_s, nc_r, core_dev).start()
        pltpu.make_async_copy(n_in.at[0, :, mine_], nbuf.at[i, x, c], nl_sem).start()
        return carry

    def far_piece(k):
        z_copy(k).wait_recv()
        go(y_copy(1, ev[2], k), 1, 64)
        go(to_core(2, k, piece(ev[2], k)), 1, 64)

    far_piece(0)
    far_piece(1)
    lax.fori_loop(0, 8, nsend, 0)
    got(kc_r.at[1], 256)
    arrive(1)
    far_piece(2)
    far_piece(3)
    for k in range(4):
        y_copy(1, ev[3], k).wait_recv()
        go(to_core(3, k, piece(ev[3], k)), 1, 64)
    got(kc_r.at[2], 256)
    arrive(2)
    got(kc_r.at[3], 256)
    arrive(3)
    for u in range(4):
        finish(u, u)
    got(qx_r.at[1], 384)

    def mid(u, carry):
        dq = jnp.zeros((128, 256), F32)
        for j in range(12):
            dq = pass3(u, u, j, 1, dq)
            pass12(u + 4, u, j, j >= 8)
        dqa[4] = dq

        @pl.when(last == 1)
        def _():
            d2 = dqa[4]
            for j in range(12, 14):
                d2 = pass3(u, u, j, 1, d2)
                pass12(u + 4, u, j, True)
            dqa[4] = d2
        dq_store(u, dqa[4])
        finish(u + 4, u)
        return carry

    lax.fori_loop(0, 3, mid, 0)

    for side in range(2):
        got(n_r.at[side, side], 512)

    def fwd(i, carry):
        for side in range(2):
            for cc_ in range(2):
                n_fwd(i, side, cc_).start()
        return carry

    lax.fori_loop(0, 4, fwd, 0)
    lax.fori_loop(3, 4, mid, 0)

    def dq_copy(h, i):
        px = xs[i]
        return rcopy(dq_ref.at[px, :, blk(h, 128)], dq_out.at[0, :, blk(x * 4 + h, 128)],
                     dq_s, dq_r, dev(x_=px))

    def dq_local(h):
        return pltpu.make_async_copy(dq_ref.at[x, :, blk(h, 128)], dq_out.at[0, :, blk(x * 4 + h, 128)],
                                     dql_sem)

    def dq_send(h):
        for i in range(3):
            dq_copy(h, i).start()
        dq_local(h).start()

    dq_send(0)
    dq_send(1)

    def back(sl, trips, first=0):
        def two(b, carry):
            j = sl * 4 + 2 * b
            rows = rows_of(j, 2)
            dk = dk_ref[rows, :]
            dv = dv_ref[rows, :]
            for u in range(4):
                q, g, _ = unit(u + 4)
                dlv = dlt[u]
                d_, p_ = [], []
                for i in range(2):
                    r = rows_of(j + i)
                    p = s_ref[u, r, :] * fac[u, pl.ds(j + i, 1)]
                    d_.append((p * (d_ref[u, r, :] - dlv)).astype(BF16))
                    p_.append(p.astype(BF16))
                ds = jnp.concatenate(d_, axis=0)
                dk = dk + dot_nn(ds, q)
                dv = dv + dot_nn(jnp.concatenate(p_, axis=0), g)
                dqa[u] += dot_nn(kt_ref[:, rows], ds)
            dk_ref[rows, :] = dk
            dv_ref[rows, :] = dv
            return carry
        lax.fori_loop(first, trips, two, 0)

    def grads(yl_, zh_, x_, c_):
        r = pl.ds(pl.multiple_of((slot(yl_, zh_, zh) * 4 + x_) * 256 + c_ * 128, 128), 128)
        return jnp.concatenate([dk_ref[r, :] * SCALE, dv_ref[r, :]], axis=1)

    quad = [(1 - yl, 1 - zh), (yl, 1 - zh), (1 - yl, zh), (yl, zh)]
    cx = []

    def core_send(k):
        for x_ in range(4):
            csend[k, x_] = grads(quad[k][0], quad[k][1], x_, 1 - c).astype(BF16)
        cx.append(go(rcopy(csend.at[k], crx.at[k], s3, c_r.at[k], core_dev), 3, 256))

    def pair(k, x_, ch):
        r = pl.ds(pl.multiple_of((slot(quad[k][0], quad[k][1], zh) * 4 + x_) * 256 + c * 128, 128), 128)
        own = dk_ref[r, :] * SCALE if ch == 0 else dv_ref[r, :]
        return own + crx[k, x_, :, ch * 128:(ch + 1) * 128].astype(F32)

    yx = {}

    def y_stage(k, sl):
        cx[k].wait_recv()
        for ch in (1, 0):
            for x_ in range(4):
                ysend[sl, ch, x_] = pair(k, x_, ch).astype(BF16)
            yx[sl, ch] = go(rcopy(ysend.at[sl, ch], yrx.at[sl, ch], s3, y_r.at[sl, ch], y_dev), 3, 128)

    back(1, 2)
    back(2, 2 * zh)
    core_send(0)
    core_send(1)
    back(0, 1)
    y_stage(0, 0)
    back(0, 2, 1)
    cx[1].wait_recv()
    for ch in range(2):
        for x_ in range(4):
            acc1[ch, x_] = pair(1, x_, ch)
    back(2, 2 * (1 - zh))
    zx = {}

    def z_stage(ch):
        yx[0, ch].wait_recv()
        zsend[ch] = (acc1[ch] + yrx[0, ch].astype(F32)).astype(BF16)
        zx[ch] = rcopy(zsend.at[ch], zrx.at[ch], z_s.at[ch], z_r.at[ch], z_dev)
        zx[ch].start()

    z_stage(1)
    back(3, last)
    core_send(2)
    core_send(3)
    y_stage(2, 1)
    for u in range(4):
        dq_store(u + 4, dqa[u])
    dq_send(2)
    dq_send(3)
    cx[3].wait_recv()
    for ch in range(2):
        for x_ in range(4):
            acc0[ch, x_] = pair(3, x_, ch)
    for ch in (1, 0):
        yx[1, ch].wait_recv()
        acc0[ch] = acc0[ch] + yrx[1, ch].astype(F32)

    zx[1].wait_send()
    z_stage(0)
    for side in range(2):
        got(n_r.at[side, 1 - side], 512)
    got(nf_r, 1024)
    got(nc_r, 512)
    pltpu.make_async_copy(kib(512), d_ref.at[0, pl.ds(0, 512)], nl_sem).wait()

    def turn(i, carry):
        nt[i] = nbuf[i].reshape(1024, 256).T
        return carry

    lax.fori_loop(0, 8, turn, 0)

    border = [1 - zh, zh]
    ko_own = []

    def final_half(ch):
        zx[ch].wait_recv()
        kga[ch, :, pl.ds(c, 1)] = (acc0[ch] + zrx[ch].astype(F32)).astype(BF16).reshape(4, 1, 128, 128)
        own = kga.at[ch, :, c]
        k2 = go(rcopy(own, own, s3, kc2_r.at[ch], core_dev), 3, 128)
        out = kg_out if ch == 0 else vg_out
        for i, px in enumerate(xs):
            go(rcopy(kga.at[ch, px, c], out.at[0, :, blk(x, 128)], s3, ko_r, dev(x_=px)), 3, 32)
        cp = pltpu.make_async_copy(kga.at[ch, x, c], out.at[0, :, blk(x, 128)], l_sem.at[4 + ch])
        cp.start()
        ko_own.append(cp)
        k2.wait_recv()
        kgall = kga[ch].reshape(1024, 128)
        w1s[ch] = dot_nn(nt[...].reshape(2048, 1024), kgall).astype(BF16).reshape(4, 2, 256, 128)
        for d in range(3):
            py = lax.rem(y + d + 1, 4)
            go(rcopy(w1s.at[ch, py], w1r.at[ch, d], s3, w1_r.at[ch], ydev[d]), 3, 128)

    def z_half(ch):
        got(w1_r.at[ch], 384)
        for bi, b in enumerate(border):
            t = w1s[ch, y, b].astype(F32)
            for d in range(3):
                t = t + w1r[ch, d, b].astype(F32)
            w2s[ch, bi] = t.astype(BF16).reshape(4, 4, 16, 128)
            for i in range(bi, 4):
                pz = lax.rem(zl + i, 4)
                sl = i if bi == 0 else 3 + i
                go(rcopy(w2s.at[ch, bi, :, pz], w2r.at[ch, sl], s3, w2_r.at[ch], dev(zh_=b, zl_=pz)), 3, 16)

    final_half(1)
    final_half(0)
    z_half(1)
    z_half(0)
    for ch in (1, 0):
        got(w2_r.at[ch], 112)
        t = w2s[ch, 1, :, pl.ds(zl, 1)].reshape(4, 16, 128).astype(F32)
        for i in range(7):
            t = t + w2r[ch, i].astype(F32)
        w3s[:, :, ch * 128:(ch + 1) * 128] = t
    self_core = x // 2

    def w4_copy(xl, cc_):
        return rcopy(w3s.at[xl * 2 + cc_], w4r.at[x], w4_s.at[xl * 2 + cc_], w4_r.at[x],
                     dev(x_=2 * c + xl, c_=cc_))

    for xl in range(2):
        for cc_ in range(2):
            is_me = (2 * c + xl == x) & (c == cc_)

            @pl.when(is_me)
            def _():
                w4r[pl.ds(x, 1)] = w3s[xl * 2 + cc_].reshape(1, 16, 256)

            @pl.when(jnp.logical_not(is_me))
            def _():
                w4_copy(xl, cc_).start()
    for xx in range(4):
        @pl.when(jnp.logical_not((x == xx) & (c == self_core)))
        def _():
            rcopy(w3s.at[0], w4r.at[xx], w4_s.at[0], w4_r.at[xx], core_dev).wait_recv()
    for xx in range(4):
        w_out[:, xx * 128:(xx + 1) * 128] = w4r[xx, :, 0:128]
        w_out[:, 512 + xx * 128:512 + (xx + 1) * 128] = w4r[xx, :, 128:256]
    for xl in range(2):
        for cc_ in range(2):
            @pl.when(jnp.logical_not((2 * c + xl == x) & (c == cc_)))
            def _():
                w4_copy(xl, cc_).wait_send()
    drain(dq_s, 384)
    got(dq_r, 384)
    pltpu.make_async_copy(kib(128), d_ref.at[0, pl.ds(0, 128)], dql_sem).wait()
    got(ko_r, 192)
    for cp in ko_own:
        cp.wait()
    zx[0].wait_send()
    drain(n_s, 2048)
    drain(nf_s, 1024)
    drain(nc_s, 512)
    drain(s1, sent[1])
    drain(s3, sent[3])


def place(*refs):
    ins, outs, sem = refs[:4], refs[4:8], refs[8]
    cps = [pltpu.make_async_copy(a, b, sem.at[i]) for i, (a, b) in enumerate(zip(ins, outs))]
    for cp in cps:
        cp.start()
    for cp in cps:
        cp.wait()


def local(query, keys, values, out_grad, normed_input, q_start, q_len):
    dma = pltpu.SemaphoreType.DMA
    V = pltpu.VMEM
    hbm = pl.BlockSpec(memory_space=pl.ANY)
    smem = pl.BlockSpec(memory_space=pltpu.SMEM)
    outs = pl.pallas_call(
        body,
        name="attention_grads",
        out_shape=(jax.ShapeDtypeStruct((1, 128, 2048), BF16), jax.ShapeDtypeStruct((1, 128, 512), BF16),
                   jax.ShapeDtypeStruct((1, 128, 512), BF16), jax.ShapeDtypeStruct((16, 1024), F32)),
        in_specs=[hbm] * 5 + [smem] * 2,
        out_specs=[hbm] * 3 + [pl.BlockSpec(memory_space=pltpu.VMEM)],
        scratch_shapes=[
            V((4, 128, 512), BF16), V((4, 128, 512), BF16), V((4, 4, 256, 256), BF16),
            V((8, 4, 2, 128, 256), BF16),
            V((4, 3584, 256), F32), V((4, 3584, 256), F32), V((4096, 128), F32), V((4096, 128), F32),
            V((4, 128, 512), BF16),
            V((4, 4, 128, 256), BF16), V((4, 4, 128, 256), BF16),
            V((2, 2, 4, 128, 128), BF16), V((2, 2, 4, 128, 128), BF16),
            V((2, 4, 128, 128), F32), V((2, 4, 128, 128), F32), V((2, 4, 128, 128), BF16), V((2, 4, 128, 128), BF16),
            V((2, 4, 2, 128, 128), BF16),
            V((2, 4, 2, 256, 128), BF16), V((2, 3, 2, 256, 128), BF16), V((8, 256, 1024), BF16),
            V((128, 4096), BF16), V((8, 3, 16, 256), F32), V((4, 16, 256), F32), V((4, 1, 256), F32),
            V((5, 128, 256), F32), V((2, 2, 4, 4, 16, 128), BF16),
            V((2, 7, 4, 16, 128), BF16), V((4, 16, 256), F32), V((4, 16, 256), F32),
            dma, dma, dma((3,)), dma((2,)), dma((4,)), dma((8,)), dma((4,)), dma, dma((2, 2)), dma, dma, dma, dma,
            dma, dma, dma((4,)), dma((2, 2)), dma((2,)), dma((2,)), dma((2,)), dma, dma((2,)), dma((2,)), dma((4,)), dma((4,)),
            dma((6,)), dma, dma,
        ],
        compiler_params=pltpu.CompilerParams(collective_id=0, has_side_effects=True, vmem_limit_bytes=60 << 20),
    )(query, out_grad, keys, values, normed_input, q_start, q_len)
    return pl.pallas_call(
        place,
        name="place_outputs",
        out_shape=[jax.ShapeDtypeStruct(o.shape, o.dtype) for o in outs],
        in_specs=[pl.BlockSpec(memory_space=pltpu.VMEM)] * 4,
        out_specs=[hbm] * 4,
        scratch_shapes=[dma((4,))],
    )(*outs)


def solution(mesh):
    tok = P("dp", "seq", None)
    return jax.shard_map(
        local, mesh=mesh,
        in_specs=(tok, tok, tok, tok, tok, P("dp"), P("dp")),
        out_specs=(tok, tok, tok, P(("seq", "dp"), None)),
        check_vma=False)
```

```python
import math
import jax
import jax.numpy as jnp
from jax import lax
from jax.experimental import pallas as pl
from jax.experimental.pallas import tpu as pltpu
from jax.sharding import PartitionSpec as P

HEAD_DIM = 128
SCALE = 1.0 / math.sqrt(HEAD_DIM)
EXPC = SCALE * math.log2(math.e)
NEG = -1e30
F32 = jnp.float32
BF16 = jnp.bfloat16


def dot_nt(a, b):
    return lax.dot_general(a, b, (((1,), (1,)), ((), ())), preferred_element_type=F32)


def dot_nn(a, b):
    return lax.dot_general(a, b, (((1,), (0,)), ((), ())), preferred_element_type=F32)


def dot_tn(a, b):
    return lax.dot_general(a, b, (((0,), (0,)), ((), ())), preferred_element_type=F32)


def coords():
    seq = lax.axis_index("seq")
    c = lax.rem(seq, 2)
    x = lax.rem(seq // 2, 4)
    zh = lax.rem(seq // 8, 2)
    yl = lax.rem(seq // 16, 2)
    s = seq // 32
    zl = lax.axis_index("dp")
    return s, yl, zh, x, c, zl


def seq_of(s, yl, zh, x, c):
    return s * 32 + yl * 16 + zh * 8 + x * 2 + c


def rcopy(src, dst, ssem, rsem, dev):
    return pltpu.make_async_remote_copy(
        src_ref=src, dst_ref=dst, send_sem=ssem, recv_sem=rsem,
        device_id={"seq": dev[0], "dp": dev[1]}, device_id_type=pl.DeviceIdType.MESH)


def greet(peers):
    barrier = pltpu.get_barrier_semaphore()
    for seq, dp in peers:
        pl.semaphore_signal(barrier, inc=1, device_id={"seq": seq, "dp": dp},
                            device_id_type=pl.DeviceIdType.MESH)
    pl.semaphore_wait(barrier, len(peers))


def blk(i, w):
    return pl.ds(pl.multiple_of(i * w, w), w)


def body(q_in, g_in, k_in, v_in, n_in, start_ref, len_ref,
         dq_out, kg_out, vg_out, w_out,
         q_ref, g_ref, kv, nbuf, s_ref, d_ref, dk_ref, dv_ref, dq_ref,
         csend, crx, ysend, yrx, acc0, acc1, zsend, zrx, kga,
         w1s, w1r, nt, kt_ref, st, fac, dlt, dqa, w2s, w2r, w3s, w4r,
         s1, s3, kx_r, qx_r, kz_r, ky_r, kc_r, n_s, n_r, nf_s, nf_r, nc_s, nc_r, dq_s, dq_r,
         c_r, y_r, z_s, z_r, kc2_r, ko_r, w1_r, w2_r, w4_s, w4_r, l_sem, nl_sem, dql_sem):
    s, yl, zh, x, c, zl = coords()
    y = s * 2 + yl
    z = zh * 4 + zl
    me8 = x * 2 + c

    def dev(s_=None, yl_=None, zh_=None, x_=None, c_=None, zl_=None):
        return (seq_of(s if s_ is None else s_, yl if yl_ is None else yl_, zh if zh_ is None else zh_,
                       x if x_ is None else x_, c if c_ is None else c_), zl if zl_ is None else zl_)

    row8 = [lax.rem(me8 + d, 8) for d in range(1, 8)]
    xs = [lax.rem(x + d, 4) for d in range(1, 4)]
    ys = [lax.rem(y + d, 4) for d in range(1, 4)]
    zs = [lax.rem(z + d, 8) for d in range(1, 8)]
    ydev = [dev(s_=p // 2, yl_=lax.rem(p, 2)) for p in ys]
    zdev = [dev(zh_=p // 4, zl_=lax.rem(p, 4)) for p in zs]
    core_dev = dev(c_=1 - c)
    y_dev = dev(yl_=1 - yl)
    z_dev = dev(zh_=1 - zh)
    greet([dev(x_=p // 2, c_=lax.rem(p, 2)) for p in row8] + ydev + zdev)

    sent = {}

    def go(cp, key, kb):
        cp.start()
        sent[key] = sent.get(key, 0) + kb
        return cp

    def kib(n):
        return s_ref.at[0, pl.ds(0, n)]

    def drain(sem, n):
        rcopy(kib(n), kib(n), sem, sem, (seq_of(s, yl, zh, x, 1 - c), zl)).wait_send()

    def got(sem, n):
        rcopy(kib(n), kib(n), sem, sem, (seq_of(s, yl, zh, x, 1 - c), zl)).wait_recv()

    crow = blk(c, 128)
    last = yl * zh

    def slot(yl_, zh_, plane):
        return jnp.where(yl_ == 0, jnp.where(zh_ == plane, 0, 1), 2 + zh_)

    mine = slot(yl, zh, zh)
    for i, px in enumerate(xs):
        go(rcopy(k_in.at[0, :, blk(px, 128)], kv.at[mine, x, crow, pl.ds(0, 128)], s1, kx_r.at[i], dev(x_=px)), 1, 32)
        go(rcopy(v_in.at[0, :, blk(px, 128)], kv.at[mine, x, crow, pl.ds(128, 128)], s1, kx_r.at[i], dev(x_=px)), 1, 32)
    own_kv = [pltpu.make_async_copy(k_in.at[0, :, blk(x, 128)], kv.at[mine, x, crow, pl.ds(0, 128)], l_sem.at[0]),
              pltpu.make_async_copy(v_in.at[0, :, blk(x, 128)], kv.at[mine, x, crow, pl.ds(128, 128)], l_sem.at[1])]
    own_q = [pltpu.make_async_copy(q_in.at[0, :, blk(x, 512)], q_ref.at[x], l_sem.at[2]),
             pltpu.make_async_copy(g_in.at[0, :, blk(x, 512)], g_ref.at[x], l_sem.at[3])]
    for cp in own_kv + own_q:
        cp.start()

    def q_send(ph):
        for i, px in enumerate(xs):
            src = pl.ds(pl.multiple_of(px * 512 + ph * 256, 256), 256)
            dst = pl.ds(ph * 256, 256)
            go(rcopy(q_in.at[0, :, src], q_ref.at[x, :, dst], s1, qx_r.at[ph], dev(x_=px)), 1, 64)
            go(rcopy(g_in.at[0, :, src], g_ref.at[x, :, dst], s1, qx_r.at[ph], dev(x_=px)), 1, 64)

    q_send(0)

    def piece(sl, k):
        return kv.at[sl, lax.rem(x - k + 4, 4), crow]

    def to_core(e, k, p):
        return rcopy(p, p, s1, kc_r.at[e], core_dev)

    def z_copy(k):
        return rcopy(piece(mine, k), piece(slot(yl, zh, 1 - zh), k), s1, kz_r.at[k], z_dev)

    def y_copy(e, sl, k):
        return rcopy(piece(sl, k), piece(sl, k), s1, ky_r.at[4 * e + k], y_dev)

    for k in range(4):
        if k == 0:
            for cp in own_kv:
                cp.wait()
        else:
            got(kx_r.at[k - 1], 64)
        go(z_copy(k), 1, 64)
        go(y_copy(0, mine, k), 1, 64)
        go(to_core(0, k, piece(mine, k)), 1, 64)
    ev = [mine, slot(1 - yl, zh, zh), slot(yl, 1 - zh, zh), slot(1 - yl, 1 - zh, zh)]

    dk_ref[...] = jnp.zeros_like(dk_ref)
    dv_ref[...] = jnp.zeros_like(dv_ref)
    st[:, 0] = jnp.full((8, 16, 256), NEG, F32)
    st[:, 1:3] = jnp.zeros((8, 2, 16, 256), F32)
    dqa[...] = jnp.zeros_like(dqa)
    start = start_ref[s]
    end = start + len_ref[s]
    lane = lax.broadcasted_iota(jnp.int32, (1, 256), 1)

    def keys(j, n):
        if isinstance(j, int):
            return kv[j // 4, j % 4:j % 4 + n].reshape(n * 256, 256)[:, 0:128]
        return kv[j // 4, pl.ds(lax.rem(j, 4), n), :, 0:128].reshape(n * 256, 128)

    def values(j):
        return kv[j // 4, j % 4, :, 128:256]

    def rows_of(j, n=1):
        return pl.ds(j * 256 if isinstance(j, int) else pl.multiple_of(j * 256, 256), n * 256)

    def unit(u):
        h, half = u // 2, (u % 2 if isinstance(u, int) else lax.rem(u, 2))
        cols = pl.ds(h * 128 if isinstance(h, int) else pl.multiple_of(h * 128, 128), 128)
        xx = pl.ds(2 * half, 2)
        pos = yl * 2048 + zh * 1024 + (2 * half + lane // 128) * 256 + c * 128 + lax.rem(lane, 128)
        lim = jnp.maximum(start, jnp.minimum(end, pos + 1))
        return q_ref[xx, :, cols].reshape(256, 128), g_ref[xx, :, cols].reshape(256, 128), lim

    def dq_store(u, dq):
        h, half = u // 2, (u % 2 if isinstance(u, int) else lax.rem(u, 2))
        cols = pl.ds(h * 128 if isinstance(h, int) else pl.multiple_of(h * 128, 128), 128)
        dq_ref[pl.ds(2 * half, 2), :, cols] = (dq.T * SCALE).astype(BF16).reshape(2, 128, 128)

    def pass12(u, su, j, masked):
        q, g, lim = unit(u)
        rows = rows_of(j)
        sc = dot_nt(kv[j // 4, (j % 4 if isinstance(j, int) else lax.rem(j, 4)), :, 0:128], q)
        if masked:
            kpos = lax.broadcasted_iota(jnp.int32, (256, 256), 0)
            sc = jnp.where(kpos < lim - j * 256, sc, NEG)
        m = jnp.max(sc, axis=0, keepdims=True)
        e = jnp.exp2((sc - m) * EXPC)
        dp = dot_nt(kv[j // 4, (j % 4 if isinstance(j, int) else lax.rem(j, 4)), :, 128:256], g)
        st[u, 0, pl.ds(j, 1)] = m
        st[u, 1, pl.ds(j, 1)] = jnp.sum(e, axis=0, keepdims=True)
        st[u, 2, pl.ds(j, 1)] = jnp.sum(e * dp, axis=0, keepdims=True)
        s_ref[su, rows, :] = e
        d_ref[su, rows, :] = dp

    def finish(u, su):
        m = jnp.max(st[u, 0], axis=0, keepdims=True)
        f = jnp.exp2((st[u, 0] - m) * EXPC)
        f = f * (1.0 / jnp.sum(st[u, 1] * f, axis=0, keepdims=True))
        fac[su] = f
        dlt[su] = jnp.sum(st[u, 2] * f, axis=0, keepdims=True)

    def pass3(u, su, j, n, dq):
        q, g, _ = unit(u)
        dlv = dlt[su]
        ds_, p_ = [], []
        for i in range(n):
            r = rows_of(j + i)
            p = s_ref[su, r, :] * fac[su, pl.ds(j + i, 1)]
            ds_.append((p * (d_ref[su, r, :] - dlv)).astype(BF16))
            p_.append(p.astype(BF16))
        ds = ds_[0] if n == 1 else jnp.concatenate(ds_, axis=0)
        p = p_[0] if n == 1 else jnp.concatenate(p_, axis=0)
        rows = rows_of(j, n)
        dk_ref[rows, :] += dot_nn(ds, q)
        dv_ref[rows, :] += dot_nn(p, g)
        return dq + dot_nn(kt_ref[:, rows], ds)

    def arrive(e):
        sl = ev[e]

        def one(b, carry):
            j = sl * 4 + b
            kt_ref[:, rows_of(j)] = keys(j, 1).T
            for u in range(4):
                pass12(u, u, j, True)
            return carry
        lax.fori_loop(0, jnp.where(sl < 3, 4, 2 * last), one, 0)

    for k in range(4):
        y_copy(0, ev[1], k).wait_recv()
        go(to_core(1, k, piece(ev[1], k)), 1, 64)
    for cp in own_q:
        cp.wait()
    got(qx_r.at[0], 384)
    q_send(1)
    got(kc_r.at[0], 256)
    arrive(0)

    def n_copy(rr, side, cc_):
        px = lax.rem(x + (1 if side == 0 else 3), 4)
        return rcopy(n_in.at[0, :, pl.ds(pl.multiple_of(rr * 512 + cc_ * 256, 256), 256)], nbuf.at[rr, x, c],
                     n_s, n_r.at[side, rr // 4], dev(x_=px, c_=cc_))

    def n_fwd(i, side, cc_):
        rr = i + 4 * side
        src = nbuf.at[rr, lax.rem(x + (3 if side == 0 else 1), 4), cc_]
        px = lax.rem(x + (1 if side == 0 else 3), 4)
        return rcopy(src, src, nf_s, nf_r, dev(x_=px))

    def nsend(i, carry):
        for cc_ in range(2):
            n_copy(i, 0, cc_).start()
            n_copy(lax.rem(i + 4, 8), 1, cc_).start()
        mine_ = pl.ds(pl.multiple_of(i * 512 + c * 256, 256), 256)
        theirs = pl.ds(pl.multiple_of(i * 512 + (1 - c) * 256, 256), 256)
        rcopy(n_in.at[0, :, theirs], nbuf.at[i, x, c], nc_s, nc_r, core_dev).start()
        pltpu.make_async_copy(n_in.at[0, :, mine_], nbuf.at[i, x, c], nl_sem).start()
        return carry

    def far_piece(k):
        z_copy(k).wait_recv()
        go(y_copy(1, ev[2], k), 1, 64)
        go(to_core(2, k, piece(ev[2], k)), 1, 64)

    far_piece(0)
    far_piece(1)
    lax.fori_loop(0, 8, nsend, 0)
    got(kc_r.at[1], 256)
    arrive(1)
    far_piece(2)
    far_piece(3)
    for k in range(4):
        y_copy(1, ev[3], k).wait_recv()
        go(to_core(3, k, piece(ev[3], k)), 1, 64)
    got(kc_r.at[2], 256)
    arrive(2)
    got(kc_r.at[3], 256)
    arrive(3)
    for u in range(4):
        finish(u, u)
    got(qx_r.at[1], 384)

    def mid(u, carry):
        dq = jnp.zeros((128, 256), F32)
        for j in range(12):
            dq = pass3(u, u, j, 1, dq)
            pass12(u + 4, u, j, j >= 8)
        dqa[4] = dq

        @pl.when(last == 1)
        def _():
            d2 = dqa[4]
            for j in range(12, 14):
                d2 = pass3(u, u, j, 1, d2)
                pass12(u + 4, u, j, True)
            dqa[4] = d2
        dq_store(u, dqa[4])
        finish(u + 4, u)
        return carry

    lax.fori_loop(0, 3, mid, 0)

    for side in range(2):
        got(n_r.at[side, side], 512)

    def fwd(i, carry):
        for side in range(2):
            for cc_ in range(2):
                n_fwd(i, side, cc_).start()
        return carry

    lax.fori_loop(0, 4, fwd, 0)
    lax.fori_loop(3, 4, mid, 0)

    def dq_copy(h, i):
        px = xs[i]
        return rcopy(dq_ref.at[px, :, blk(h, 128)], dq_out.at[0, :, blk(x * 4 + h, 128)],
                     dq_s, dq_r, dev(x_=px))

    def dq_local(h):
        return pltpu.make_async_copy(dq_ref.at[x, :, blk(h, 128)], dq_out.at[0, :, blk(x * 4 + h, 128)],
                                     dql_sem)

    def dq_send(h):
        for i in range(3):
            dq_copy(h, i).start()
        dq_local(h).start()

    dq_send(0)
    dq_send(1)

    def back(sl, trips, first=0):
        def two(b, carry):
            j = sl * 4 + 2 * b
            rows = rows_of(j, 2)
            dk = dk_ref[rows, :]
            dv = dv_ref[rows, :]
            for u in range(4):
                q, g, _ = unit(u + 4)
                dlv = dlt[u]
                d_, p_ = [], []
                for i in range(2):
                    r = rows_of(j + i)
                    p = s_ref[u, r, :] * fac[u, pl.ds(j + i, 1)]
                    d_.append((p * (d_ref[u, r, :] - dlv)).astype(BF16))
                    p_.append(p.astype(BF16))
                ds = jnp.concatenate(d_, axis=0)
                dk = dk + dot_nn(ds, q)
                dv = dv + dot_nn(jnp.concatenate(p_, axis=0), g)
                dqa[u] += dot_nn(kt_ref[:, rows], ds)
            dk_ref[rows, :] = dk
            dv_ref[rows, :] = dv
            return carry
        lax.fori_loop(first, trips, two, 0)

    def grads(yl_, zh_, x_, c_):
        r = pl.ds(pl.multiple_of((slot(yl_, zh_, zh) * 4 + x_) * 256 + c_ * 128, 128), 128)
        return jnp.concatenate([dk_ref[r, :] * SCALE, dv_ref[r, :]], axis=1)

    quad = [(1 - yl, 1 - zh), (yl, 1 - zh), (1 - yl, zh), (yl, zh)]
    cx = []

    def core_send(k):
        for x_ in range(4):
            csend[k, x_] = grads(quad[k][0], quad[k][1], x_, 1 - c).astype(BF16)
        cx.append(go(rcopy(csend.at[k], crx.at[k], s3, c_r.at[k], core_dev), 3, 256))

    def pair(k, x_, ch):
        r = pl.ds(pl.multiple_of((slot(quad[k][0], quad[k][1], zh) * 4 + x_) * 256 + c * 128, 128), 128)
        own = dk_ref[r, :] * SCALE if ch == 0 else dv_ref[r, :]
        return own + crx[k, x_, :, ch * 128:(ch + 1) * 128].astype(F32)

    yx = {}

    def y_stage(k, sl):
        cx[k].wait_recv()
        for ch in (1, 0):
            for x_ in range(4):
                ysend[sl, ch, x_] = pair(k, x_, ch).astype(BF16)
            yx[sl, ch] = go(rcopy(ysend.at[sl, ch], yrx.at[sl, ch], s3, y_r.at[sl, ch], y_dev), 3, 128)

    back(1, 2)
    back(2, 2 * zh)
    core_send(0)
    core_send(1)
    back(0, 2)
    y_stage(0, 0)
    cx[1].wait_recv()
    for ch in range(2):
        for x_ in range(4):
            acc1[ch, x_] = pair(1, x_, ch)
    back(2, 2 * (1 - zh))
    back(3, last)
    core_send(2)
    core_send(3)
    zx = {}

    def z_stage(ch):
        yx[0, ch].wait_recv()
        zsend[ch] = (acc1[ch] + yrx[0, ch].astype(F32)).astype(BF16)
        zx[ch] = rcopy(zsend.at[ch], zrx.at[ch], z_s.at[ch], z_r.at[ch], z_dev)
        zx[ch].start()

    z_stage(1)
    y_stage(2, 1)
    for u in range(4):
        dq_store(u + 4, dqa[u])
    dq_send(2)
    dq_send(3)
    cx[3].wait_recv()
    for ch in range(2):
        for x_ in range(4):
            acc0[ch, x_] = pair(3, x_, ch)
    for ch in (1, 0):
        yx[1, ch].wait_recv()
        acc0[ch] = acc0[ch] + yrx[1, ch].astype(F32)

    zx[1].wait_send()
    z_stage(0)
    for side in range(2):
        got(n_r.at[side, 1 - side], 512)
    got(nf_r, 1024)
    got(nc_r, 512)
    pltpu.make_async_copy(kib(512), d_ref.at[0, pl.ds(0, 512)], nl_sem).wait()

    def turn(i, carry):
        nt[i] = nbuf[i].reshape(1024, 256).T
        return carry

    lax.fori_loop(0, 8, turn, 0)

    border = [1 - zh, zh]
    ko_own = []

    def final_half(ch):
        zx[ch].wait_recv()
        kga[ch, :, pl.ds(c, 1)] = (acc0[ch] + zrx[ch].astype(F32)).astype(BF16).reshape(4, 1, 128, 128)
        own = kga.at[ch, :, c]
        k2 = go(rcopy(own, own, s3, kc2_r.at[ch], core_dev), 3, 128)
        out = kg_out if ch == 0 else vg_out
        for i, px in enumerate(xs):
            go(rcopy(kga.at[ch, px, c], out.at[0, :, blk(x, 128)], s3, ko_r, dev(x_=px)), 3, 32)
        cp = pltpu.make_async_copy(kga.at[ch, x, c], out.at[0, :, blk(x, 128)], l_sem.at[4 + ch])
        cp.start()
        ko_own.append(cp)
        k2.wait_recv()
        kgall = kga[ch].reshape(1024, 128)
        w1s[ch] = dot_nn(nt[...].reshape(2048, 1024), kgall).astype(BF16).reshape(4, 2, 256, 128)
        for d in (1, 0, 2):
            py = lax.rem(y + d + 1, 4)
            go(rcopy(w1s.at[ch, py], w1r.at[ch, d], s3, w1_r.at[ch], ydev[d]), 3, 128)

    def z_half(ch):
        got(w1_r.at[ch], 384)
        for bi, b in enumerate(border):
            t = w1s[ch, y, b].astype(F32)
            for d in range(3):
                t = t + w1r[ch, d, b].astype(F32)
            w2s[ch, bi] = t.astype(BF16).reshape(4, 4, 16, 128)
            for i in range(bi, 4):
                pz = lax.rem(zl + i, 4)
                sl = i if bi == 0 else 3 + i
                go(rcopy(w2s.at[ch, bi, :, pz], w2r.at[ch, sl], s3, w2_r.at[ch], dev(zh_=b, zl_=pz)), 3, 16)

    final_half(1)
    final_half(0)
    z_half(1)
    z_half(0)
    for ch in (1, 0):
        got(w2_r.at[ch], 112)
        t = w2s[ch, 1, :, pl.ds(zl, 1)].reshape(4, 16, 128).astype(F32)
        for i in range(7):
            t = t + w2r[ch, i].astype(F32)
        w3s[:, :, ch * 128:(ch + 1) * 128] = t
    self_core = x // 2

    def w4_copy(xl, cc_):
        return rcopy(w3s.at[xl * 2 + cc_], w4r.at[x], w4_s.at[xl * 2 + cc_], w4_r.at[x],
                     dev(x_=2 * c + xl, c_=cc_))

    for xl in range(2):
        for cc_ in range(2):
            is_me = (2 * c + xl == x) & (c == cc_)

            @pl.when(is_me)
            def _():
                w4r[pl.ds(x, 1)] = w3s[xl * 2 + cc_].reshape(1, 16, 256)

            @pl.when(jnp.logical_not(is_me))
            def _():
                w4_copy(xl, cc_).start()
    for xx in range(4):
        @pl.when(jnp.logical_not((x == xx) & (c == self_core)))
        def _():
            rcopy(w3s.at[0], w4r.at[xx], w4_s.at[0], w4_r.at[xx], core_dev).wait_recv()
    for xx in range(4):
        w_out[:, xx * 128:(xx + 1) * 128] = w4r[xx, :, 0:128]
        w_out[:, 512 + xx * 128:512 + (xx + 1) * 128] = w4r[xx, :, 128:256]
    for xl in range(2):
        for cc_ in range(2):
            @pl.when(jnp.logical_not((2 * c + xl == x) & (c == cc_)))
            def _():
                w4_copy(xl, cc_).wait_send()
    drain(dq_s, 384)
    got(dq_r, 384)
    pltpu.make_async_copy(kib(128), d_ref.at[0, pl.ds(0, 128)], dql_sem).wait()
    got(ko_r, 192)
    for cp in ko_own:
        cp.wait()
    zx[0].wait_send()
    drain(n_s, 2048)
    drain(nf_s, 1024)
    drain(nc_s, 512)
    drain(s1, sent[1])
    drain(s3, sent[3])


def place(*refs):
    ins, outs, sem = refs[:4], refs[4:8], refs[8]
    cps = [pltpu.make_async_copy(a, b, sem.at[i]) for i, (a, b) in enumerate(zip(ins, outs))]
    for cp in cps:
        cp.start()
    for cp in cps:
        cp.wait()


def local(query, keys, values, out_grad, normed_input, q_start, q_len):
    dma = pltpu.SemaphoreType.DMA
    V = pltpu.VMEM
    hbm = pl.BlockSpec(memory_space=pl.ANY)
    smem = pl.BlockSpec(memory_space=pltpu.SMEM)
    outs = pl.pallas_call(
        body,
        name="attention_grads",
        out_shape=(jax.ShapeDtypeStruct((1, 128, 2048), BF16), jax.ShapeDtypeStruct((1, 128, 512), BF16),
                   jax.ShapeDtypeStruct((1, 128, 512), BF16), jax.ShapeDtypeStruct((16, 1024), F32)),
        in_specs=[hbm] * 5 + [smem] * 2,
        out_specs=[hbm] * 3 + [pl.BlockSpec(memory_space=pltpu.VMEM)],
        scratch_shapes=[
            V((4, 128, 512), BF16), V((4, 128, 512), BF16), V((4, 4, 256, 256), BF16),
            V((8, 4, 2, 128, 256), BF16),
            V((4, 3584, 256), F32), V((4, 3584, 256), F32), V((4096, 128), F32), V((4096, 128), F32),
            V((4, 128, 512), BF16),
            V((4, 4, 128, 256), BF16), V((4, 4, 128, 256), BF16),
            V((2, 2, 4, 128, 128), BF16), V((2, 2, 4, 128, 128), BF16),
            V((2, 4, 128, 128), F32), V((2, 4, 128, 128), F32), V((2, 4, 128, 128), BF16), V((2, 4, 128, 128), BF16),
            V((2, 4, 2, 128, 128), BF16),
            V((2, 4, 2, 256, 128), BF16), V((2, 3, 2, 256, 128), BF16), V((8, 256, 1024), BF16),
            V((128, 4096), BF16), V((8, 3, 16, 256), F32), V((4, 16, 256), F32), V((4, 1, 256), F32),
            V((5, 128, 256), F32), V((2, 2, 4, 4, 16, 128), BF16),
            V((2, 7, 4, 16, 128), BF16), V((4, 16, 256), F32), V((4, 16, 256), F32),
            dma, dma, dma((3,)), dma((2,)), dma((4,)), dma((8,)), dma((4,)), dma, dma((2, 2)), dma, dma, dma, dma,
            dma, dma, dma((4,)), dma((2, 2)), dma((2,)), dma((2,)), dma((2,)), dma, dma((2,)), dma((2,)), dma((4,)), dma((4,)),
            dma((6,)), dma, dma,
        ],
        compiler_params=pltpu.CompilerParams(collective_id=0, has_side_effects=True, vmem_limit_bytes=60 << 20),
    )(query, out_grad, keys, values, normed_input, q_start, q_len)
    return pl.pallas_call(
        place,
        name="place_outputs",
        out_shape=[jax.ShapeDtypeStruct(o.shape, o.dtype) for o in outs],
        in_specs=[pl.BlockSpec(memory_space=pltpu.VMEM)] * 4,
        out_specs=[hbm] * 4,
        scratch_shapes=[dma((4,))],
    )(*outs)


def solution(mesh):
    tok = P("dp", "seq", None)
    return jax.shard_map(
        local, mesh=mesh,
        in_specs=(tok, tok, tok, tok, tok, P("dp"), P("dp")),
        out_specs=(tok, tok, tok, P(("seq", "dp"), None)),
        check_vma=False)
```

```python
import math
import jax
import jax.numpy as jnp
from jax import lax
from jax.experimental import pallas as pl
from jax.experimental.pallas import tpu as pltpu
from jax.sharding import PartitionSpec as P

HEAD_DIM = 128
SCALE = 1.0 / math.sqrt(HEAD_DIM)
EXPC = SCALE * math.log2(math.e)
NEG = -1e30
F32 = jnp.float32
BF16 = jnp.bfloat16


def dot_nt(a, b):
    return lax.dot_general(a, b, (((1,), (1,)), ((), ())), preferred_element_type=F32)


def dot_nn(a, b):
    return lax.dot_general(a, b, (((1,), (0,)), ((), ())), preferred_element_type=F32)


def dot_tn(a, b):
    return lax.dot_general(a, b, (((0,), (0,)), ((), ())), preferred_element_type=F32)


def coords():
    seq = lax.axis_index("seq")
    c = lax.rem(seq, 2)
    x = lax.rem(seq // 2, 4)
    zh = lax.rem(seq // 8, 2)
    yl = lax.rem(seq // 16, 2)
    s = seq // 32
    zl = lax.axis_index("dp")
    return s, yl, zh, x, c, zl


def seq_of(s, yl, zh, x, c):
    return s * 32 + yl * 16 + zh * 8 + x * 2 + c


def rcopy(src, dst, ssem, rsem, dev):
    return pltpu.make_async_remote_copy(
        src_ref=src, dst_ref=dst, send_sem=ssem, recv_sem=rsem,
        device_id={"seq": dev[0], "dp": dev[1]}, device_id_type=pl.DeviceIdType.MESH)


def greet(peers):
    barrier = pltpu.get_barrier_semaphore()
    for seq, dp in peers:
        pl.semaphore_signal(barrier, inc=1, device_id={"seq": seq, "dp": dp},
                            device_id_type=pl.DeviceIdType.MESH)
    pl.semaphore_wait(barrier, len(peers))


def blk(i, w):
    return pl.ds(pl.multiple_of(i * w, w), w)


def body(q_in, g_in, k_in, v_in, n_in, start_ref, len_ref,
         dq_out, kg_out, vg_out, w_out,
         q_ref, g_ref, kv, nbuf, s_ref, d_ref, dk_ref, dv_ref, dq_ref,
         csend, crx, ysend, yrx, acc0, acc1, zsend, zrx, kga,
         w1s, w1r, nt, kt_ref, st, fac, dlt, dqa, w2s, w2r, w3s, w4r,
         s1, s3, kx_r, qx_r, kz_r, ky_r, kc_r, n_s, n_r, nf_s, nf_r, nc_s, nc_r, dq_s, dq_r,
         c_r, y_r, z_s, z_r, kc2_r, ko_r, w1_r, w2_r, w4_s, w4_r, l_sem, nl_sem, dql_sem):
    s, yl, zh, x, c, zl = coords()
    y = s * 2 + yl
    z = zh * 4 + zl
    me8 = x * 2 + c

    def dev(s_=None, yl_=None, zh_=None, x_=None, c_=None, zl_=None):
        return (seq_of(s if s_ is None else s_, yl if yl_ is None else yl_, zh if zh_ is None else zh_,
                       x if x_ is None else x_, c if c_ is None else c_), zl if zl_ is None else zl_)

    row8 = [lax.rem(me8 + d, 8) for d in range(1, 8)]
    xs = [lax.rem(x + d, 4) for d in range(1, 4)]
    ys = [lax.rem(y + d, 4) for d in range(1, 4)]
    zs = [lax.rem(z + d, 8) for d in range(1, 8)]
    ydev = [dev(s_=p // 2, yl_=lax.rem(p, 2)) for p in ys]
    zdev = [dev(zh_=p // 4, zl_=lax.rem(p, 4)) for p in zs]
    core_dev = dev(c_=1 - c)
    y_dev = dev(yl_=1 - yl)
    z_dev = dev(zh_=1 - zh)
    greet([dev(x_=p // 2, c_=lax.rem(p, 2)) for p in row8] + ydev + zdev)

    sent = {}

    def go(cp, key, kb):
        cp.start()
        sent[key] = sent.get(key, 0) + kb
        return cp

    def kib(n):
        return s_ref.at[0, pl.ds(0, n)]

    def drain(sem, n):
        rcopy(kib(n), kib(n), sem, sem, (seq_of(s, yl, zh, x, 1 - c), zl)).wait_send()

    def got(sem, n):
        rcopy(kib(n), kib(n), sem, sem, (seq_of(s, yl, zh, x, 1 - c), zl)).wait_recv()

    crow = blk(c, 128)
    last = yl * zh

    def slot(yl_, zh_, plane):
        return jnp.where(yl_ == 0, jnp.where(zh_ == plane, 0, 1), 2 + zh_)

    mine = slot(yl, zh, zh)
    for i, px in enumerate(xs):
        go(rcopy(k_in.at[0, :, blk(px, 128)], kv.at[mine, x, crow, pl.ds(0, 128)], s1, kx_r.at[i], dev(x_=px)), 1, 32)
        go(rcopy(v_in.at[0, :, blk(px, 128)], kv.at[mine, x, crow, pl.ds(128, 128)], s1, kx_r.at[i], dev(x_=px)), 1, 32)
    own_kv = [pltpu.make_async_copy(k_in.at[0, :, blk(x, 128)], kv.at[mine, x, crow, pl.ds(0, 128)], l_sem.at[0]),
              pltpu.make_async_copy(v_in.at[0, :, blk(x, 128)], kv.at[mine, x, crow, pl.ds(128, 128)], l_sem.at[1])]
    own_q = [pltpu.make_async_copy(q_in.at[0, :, blk(x, 512)], q_ref.at[x], l_sem.at[2]),
             pltpu.make_async_copy(g_in.at[0, :, blk(x, 512)], g_ref.at[x], l_sem.at[3])]
    for cp in own_kv + own_q:
        cp.start()

    def q_send(ph):
        for px in (xs[1], xs[0], xs[2]):
            src = pl.ds(pl.multiple_of(px * 512 + ph * 256, 256), 256)
            dst = pl.ds(ph * 256, 256)
            go(rcopy(q_in.at[0, :, src], q_ref.at[x, :, dst], s1, qx_r.at[ph], dev(x_=px)), 1, 64)
            go(rcopy(g_in.at[0, :, src], g_ref.at[x, :, dst], s1, qx_r.at[ph], dev(x_=px)), 1, 64)

    q_send(0)

    def piece(sl, k):
        return kv.at[sl, lax.rem(x - k + 4, 4), crow]

    def to_core(e, k, p):
        return rcopy(p, p, s1, kc_r.at[e], core_dev)

    def z_copy(k):
        return rcopy(piece(mine, k), piece(slot(yl, zh, 1 - zh), k), s1, kz_r.at[k], z_dev)

    def y_copy(e, sl, k):
        return rcopy(piece(sl, k), piece(sl, k), s1, ky_r.at[4 * e + k], y_dev)

    for k in range(4):
        if k == 0:
            for cp in own_kv:
                cp.wait()
        else:
            got(kx_r.at[k - 1], 64)
        go(z_copy(k), 1, 64)
        go(y_copy(0, mine, k), 1, 64)
        go(to_core(0, k, piece(mine, k)), 1, 64)
    ev = [mine, slot(1 - yl, zh, zh), slot(yl, 1 - zh, zh), slot(1 - yl, 1 - zh, zh)]

    dk_ref[...] = jnp.zeros_like(dk_ref)
    dv_ref[...] = jnp.zeros_like(dv_ref)
    st[:, 0] = jnp.full((8, 16, 256), NEG, F32)
    st[:, 1:3] = jnp.zeros((8, 2, 16, 256), F32)
    dqa[...] = jnp.zeros_like(dqa)
    start = start_ref[s]
    end = start + len_ref[s]
    lane = lax.broadcasted_iota(jnp.int32, (1, 256), 1)

    def keys(j, n):
        if isinstance(j, int):
            return kv[j // 4, j % 4:j % 4 + n].reshape(n * 256, 256)[:, 0:128]
        return kv[j // 4, pl.ds(lax.rem(j, 4), n), :, 0:128].reshape(n * 256, 128)

    def values(j):
        return kv[j // 4, j % 4, :, 128:256]

    def rows_of(j, n=1):
        return pl.ds(j * 256 if isinstance(j, int) else pl.multiple_of(j * 256, 256), n * 256)

    def unit(u):
        h, half = u // 2, (u % 2 if isinstance(u, int) else lax.rem(u, 2))
        cols = pl.ds(h * 128 if isinstance(h, int) else pl.multiple_of(h * 128, 128), 128)
        xx = pl.ds(2 * half, 2)
        pos = yl * 2048 + zh * 1024 + (2 * half + lane // 128) * 256 + c * 128 + lax.rem(lane, 128)
        lim = jnp.maximum(start, jnp.minimum(end, pos + 1))
        return q_ref[xx, :, cols].reshape(256, 128), g_ref[xx, :, cols].reshape(256, 128), lim

    def dq_store(u, dq):
        h, half = u // 2, (u % 2 if isinstance(u, int) else lax.rem(u, 2))
        cols = pl.ds(h * 128 if isinstance(h, int) else pl.multiple_of(h * 128, 128), 128)
        dq_ref[pl.ds(2 * half, 2), :, cols] = (dq.T * SCALE).astype(BF16).reshape(2, 128, 128)

    def pass12(u, su, j, masked):
        q, g, lim = unit(u)
        rows = rows_of(j)
        sc = dot_nt(kv[j // 4, (j % 4 if isinstance(j, int) else lax.rem(j, 4)), :, 0:128], q)
        if masked:
            kpos = lax.broadcasted_iota(jnp.int32, (256, 256), 0)
            sc = jnp.where(kpos < lim - j * 256, sc, NEG)
        m = jnp.max(sc, axis=0, keepdims=True)
        e = jnp.exp2((sc - m) * EXPC)
        dp = dot_nt(kv[j // 4, (j % 4 if isinstance(j, int) else lax.rem(j, 4)), :, 128:256], g)
        st[u, 0, pl.ds(j, 1)] = m
        st[u, 1, pl.ds(j, 1)] = jnp.sum(e, axis=0, keepdims=True)
        st[u, 2, pl.ds(j, 1)] = jnp.sum(e * dp, axis=0, keepdims=True)
        s_ref[su, rows, :] = e
        d_ref[su, rows, :] = dp

    def finish(u, su):
        m = jnp.max(st[u, 0], axis=0, keepdims=True)
        f = jnp.exp2((st[u, 0] - m) * EXPC)
        f = f * (1.0 / jnp.sum(st[u, 1] * f, axis=0, keepdims=True))
        fac[su] = f
        dlt[su] = jnp.sum(st[u, 2] * f, axis=0, keepdims=True)

    def pass3(u, su, j, n, dq):
        q, g, _ = unit(u)
        dlv = dlt[su]
        ds_, p_ = [], []
        for i in range(n):
            r = rows_of(j + i)
            p = s_ref[su, r, :] * fac[su, pl.ds(j + i, 1)]
            ds_.append((p * (d_ref[su, r, :] - dlv)).astype(BF16))
            p_.append(p.astype(BF16))
        ds = ds_[0] if n == 1 else jnp.concatenate(ds_, axis=0)
        p = p_[0] if n == 1 else jnp.concatenate(p_, axis=0)
        rows = rows_of(j, n)
        dk_ref[rows, :] += dot_nn(ds, q)
        dv_ref[rows, :] += dot_nn(p, g)
        return dq + dot_nn(kt_ref[:, rows], ds)

    def arrive(e):
        sl = ev[e]

        def one(b, carry):
            j = sl * 4 + b
            kt_ref[:, rows_of(j)] = keys(j, 1).T
            for u in range(4):
                pass12(u, u, j, True)
            return carry
        lax.fori_loop(0, jnp.where(sl < 3, 4, 2 * last), one, 0)

    for k in range(4):
        y_copy(0, ev[1], k).wait_recv()
        go(to_core(1, k, piece(ev[1], k)), 1, 64)
    for cp in own_q:
        cp.wait()
    got(qx_r.at[0], 384)
    q_send(1)
    got(kc_r.at[0], 256)
    arrive(0)

    def n_copy(rr, side, cc_):
        px = lax.rem(x + (1 if side == 0 else 3), 4)
        return rcopy(n_in.at[0, :, pl.ds(pl.multiple_of(rr * 512 + cc_ * 256, 256), 256)], nbuf.at[rr, x, c],
                     n_s, n_r.at[side, rr // 4], dev(x_=px, c_=cc_))

    def n_fwd(i, side, cc_):
        rr = i + 4 * side
        src = nbuf.at[rr, lax.rem(x + (3 if side == 0 else 1), 4), cc_]
        px = lax.rem(x + (1 if side == 0 else 3), 4)
        return rcopy(src, src, nf_s, nf_r, dev(x_=px))

    def nsend(i, carry):
        for cc_ in range(2):
            n_copy(i, 0, cc_).start()
            n_copy(lax.rem(i + 4, 8), 1, cc_).start()
        mine_ = pl.ds(pl.multiple_of(i * 512 + c * 256, 256), 256)
        theirs = pl.ds(pl.multiple_of(i * 512 + (1 - c) * 256, 256), 256)
        rcopy(n_in.at[0, :, theirs], nbuf.at[i, x, c], nc_s, nc_r, core_dev).start()
        pltpu.make_async_copy(n_in.at[0, :, mine_], nbuf.at[i, x, c], nl_sem).start()
        return carry

    def far_piece(k):
        z_copy(k).wait_recv()
        go(y_copy(1, ev[2], k), 1, 64)
        go(to_core(2, k, piece(ev[2], k)), 1, 64)

    far_piece(0)
    far_piece(1)
    lax.fori_loop(0, 8, nsend, 0)
    got(kc_r.at[1], 256)
    arrive(1)
    far_piece(2)
    far_piece(3)
    for k in range(4):
        y_copy(1, ev[3], k).wait_recv()
        go(to_core(3, k, piece(ev[3], k)), 1, 64)
    got(kc_r.at[2], 256)
    arrive(2)
    got(kc_r.at[3], 256)
    arrive(3)
    for u in range(4):
        finish(u, u)
    got(qx_r.at[1], 384)

    def mid(u, carry):
        dq = jnp.zeros((128, 256), F32)
        for j in range(12):
            dq = pass3(u, u, j, 1, dq)
            pass12(u + 4, u, j, j >= 8)
        dqa[4] = dq

        @pl.when(last == 1)
        def _():
            d2 = dqa[4]
            for j in range(12, 14):
                d2 = pass3(u, u, j, 1, d2)
                pass12(u + 4, u, j, True)
            dqa[4] = d2
        dq_store(u, dqa[4])
        finish(u + 4, u)
        return carry

    lax.fori_loop(0, 3, mid, 0)

    for side in range(2):
        got(n_r.at[side, side], 512)

    def fwd(i, carry):
        for side in range(2):
            for cc_ in range(2):
                n_fwd(i, side, cc_).start()
        return carry

    lax.fori_loop(0, 4, fwd, 0)
    lax.fori_loop(3, 4, mid, 0)

    def dq_copy(h, i):
        px = xs[i]
        return rcopy(dq_ref.at[px, :, blk(h, 128)], dq_out.at[0, :, blk(x * 4 + h, 128)],
                     dq_s, dq_r, dev(x_=px))

    def dq_local(h):
        return pltpu.make_async_copy(dq_ref.at[x, :, blk(h, 128)], dq_out.at[0, :, blk(x * 4 + h, 128)],
                                     dql_sem)

    def dq_send(h):
        for i in range(3):
            dq_copy(h, i).start()
        dq_local(h).start()

    dq_send(0)
    dq_send(1)

    def back(sl, trips, first=0):
        def two(b, carry):
            j = sl * 4 + 2 * b
            rows = rows_of(j, 2)
            dk = dk_ref[rows, :]
            dv = dv_ref[rows, :]
            for u in range(4):
                q, g, _ = unit(u + 4)
                dlv = dlt[u]
                d_, p_ = [], []
                for i in range(2):
                    r = rows_of(j + i)
                    p = s_ref[u, r, :] * fac[u, pl.ds(j + i, 1)]
                    d_.append((p * (d_ref[u, r, :] - dlv)).astype(BF16))
                    p_.append(p.astype(BF16))
                ds = jnp.concatenate(d_, axis=0)
                dk = dk + dot_nn(ds, q)
                dv = dv + dot_nn(jnp.concatenate(p_, axis=0), g)
                dqa[u] += dot_nn(kt_ref[:, rows], ds)
            dk_ref[rows, :] = dk
            dv_ref[rows, :] = dv
            return carry
        lax.fori_loop(first, trips, two, 0)

    def grads(yl_, zh_, x_, c_):
        r = pl.ds(pl.multiple_of((slot(yl_, zh_, zh) * 4 + x_) * 256 + c_ * 128, 128), 128)
        return jnp.concatenate([dk_ref[r, :] * SCALE, dv_ref[r, :]], axis=1)

    quad = [(1 - yl, 1 - zh), (yl, 1 - zh), (1 - yl, zh), (yl, zh)]
    cx = []

    def core_send(k):
        for x_ in range(4):
            csend[k, x_] = grads(quad[k][0], quad[k][1], x_, 1 - c).astype(BF16)
        cx.append(go(rcopy(csend.at[k], crx.at[k], s3, c_r.at[k], core_dev), 3, 256))

    def pair(k, x_, ch):
        r = pl.ds(pl.multiple_of((slot(quad[k][0], quad[k][1], zh) * 4 + x_) * 256 + c * 128, 128), 128)
        own = dk_ref[r, :] * SCALE if ch == 0 else dv_ref[r, :]
        return own + crx[k, x_, :, ch * 128:(ch + 1) * 128].astype(F32)

    yx = {}

    def y_stage(k, sl):
        cx[k].wait_recv()
        for ch in (1, 0):
            for x_ in range(4):
                ysend[sl, ch, x_] = pair(k, x_, ch).astype(BF16)
            yx[sl, ch] = go(rcopy(ysend.at[sl, ch], yrx.at[sl, ch], s3, y_r.at[sl, ch], y_dev), 3, 128)

    back(1, 2)
    back(2, 2 * zh)
    core_send(0)
    core_send(1)
    back(0, 2)
    y_stage(0, 0)
    cx[1].wait_recv()
    for ch in range(2):
        for x_ in range(4):
            acc1[ch, x_] = pair(1, x_, ch)
    back(2, 2 * (1 - zh))
    back(3, last)
    core_send(2)
    core_send(3)
    zx = {}

    def z_stage(ch):
        yx[0, ch].wait_recv()
        zsend[ch] = (acc1[ch] + yrx[0, ch].astype(F32)).astype(BF16)
        zx[ch] = rcopy(zsend.at[ch], zrx.at[ch], z_s.at[ch], z_r.at[ch], z_dev)
        zx[ch].start()

    z_stage(1)
    y_stage(2, 1)
    for u in range(4):
        dq_store(u + 4, dqa[u])
    dq_send(2)
    dq_send(3)
    cx[3].wait_recv()
    for ch in range(2):
        for x_ in range(4):
            acc0[ch, x_] = pair(3, x_, ch)
    for ch in (1, 0):
        yx[1, ch].wait_recv()
        acc0[ch] = acc0[ch] + yrx[1, ch].astype(F32)

    zx[1].wait_send()
    z_stage(0)
    for side in range(2):
        got(n_r.at[side, 1 - side], 512)
    got(nf_r, 1024)
    got(nc_r, 512)
    pltpu.make_async_copy(kib(512), d_ref.at[0, pl.ds(0, 512)], nl_sem).wait()

    def turn(i, carry):
        nt[i] = nbuf[i].reshape(1024, 256).T
        return carry

    lax.fori_loop(0, 8, turn, 0)

    border = [1 - zh, zh]
    ko_own = []

    def final_half(ch):
        zx[ch].wait_recv()
        kga[ch, :, pl.ds(c, 1)] = (acc0[ch] + zrx[ch].astype(F32)).astype(BF16).reshape(4, 1, 128, 128)
        own = kga.at[ch, :, c]
        k2 = go(rcopy(own, own, s3, kc2_r.at[ch], core_dev), 3, 128)
        out = kg_out if ch == 0 else vg_out
        for i, px in enumerate(xs):
            go(rcopy(kga.at[ch, px, c], out.at[0, :, blk(x, 128)], s3, ko_r, dev(x_=px)), 3, 32)
        cp = pltpu.make_async_copy(kga.at[ch, x, c], out.at[0, :, blk(x, 128)], l_sem.at[4 + ch])
        cp.start()
        ko_own.append(cp)
        k2.wait_recv()
        kgall = kga[ch].reshape(1024, 128)
        w1s[ch] = dot_nn(nt[...].reshape(2048, 1024), kgall).astype(BF16).reshape(4, 2, 256, 128)
        for d in (1, 0, 2):
            py = lax.rem(y + d + 1, 4)
            go(rcopy(w1s.at[ch, py], w1r.at[ch, d], s3, w1_r.at[ch], ydev[d]), 3, 128)

    def z_half(ch):
        got(w1_r.at[ch], 384)
        for bi, b in enumerate(border):
            t = w1s[ch, y, b].astype(F32)
            for d in range(3):
                t = t + w1r[ch, d, b].astype(F32)
            w2s[ch, bi] = t.astype(BF16).reshape(4, 4, 16, 128)
            for i in range(bi, 4):
                pz = lax.rem(zl + i, 4)
                sl = i if bi == 0 else 3 + i
                go(rcopy(w2s.at[ch, bi, :, pz], w2r.at[ch, sl], s3, w2_r.at[ch], dev(zh_=b, zl_=pz)), 3, 16)

    final_half(1)
    final_half(0)
    z_half(1)
    z_half(0)
    for ch in (1, 0):
        got(w2_r.at[ch], 112)
        t = w2s[ch, 1, :, pl.ds(zl, 1)].reshape(4, 16, 128).astype(F32)
        for i in range(7):
            t = t + w2r[ch, i].astype(F32)
        w3s[:, :, ch * 128:(ch + 1) * 128] = t
    self_core = x // 2

    def w4_copy(xl, cc_):
        return rcopy(w3s.at[xl * 2 + cc_], w4r.at[x], w4_s.at[xl * 2 + cc_], w4_r.at[x],
                     dev(x_=2 * c + xl, c_=cc_))

    for xl in range(2):
        for cc_ in range(2):
            is_me = (2 * c + xl == x) & (c == cc_)

            @pl.when(is_me)
            def _():
                w4r[pl.ds(x, 1)] = w3s[xl * 2 + cc_].reshape(1, 16, 256)

            @pl.when(jnp.logical_not(is_me))
            def _():
                w4_copy(xl, cc_).start()
    for xx in range(4):
        @pl.when(jnp.logical_not((x == xx) & (c == self_core)))
        def _():
            rcopy(w3s.at[0], w4r.at[xx], w4_s.at[0], w4_r.at[xx], core_dev).wait_recv()
    for xx in range(4):
        w_out[:, xx * 128:(xx + 1) * 128] = w4r[xx, :, 0:128]
        w_out[:, 512 + xx * 128:512 + (xx + 1) * 128] = w4r[xx, :, 128:256]
    for xl in range(2):
        for cc_ in range(2):
            @pl.when(jnp.logical_not((2 * c + xl == x) & (c == cc_)))
            def _():
                w4_copy(xl, cc_).wait_send()
    drain(dq_s, 384)
    got(dq_r, 384)
    pltpu.make_async_copy(kib(128), d_ref.at[0, pl.ds(0, 128)], dql_sem).wait()
    got(ko_r, 192)
    for cp in ko_own:
        cp.wait()
    zx[0].wait_send()
    drain(n_s, 2048)
    drain(nf_s, 1024)
    drain(nc_s, 512)
    drain(s1, sent[1])
    drain(s3, sent[3])


def place(*refs):
    ins, outs, sem = refs[:4], refs[4:8], refs[8]
    cps = [pltpu.make_async_copy(a, b, sem.at[i]) for i, (a, b) in enumerate(zip(ins, outs))]
    for cp in cps:
        cp.start()
    for cp in cps:
        cp.wait()


def local(query, keys, values, out_grad, normed_input, q_start, q_len):
    dma = pltpu.SemaphoreType.DMA
    V = pltpu.VMEM
    hbm = pl.BlockSpec(memory_space=pl.ANY)
    smem = pl.BlockSpec(memory_space=pltpu.SMEM)
    outs = pl.pallas_call(
        body,
        name="attention_grads",
        out_shape=(jax.ShapeDtypeStruct((1, 128, 2048), BF16), jax.ShapeDtypeStruct((1, 128, 512), BF16),
                   jax.ShapeDtypeStruct((1, 128, 512), BF16), jax.ShapeDtypeStruct((16, 1024), F32)),
        in_specs=[hbm] * 5 + [smem] * 2,
        out_specs=[hbm] * 3 + [pl.BlockSpec(memory_space=pltpu.VMEM)],
        scratch_shapes=[
            V((4, 128, 512), BF16), V((4, 128, 512), BF16), V((4, 4, 256, 256), BF16),
            V((8, 4, 2, 128, 256), BF16),
            V((4, 3584, 256), F32), V((4, 3584, 256), F32), V((4096, 128), F32), V((4096, 128), F32),
            V((4, 128, 512), BF16),
            V((4, 4, 128, 256), BF16), V((4, 4, 128, 256), BF16),
            V((2, 2, 4, 128, 128), BF16), V((2, 2, 4, 128, 128), BF16),
            V((2, 4, 128, 128), F32), V((2, 4, 128, 128), F32), V((2, 4, 128, 128), BF16), V((2, 4, 128, 128), BF16),
            V((2, 4, 2, 128, 128), BF16),
            V((2, 4, 2, 256, 128), BF16), V((2, 3, 2, 256, 128), BF16), V((8, 256, 1024), BF16),
            V((128, 4096), BF16), V((8, 3, 16, 256), F32), V((4, 16, 256), F32), V((4, 1, 256), F32),
            V((5, 128, 256), F32), V((2, 2, 4, 4, 16, 128), BF16),
            V((2, 7, 4, 16, 128), BF16), V((4, 16, 256), F32), V((4, 16, 256), F32),
            dma, dma, dma((3,)), dma((2,)), dma((4,)), dma((8,)), dma((4,)), dma, dma((2, 2)), dma, dma, dma, dma,
            dma, dma, dma((4,)), dma((2, 2)), dma((2,)), dma((2,)), dma((2,)), dma, dma((2,)), dma((2,)), dma((4,)), dma((4,)),
            dma((6,)), dma, dma,
        ],
        compiler_params=pltpu.CompilerParams(collective_id=0, has_side_effects=True, vmem_limit_bytes=60 << 20),
    )(query, out_grad, keys, values, normed_input, q_start, q_len)
    return pl.pallas_call(
        place,
        name="place_outputs",
        out_shape=[jax.ShapeDtypeStruct(o.shape, o.dtype) for o in outs],
        in_specs=[pl.BlockSpec(memory_space=pltpu.VMEM)] * 4,
        out_specs=[hbm] * 4,
        scratch_shapes=[dma((4,))],
    )(*outs)


def solution(mesh):
    tok = P("dp", "seq", None)
    return jax.shard_map(
        local, mesh=mesh,
        in_specs=(tok, tok, tok, tok, tok, P("dp"), P("dp")),
        out_specs=(tok, tok, tok, P(("seq", "dp"), None)),
        check_vma=False)
```
